32 devices in a mesh: dir: 4 (over z), bl: 8 (over y, x, core).
Axes of the slice: x: 2, y: 2, z: 4, core: 2. Of those that a mesh axis runs over, the one named last changes fastest.
Arguments:
- observed: float32 [32, 2, 30720], P('dir', None, 'bl'), may hold values from -6 to 6
- baseline_uvw_rows: float32 [3, 65536], P(None, 'bl'), may hold values from -600 to 600
- frequencies: float32 [32], replicated, may hold values from 0.8 to 1.2
- source_offset: float32 [2, 128], replicated, may hold values from -0.05 to 0.05
- source_flux: float32 [32, 128], replicated, may hold values from 0.02 to 0.3
- source_group: int32 [128], replicated, may hold values from 0 to 3, as said below
- direction_gain: float32 [4, 32, 2, 512], P('dir'), may hold values from -4.2 to 4.2
- station_first: int32 [4096], replicated, may hold values from 0 to 511
- station_second: int32 [4096], replicated, may hold values from 0 to 511
- average_exponent: int32 [4096], replicated, may hold values from 0 to 4, as said below
- owner_plan: int32 [8, 8], replicated, may hold values from 0 to 7, as said below
Outputs:
- residual: float32 [32, 2, 30720], P('dir', None, 'bl')
The draws below stay inside these ranges and needn't reach their ends.
Inputs may be any that keep to these rules, and one draw needn't show every extreme that they name: `source_group`: each of the 4 groups is named by exactly 32 sources. `average_exponent`: summed over the blocks that owner_plan gives one owner, the averaged rows are at most 3840, and some owner has exactly 3840. Each row of owner_plan names every owner exactly once.
All inputs are finite; a program needn't handle non-finite values.
Results may differ from the reference program's by a relative error of at most 0.0003.
Values sent between devices are 32-bit elements; how exact they have to be, the bound alone decides.
A program may use at most 64 MiB of HBM per device.

```python
import math
import jax
import jax.numpy as jnp
from jax import lax

F = 32
TIME_SAMPLES = 16
STATION_COUNT = 512
SRC_GRP = 32
BL_DEV = 512
GROUPS = 4
SOURCES = 128
BLOCK = 64
BASELINE_COUNT = 4096
CAP_DEV = 3840
BDA_ROWS = 30720
N_DIR = 4
N_BL = 8


def shuffled(row_key):
    return jax.random.permutation(row_key, N_BL)


def plan_and_exponents(key):
    pick_key = jax.random.fold_in(key, 101)
    peak_key = jax.random.fold_in(key, 202)
    order_key = jax.random.fold_in(key, 303)
    jitter_key = jax.random.fold_in(key, 404)
    heavy_owner = jax.random.randint(pick_key, (), 0, N_BL)
    peak_block = jax.random.randint(peak_key, (N_BL,), 0, N_BL)
    orders = jax.vmap(shuffled)(jax.random.split(order_key, N_BL)).astype(jnp.int32)
    at_peak = jnp.take_along_axis(orders, peak_block[:, None], axis=1)
    owner_plan = ((orders - at_peak + heavy_owner) % N_BL).astype(jnp.int32)
    baseline_number = jnp.arange(BASELINE_COUNT, dtype=jnp.int32)
    predictor = baseline_number // BL_DEV
    block_pos = baseline_number % BL_DEV // BLOCK
    lowest = 3 - 4 * predictor // N_BL
    jitter_values = jax.random.randint(jitter_key, (BASELINE_COUNT,), 0, 2)
    exponents = lowest + jnp.where(block_pos == peak_block[predictor], 0, jitter_values)
    return (owner_plan, exponents.astype(jnp.int32))


def draw_owner_plan(key, part):
    return plan_and_exponents(key)[0]


def draw_average_exponent(key, part):
    return plan_and_exponents(key)[1]


def draw_source_group(key, part):
    order = jax.random.permutation(jax.random.fold_in(key, 505), SOURCES)
    return (order // SRC_GRP).astype(jnp.int32)


def touch_ends(array, key, least, largest):
    dims = array.shape
    place = [jax.random.randint(jax.random.fold_in(key, axis), (), 0, dims[axis]) for axis in range(len(dims))]
    array = array.at[tuple(place)].set(least)
    longest = dims.index(max(dims))
    place[longest] = (place[longest] + 1) % dims[longest]
    return array.at[tuple(place)].set(largest)


def block_scale(own_key, shape, shards, smallest, top_value):
    loudness, own = 1.0, jax.random.fold_in(own_key, 6)
    for dim, shards_of in shards:
        draws = jnp.exp(jax.random.uniform(jax.random.fold_in(own, dim), (shards_of,), jnp.float32, smallest / len(shards), top_value / len(shards)))
        loudness = loudness * jnp.repeat(draws, shape[dim] // shards_of).reshape([-1 if axis == dim else 1 for axis in range(len(shape))])
    return loudness


def noise(own_key, dims, width, limit, shards=(), held_as=jnp.bfloat16):
    loudness = block_scale(own_key, dims, shards, -0.22, 0.18) if shards else 1.0
    values = jax.random.normal(own_key, dims, jnp.float32) * width * loudness
    return jnp.minimum(jnp.maximum(values, -limit), limit).astype(held_as)


def setup_inputs(seed: int = 0) -> dict:
    streams_of = jax.random.split(jax.random.key(seed), 12)
    observed = noise(streams_of[0], (F, 2, BDA_ROWS), 1.0, 6.0, ((0, 4), (2, 8)), jnp.float32)
    baseline_uvw_rows = noise(streams_of[1], (3, BASELINE_COUNT * TIME_SAMPLES), 100.0, 600.0, ((1, 8),), jnp.float32)
    frequencies = jnp.clip(jax.random.uniform(streams_of[2], (F,), jnp.float32, 0.8, 1.2), 0.8, 1.2)
    source_offset = jnp.clip(jax.random.uniform(streams_of[3], (2, SOURCES), jnp.float32, -0.05, 0.05), -0.05, 0.05)
    source_flux = jnp.clip(jnp.exp(jax.random.uniform(streams_of[4], (F, SOURCES), jnp.float32, math.log(0.02), math.log(0.3))), 0.02, 0.3)
    source_group = draw_source_group(jax.random.fold_in(streams_of[11], 71), 0)
    direction_gain = noise(streams_of[6], (GROUPS, F, 2, STATION_COUNT), 0.7, 4.2, ((0, 4),), jnp.float32)
    station_first = touch_ends(jax.random.randint(streams_of[7], (BASELINE_COUNT,), 0, STATION_COUNT), jax.random.fold_in(streams_of[7], 1), 0, STATION_COUNT - 1).astype(jnp.int32)
    station_second = touch_ends(jax.random.randint(streams_of[8], (BASELINE_COUNT,), 0, STATION_COUNT), jax.random.fold_in(streams_of[8], 1), 0, STATION_COUNT - 1).astype(jnp.int32)
    average_exponent = draw_average_exponent(jax.random.fold_in(streams_of[11], 71), 0)
    owner_plan = draw_owner_plan(jax.random.fold_in(streams_of[11], 71), 0)
    return {"observed": observed, "baseline_uvw_rows": baseline_uvw_rows, "frequencies": frequencies, "source_offset": source_offset, "source_flux": source_flux, "source_group": source_group, "direction_gain": direction_gain, "station_first": station_first, "station_second": station_second, "average_exponent": average_exponent, "owner_plan": owner_plan}


def layout_tables(average_exponent, owner_plan, owners_total, block_len):
    factor = jnp.left_shift(jnp.ones_like(average_exponent), average_exponent)
    row_count = (TIME_SAMPLES // factor).astype(jnp.int32)
    grouped = row_count.reshape(owners_total, owners_total, block_len)
    block_rows = lax.optimization_barrier(jnp.sum(grouped, axis=2, dtype=jnp.int32))
    in_block = (jnp.cumsum(grouped, axis=2, dtype=jnp.int32) - grouped).reshape(-1)
    owner_ids = jnp.arange(owners_total, dtype=jnp.int32)
    matches = (owner_plan[:, :, None] == owner_ids[None, None, :]).astype(jnp.int32)
    to_owner = lax.optimization_barrier(jnp.sum(block_rows[:, :, None] * matches, axis=1, dtype=jnp.int32))
    before = jnp.cumsum(to_owner, axis=0, dtype=jnp.int32) - to_owner
    offset = jnp.take_along_axis(before, owner_plan, axis=1)
    return (factor, row_count, in_block, offset)

def average_rows(values, exponent, factor):
    leading = values.shape[0]
    shaped = values.reshape(leading, 2, exponent.shape[0], TIME_SAMPLES)
    sample_index = jnp.arange(TIME_SAMPLES, dtype=jnp.int32)
    bin_index = jnp.right_shift(sample_index[:, None], exponent[None, :])
    weights = (bin_index[None, :, :] == sample_index[:, None, None]).astype(jnp.float32) / factor[None, None, :].astype(jnp.float32)
    return jnp.einsum('czbt,itb->czib', shaped, weights, precision=lax.Precision.HIGHEST)

def place_rows(averaged, target, capacity):
    leading = averaged.shape[0]
    flat_values = averaged.reshape(leading, 2, -1)
    empty_rows = jnp.zeros((leading, 2, capacity), jnp.float32)
    return empty_rows.at[:, :, target.reshape(-1)].add(flat_values, mode='drop')

def reference(observed, baseline_uvw_rows, frequencies, source_offset, source_flux, source_group, direction_gain, station_first, station_second, average_exponent, owner_plan):
    member = (source_group[:, None] == jnp.arange(N_DIR, dtype=jnp.int32)[None, :]).astype(jnp.float32)
    east_offset = source_offset[0]
    north_offset = source_offset[1]
    depth_term = jnp.sqrt(1.0 - east_offset * east_offset - north_offset * north_offset) - 1.0
    total_rows = BL_DEV * TIME_SAMPLES
    row_block = min(total_rows, 1024)
    chan_block = 4 if F % 4 == 0 else F
    gain_by_channel = jnp.transpose(direction_gain, (1, 0, 2, 3))
    split_freq = frequencies.reshape(-1, chan_block)
    split_flux = source_flux.reshape(-1, chan_block, source_flux.shape[1])

    def device_rows(pieces):
        coords, first_ids, second_ids = pieces

        def row_piece(coord_block):
            phase_base = 2.0 * jnp.pi * (east_offset[:, None] * coord_block[0][None, :] + north_offset[:, None] * coord_block[1][None, :] + depth_term[:, None] * coord_block[2][None, :])

            def channel_piece(pair_args):
                block_freq, block_flux = pair_args
                angles = block_freq[:, None, None] * phase_base[None, :, :]
                weighted = block_flux[:, :, None] * member[None, :, :]
                real_group = jnp.einsum('ckg,ckr->cgr', weighted, jnp.cos(angles), precision=lax.Precision.HIGHEST)
                imag_group = -jnp.einsum('ckg,ckr->cgr', weighted, jnp.sin(angles), precision=lax.Precision.HIGHEST)
                return (real_group, imag_group)
            real_group, imag_group = lax.map(channel_piece, (split_freq, split_flux))
            return (real_group.reshape(F, N_DIR, row_block), imag_group.reshape(F, N_DIR, row_block))
        blocks = jnp.transpose(coords.reshape(3, -1, row_block), (1, 0, 2))
        real_group, imag_group = lax.map(row_piece, blocks)
        real_group = jnp.transpose(real_group, (1, 2, 0, 3)).reshape(F, N_DIR, total_rows)
        imag_group = jnp.transpose(imag_group, (1, 2, 0, 3)).reshape(F, N_DIR, total_rows)
        gain_first = jnp.take(gain_by_channel, first_ids, axis=3)
        gain_second = jnp.take(gain_by_channel, second_ids, axis=3)
        gain_real = gain_first[:, :, 0] * gain_second[:, :, 0] + gain_first[:, :, 1] * gain_second[:, :, 1]
        gain_imag = gain_first[:, :, 1] * gain_second[:, :, 0] - gain_first[:, :, 0] * gain_second[:, :, 1]
        gain_real = jnp.repeat(gain_real, TIME_SAMPLES, axis=2)
        gain_imag = jnp.repeat(gain_imag, TIME_SAMPLES, axis=2)
        model_real = lax.optimization_barrier(jnp.sum(real_group * gain_real - imag_group * gain_imag, axis=1))
        model_imag = lax.optimization_barrier(jnp.sum(real_group * gain_imag + imag_group * gain_real, axis=1))
        return jnp.stack([model_real, model_imag], axis=1)
    full_model = lax.map(device_rows, (jnp.transpose(baseline_uvw_rows.reshape(3, N_BL, -1), (1, 0, 2)), station_first.reshape(N_BL, -1), station_second.reshape(N_BL, -1)))
    model_rows = jnp.transpose(full_model, (1, 2, 0, 3)).reshape(F, 2, -1)
    block_len = BL_DEV // N_BL
    factor, row_count, in_block, offset = layout_tables(average_exponent, owner_plan, N_BL, block_len)
    averaged = average_rows(model_rows, average_exponent, factor)
    baseline_number = jnp.arange(BL_DEV * N_BL, dtype=jnp.int32)
    predictor = baseline_number // BL_DEV
    block_pos = baseline_number % BL_DEV // block_len
    owner_of = owner_plan[predictor, block_pos]
    row_start = owner_of * CAP_DEV + offset[predictor, block_pos] + in_block
    sample_index = jnp.arange(TIME_SAMPLES, dtype=jnp.int32)
    target = jnp.where(sample_index[:, None] < row_count[None, :], row_start[None, :] + sample_index[:, None], CAP_DEV * N_BL).astype(jnp.int32)
    return observed - place_rows(averaged, target, CAP_DEV * N_BL)
```

```python
import functools
import math

import jax
import jax.numpy as jnp
from jax import lax
from jax.experimental import pallas as pl
from jax.experimental.pallas import tpu as pltpu
from jax.sharding import PartitionSpec as P

LANES = 128
UNROLL = 32
MESH = pl.DeviceIdType.MESH
HIGH = lax.Precision.HIGHEST
NT = (((1,), (1,)), ((), ()))
P0, P1, P2, P3 = -2.2636507847492298, 1.3870216243251186, 4.937789609959605, 0.5033641130059734
K0, K1, K2 = 0.9997897140197886, -10.245898871410082, 1.823099221649536


def iota(shape, axis):
    return lax.broadcasted_iota(jnp.int32, shape, axis)


def take(values, index):
    return jnp.take_along_axis(values, index, axis=1, mode="promise_in_bounds")


def prepare_kernel(
    groups,
    owners,
    time,
    uvw_ref,
    freq_ref,
    offs_ref,
    flux_ref,
    group_ref,
    gain_ref,
    ids_ref,
    exps_ref,
    plan_ref,
    plan_smem,
    sky_ref,
    wide_ref,
    base_ref,
    order_ref,
    pair_ref,
    mask_ref,
    start_ref,
    table_ref,
):
    d = lax.axis_index("dir")
    p = lax.axis_index("bl")
    cl = wide_ref.shape[1]
    sources = offs_ref.shape[1]
    per_group = sources // groups
    bl_dev = ids_ref.shape[1]
    block_len = bl_dev // owners
    slots = block_len * time
    block_tiles = slots // LANES
    per_tile = LANES // time
    log_time = int(math.log2(time))
    chunks = bl_dev // LANES

    for k in range(owners):
        order_ref[plan_smem[p, k]] = uvw_ref[:, k * slots : (k + 1) * slots]
    plan = plan_ref[...].astype(jnp.float32)
    own_plan = jnp.sum(
        jnp.where(iota((owners, owners), 0) == p, plan, 0.0), axis=0, keepdims=True
    )
    held_by = jnp.abs(own_plan - iota((owners, owners), 0).astype(jnp.float32)) < 0.5
    block_of = jnp.sum(
        jnp.where(held_by, iota((owners, owners), 1).astype(jnp.float32), 0.0), axis=1, keepdims=True
    )

    member_row = group_ref[...].astype(jnp.float32)
    eye = (iota((sources, sources), 0) == iota((sources, sources), 1)).astype(jnp.float32)
    member_col = lax.dot_general(eye, member_row, NT, precision=HIGH)
    earlier = iota((sources, sources), 0) < iota((sources, sources), 1)
    same = (jnp.abs(member_col - member_row) < 0.5) & earlier
    rank = jnp.sum(same.astype(jnp.float32), axis=0, keepdims=True)
    place = (member_row * per_group + rank + 0.5).astype(jnp.int32)
    pick = (iota((sources, sources), 0) == place).astype(jnp.float32)
    offs = lax.dot_general(pick, offs_ref[...], NT, precision=HIGH)
    east, north = offs[:, 0:1], offs[:, 1:2]
    depth = jnp.sqrt(1.0 - east * east - north * north) - 1.0
    sky_ref[0] = jnp.broadcast_to(east, sky_ref.shape[1:])
    sky_ref[1] = jnp.broadcast_to(north, sky_ref.shape[1:])
    sky_ref[2] = jnp.broadcast_to(depth, sky_ref.shape[1:])
    channel = iota((cl, flux_ref.shape[0]), 1) == d * cl + iota((cl, flux_ref.shape[0]), 0)
    channel = channel.astype(jnp.float32)
    own_flux = jnp.dot(channel, flux_ref[...], precision=HIGH)
    flux = lax.dot_general(own_flux, pick, NT, precision=HIGH)
    for k in range(sources):
        wide_ref[k] = jnp.broadcast_to(flux[:, k : k + 1], (cl, LANES))
    for g in range(groups):
        part = jnp.sum(flux[:, g * per_group : (g + 1) * per_group], axis=1, keepdims=True)
        base_ref[g] = jnp.broadcast_to(part, (cl, LANES))
    freq = jnp.sum(channel * freq_ref[...], axis=1, keepdims=True)
    base_ref[groups] = jnp.broadcast_to(freq, (cl, LANES))

    lane = iota((owners, LANES), 1)
    row = iota((owners, LANES), 0)
    station_total = gain_ref.shape[3]
    for g in range(groups):
        for z in range(2):
            table_ref[g, z] = gain_ref[0, g * cl : (g + 1) * cl, z, :]
    for chunk in range(chunks):
        lanes = pl.ds(chunk * LANES, LANES)
        where_from = jnp.where((chunk * LANES + lane) // block_len == row, block_of, 0.0)
        where_from = (jnp.sum(where_from, axis=0, keepdims=True) + 0.5).astype(jnp.int32)
        source = where_from * block_len + (chunk * LANES + iota((1, LANES), 1)) % block_len
        source = jnp.broadcast_to(source, (cl, LANES))
        looked = []
        for which in range(2):
            ids = jnp.zeros((cl, LANES), jnp.int32)
            for part in range(chunks):
                table = ids_ref[which : which + 1, part * LANES : (part + 1) * LANES]
                table = jnp.broadcast_to(table, (cl, LANES))
                ids = jnp.where((source >> 7) == part, take(table, source & (LANES - 1)), ids)
            low, high = ids & (LANES - 1), ids >> 7
            rows = []
            for g in range(groups):
                for z in range(2):
                    total = jnp.zeros((cl, LANES), jnp.float32)
                    for part in range(station_total // LANES):
                        table = table_ref[g, z, :, pl.ds(part * LANES, LANES)]
                        total = jnp.where(high == part, take(table, low), total)
                    rows.append(total)
            looked.append(rows)
        first, second = looked
        for g in range(groups):
            ar, ai, br, bi = first[2 * g], first[2 * g + 1], second[2 * g], second[2 * g + 1]
            pair_ref[g, 0, :, lanes] = ar * br + ai * bi
            pair_ref[g, 1, :, lanes] = ai * br - ar * bi

    rows_all = jnp.right_shift(jnp.full(exps_ref.shape, time, jnp.int32), exps_ref[...])
    rows_all = rows_all.astype(jnp.float32)
    to_owner = jnp.zeros((owners, 1), jnp.float32)
    for k in range(owners):
        count = jnp.sum(rows_all[:, k * block_len : (k + 1) * block_len], axis=1, keepdims=True)
        to_owner = to_owner + jnp.where(plan_ref[:, k : k + 1] == p, count, 0.0)
    starts = jnp.sum(jnp.where(row < lane, to_owner, 0.0), axis=0, keepdims=True)
    start_ref[...] = (starts + 0.5).astype(jnp.int32)

    exps = []
    for t in range(block_tiles):
        source = (block_of + 0.5).astype(jnp.int32) * block_len + t * per_tile + lane // time
        found = jnp.zeros((owners, LANES), jnp.int32)
        for part in range(chunks):
            table = ids_ref[2:3, part * LANES : (part + 1) * LANES]
            table = jnp.broadcast_to(table, (owners, LANES))
            if owners > 8:
                got = jnp.concatenate(
                    [take(table[i : i + 8], source[i : i + 8] & (LANES - 1)) for i in range(0, owners, 8)]
                )
            else:
                got = take(table, source & (LANES - 1))
            found = jnp.where((source >> 7) == part, got, found)
        exps.append(found)
    exps = jnp.concatenate(exps, axis=1)

    def put(index, values):
        for t in range(block_tiles):
            mask_ref[index, t] = values[:, t * LANES : (t + 1) * LANES]

    position = iota((owners, slots), 1)
    width = jnp.left_shift(jnp.ones_like(exps), exps)
    valid = ((position & (width - 1)) == 0).astype(jnp.int32)
    prefix = valid
    shift = 1
    while shift < slots:
        prefix = prefix + jnp.where(position >= shift, pltpu.roll(prefix, shift, 1), 0)
        shift *= 2
    count = jnp.max(prefix, axis=1, keepdims=True)
    move = position - (prefix - valid)
    scale = jnp.ones((owners, slots), jnp.float32)
    for s in range(log_time):
        scale = jnp.where(exps > s, scale * 0.5, scale)
        put(s, (exps > s).astype(jnp.float32))
    bits = int(math.log2(slots))
    held = jnp.where(valid == 1, move, 0)
    for b in range(bits):
        here = (held >> b) & 1
        moved = pltpu.roll(held, slots - (1 << b), 1)
        come = (moved >> b) & 1
        put(log_time + b, come.astype(jnp.float32))
        held = jnp.where(come == 1, moved, jnp.where(here == 1, 0, held))
    put(log_time + bits, (position < count).astype(jnp.float32))
    put(log_time + bits + 1, scale)


def predict_kernel(
    groups,
    owners,
    time,
    tiles,
    sky_ref,
    wide_ref,
    base_ref,
    order_ref,
    pair_ref,
    mask_ref,
    piece_ref,
    q_ref,
    sum_ref,
    send_ref,
    gather_ref,
    gain_send,
    gain_recv,
    piece_send,
    piece_recv,
):
    d = lax.axis_index("dir")
    p = lax.axis_index("bl")
    sources, cl, _ = wide_ref.shape
    per_group = sources // groups
    slots = order_ref.shape[2]
    block_len = slots // time
    block_tiles = slots // LANES
    per_tile = LANES // time
    log_time = int(math.log2(time))
    bits = int(math.log2(slots))

    barrier = pltpu.get_barrier_semaphore()
    for axis, me, size in (("dir", d, groups), ("bl", p, owners)):
        for step in range(1, size):
            pl.semaphore_signal(
                barrier, inc=1, device_id={axis: lax.rem(me + step, size)}, device_id_type=MESH
            )

    def gain_copy(step):
        other = lax.rem(d + step, groups)
        return pltpu.make_async_remote_copy(
            src_ref=pair_ref.at[other],
            dst_ref=gather_ref.at[d],
            send_sem=gain_send.at[step - 1],
            recv_sem=gain_recv.at[step - 1],
            device_id={"dir": other},
            device_id_type=MESH,
        )

    def piece_copy(step):
        return pltpu.make_async_remote_copy(
            src_ref=send_ref.at[step],
            dst_ref=piece_ref.at[p],
            send_sem=piece_send.at[step],
            recv_sem=piece_recv.at[step],
            device_id={"bl": lax.rem(p + 1 + step, owners)},
            device_id_type=MESH,
        )

    gather_ref[d] = pair_ref[d]
    pl.semaphore_wait(barrier, groups - 1 + owners - 1)
    for step in range(1, groups):
        gain_copy(step).start()
    freq = base_ref[groups]
    flux_sum = [base_ref[g] for g in range(groups)]
    lane = iota((cl, LANES), 1)

    def block_body(turn, carry):
        owner = lax.rem(p + 1 + turn, owners)
        for t in range(block_tiles):
            ln = slice(t * LANES, (t + 1) * LANES)
            u = order_ref[owner, 0:1, ln]
            v = order_ref[owner, 1:2, ln]
            w = order_ref[owner, 2:3, ln]
            q_ref[t] = sky_ref[0] * u + sky_ref[1] * v + sky_ref[2] * w

        @pl.when(turn > 0)
        def _():
            piece_copy(turn - 1).start()

        def tile_body(step, carry):
            for g in range(groups):

                def source(i, acc):
                    acc = list(acc)
                    index = g * per_group + i
                    amount = wide_ref[index]
                    for t in range(tiles):
                        turns = freq * q_ref[step * tiles + t, pl.ds(index, cl, stride=0), :]
                        x = turns - jnp.round(turns)
                        z = x * x
                        m = (z + P0) * z
                        s = x * (m + P1)
                        weighted = amount * s
                        acc[2 * t] = acc[2 * t] + weighted * s
                        acc[2 * t + 1] = acc[2 * t + 1] + weighted * ((m + P2) * (m + P3))
                    return tuple(acc)

                acc = tuple(jnp.zeros((cl, LANES), jnp.float32) for _ in range(2 * tiles))
                acc = lax.fori_loop(0, per_group, source, acc, unroll=UNROLL)
                for t in range(tiles):
                    sum_ref[step * tiles + t, 2 * g] = K0 * flux_sum[g] + K1 * acc[2 * t]
                    sum_ref[step * tiles + t, 2 * g + 1] = -K2 * acc[2 * t + 1]
            return carry

        lax.fori_loop(0, block_tiles // tiles, tile_body, 0)

        @pl.when(turn == 0)
        def _():
            for step in range(1, groups):
                gain_copy(step).wait()

        model = ([], [])
        for t in range(block_tiles):
            first_bl = owner * block_len + t * per_tile
            chunk = pl.multiple_of((first_bl // LANES) * LANES, LANES)
            index = first_bl % LANES + lane // time
            model_r = jnp.zeros((cl, LANES), jnp.float32)
            model_i = jnp.zeros((cl, LANES), jnp.float32)
            for g in range(groups):
                gr = take(gather_ref[g, 0, :, pl.ds(chunk, LANES)], index)
                gi = take(gather_ref[g, 1, :, pl.ds(chunk, LANES)], index)
                real, imag = sum_ref[t, 2 * g], sum_ref[t, 2 * g + 1]
                model_r = model_r + (real * gr - imag * gi)
                model_i = model_i + (real * gi + imag * gr)
            model[0].append(model_r)
            model[1].append(model_i)

        def wide(index):
            return jnp.concatenate(
                [mask_ref[index, t, pl.ds(owner, cl, stride=0), :] for t in range(block_tiles)], axis=1
            )

        for z in range(2):
            x = jnp.concatenate(model[z], axis=1) * wide(log_time + bits + 1)
            for s in range(log_time):
                x = x + wide(s) * pltpu.roll(x, slots - (1 << s), 1)
            for b in range(bits):
                x = jnp.where(wide(log_time + b) > 0.5, pltpu.roll(x, slots - (1 << b), 1), x)
            send_ref[turn, z] = jnp.where(wide(log_time + bits) > 0.5, x, 0.0)
        return carry

    lax.fori_loop(0, owners, block_body, 0)
    piece_ref[p] = send_ref[owners - 1]
    for step in range(owners - 1):
        piece_copy(step).wait()


def place_kernel(start_ref, piece_ref, observed_ref, out_ref, total_ref):
    owners, _, cl, slots = piece_ref.shape
    capacity = observed_ref.shape[2]
    total_ref[...] = jnp.zeros_like(total_ref)
    position = iota((cl, LANES), 1)
    for index in range(owners):
        start = start_ref[0, index]
        low = start & (LANES - 1)
        base = pl.multiple_of(start - low, LANES)
        for z in range(2):
            spun = [
                pltpu.roll(piece_ref[index, z, :, pl.ds(t * LANES, LANES)], low, 1)
                for t in range(slots // LANES)
            ]
            for t in range(slots // LANES + 1):
                value = jnp.zeros((cl, LANES), jnp.float32)
                if t < slots // LANES:
                    value = jnp.where(position >= low, spun[t], value)
                if t > 0:
                    value = jnp.where(position < low, spun[t - 1], value)
                lanes = pl.ds(base + t * LANES, LANES)
                total_ref[z, :, lanes] = total_ref[z, :, lanes] + value
    for z in range(2):
        out_ref[:, z, :] = observed_ref[:, z, :] - total_ref[z, :, pl.ds(0, capacity)]


def on_device(
    observed,
    baseline_uvw_rows,
    frequencies,
    source_offset,
    source_flux,
    source_group,
    direction_gain,
    station_first,
    station_second,
    average_exponent,
    owner_plan,
):
    owners = lax.axis_size("bl")
    groups = lax.axis_size("dir")
    cl, _, capacity = observed.shape
    bl_dev = station_first.shape[0] // owners
    rows = baseline_uvw_rows.shape[1]
    time = rows // bl_dev
    slots = rows // owners
    tiles = slots // LANES
    sources = source_group.shape[0]
    ids = jnp.stack([station_first, station_second, average_exponent])
    ids = lax.dynamic_slice_in_dim(ids, lax.axis_index("bl") * bl_dev, bl_dev, 1)
    vmem = pl.BlockSpec(memory_space=pltpu.VMEM)
    smem = pl.BlockSpec(memory_space=pltpu.SMEM)
    masks = int(math.log2(time)) + int(math.log2(slots)) + 2
    f32 = jnp.float32
    shape = jax.ShapeDtypeStruct
    *prepared, starts = pl.pallas_call(
        functools.partial(prepare_kernel, groups, owners, time),
        out_shape=(
            shape((3, sources, LANES), f32),
            shape((sources, cl, LANES), f32),
            shape((groups + 1, cl, LANES), f32),
            shape((owners, 3, slots), f32),
            shape((groups, 2, cl, bl_dev), f32),
            shape((masks, tiles, owners, LANES), f32),
            shape((1, LANES), jnp.int32),
        ),
        in_specs=[vmem] * 9 + [smem],
        out_specs=(vmem,) * 7,
        scratch_shapes=[pltpu.VMEM((groups, 2, cl, direction_gain.shape[3]), f32)],
        compiler_params=pltpu.CompilerParams(vmem_limit_bytes=32 << 20),
        name="prepare",
    )(
        baseline_uvw_rows,
        frequencies.reshape(1, -1),
        source_offset,
        source_flux,
        source_group.reshape(1, -1),
        direction_gain,
        ids,
        average_exponent.reshape(owners, bl_dev),
        owner_plan,
        owner_plan,
    )
    dma = pltpu.SemaphoreType.DMA
    pieces = pl.pallas_call(
        functools.partial(predict_kernel, groups, owners, time, min(4, tiles)),
        out_shape=shape((owners, 2, cl, slots), f32),
        in_specs=[vmem] * 6,
        out_specs=vmem,
        scratch_shapes=[
            pltpu.VMEM((tiles, sources, LANES), f32),
            pltpu.VMEM((tiles, 2 * groups, cl, LANES), f32),
            pltpu.VMEM((owners, 2, cl, slots), f32),
            pltpu.VMEM((groups, 2, cl, bl_dev), f32),
            dma((groups - 1,)),
            dma((groups - 1,)),
            dma((owners - 1,)),
            dma((owners - 1,)),
        ],
        compiler_params=pltpu.CompilerParams(
            vmem_limit_bytes=32 << 20, collective_id=0, has_side_effects=True
        ),
        name="predict",
    )(*prepared)
    return pl.pallas_call(
        place_kernel,
        out_shape=jax.ShapeDtypeStruct(observed.shape, f32),
        in_specs=[smem, vmem, vmem],
        out_specs=vmem,
        scratch_shapes=[pltpu.VMEM((2, cl, capacity + slots + LANES), f32)],
        compiler_params=pltpu.CompilerParams(vmem_limit_bytes=32 << 20),
        name="place",
    )(starts, pieces, observed)


def solution(mesh):
    placed = (
        P("dir", None, "bl"),
        P(None, "bl"),
        P(),
        P(),
        P(),
        P(),
        P("dir", None, None, None),
        P(),
        P(),
        P(),
        P(),
    )
    return jax.shard_map(
        on_device, mesh=mesh, in_specs=placed, out_specs=P("dir", None, "bl"), check_vma=False
    )
```

```python
import functools
import math

import jax
import jax.numpy as jnp
from jax import lax
from jax.experimental import pallas as pl
from jax.experimental.pallas import tpu as pltpu
from jax.sharding import PartitionSpec as P

LANES = 128
UNROLL = 32
MESH = pl.DeviceIdType.MESH
HIGH = lax.Precision.HIGHEST
NT = (((1,), (1,)), ((), ()))
P0, P1, P2, P3 = -2.2636507847492298, 1.3870216243251186, 4.937789609959605, 0.5033641130059734
K0, K1, K2 = 0.9997897140197886, -10.245898871410082, 1.823099221649536


def iota(shape, axis):
    return lax.broadcasted_iota(jnp.int32, shape, axis)


def take(values, index):
    return jnp.take_along_axis(values, index, axis=1, mode="promise_in_bounds")


def prepare_kernel(
    groups,
    owners,
    time,
    uvw_ref,
    freq_ref,
    offs_ref,
    flux_ref,
    group_ref,
    gain_ref,
    ids_ref,
    exps_ref,
    plan_ref,
    plan_smem,
    sky_ref,
    wide_ref,
    base_ref,
    order_ref,
    pair_ref,
    mask_ref,
    start_ref,
    table_ref,
):
    d = lax.axis_index("dir")
    p = lax.axis_index("bl")
    cl = wide_ref.shape[1]
    sources = offs_ref.shape[1]
    per_group = sources // groups
    bl_dev = ids_ref.shape[1]
    block_len = bl_dev // owners
    slots = block_len * time
    block_tiles = slots // LANES
    per_tile = LANES // time
    log_time = int(math.log2(time))
    chunks = bl_dev // LANES

    for k in range(owners):
        order_ref[plan_smem[p, k]] = uvw_ref[:, k * slots : (k + 1) * slots]
    plan = plan_ref[...].astype(jnp.float32)
    own_plan = jnp.sum(
        jnp.where(iota((owners, owners), 0) == p, plan, 0.0), axis=0, keepdims=True
    )
    held_by = jnp.abs(own_plan - iota((owners, owners), 0).astype(jnp.float32)) < 0.5
    block_of = jnp.sum(
        jnp.where(held_by, iota((owners, owners), 1).astype(jnp.float32), 0.0), axis=1, keepdims=True
    )

    member_row = group_ref[...].astype(jnp.float32)
    eye = (iota((sources, sources), 0) == iota((sources, sources), 1)).astype(jnp.float32)
    member_col = lax.dot_general(eye, member_row, NT, precision=HIGH)
    earlier = iota((sources, sources), 0) < iota((sources, sources), 1)
    same = (jnp.abs(member_col - member_row) < 0.5) & earlier
    rank = jnp.sum(same.astype(jnp.float32), axis=0, keepdims=True)
    place = (member_row * per_group + rank + 0.5).astype(jnp.int32)
    pick = (iota((sources, sources), 0) == place).astype(jnp.float32)
    offs = lax.dot_general(pick, offs_ref[...], NT, precision=HIGH)
    east, north = offs[:, 0:1], offs[:, 1:2]
    depth = jnp.sqrt(1.0 - east * east - north * north) - 1.0
    sky_ref[0] = jnp.broadcast_to(east, sky_ref.shape[1:])
    sky_ref[1] = jnp.broadcast_to(north, sky_ref.shape[1:])
    sky_ref[2] = jnp.broadcast_to(depth, sky_ref.shape[1:])
    channel = iota((cl, flux_ref.shape[0]), 1) == d * cl + iota((cl, flux_ref.shape[0]), 0)
    channel = channel.astype(jnp.float32)
    own_flux = jnp.dot(channel, flux_ref[...], precision=HIGH)
    flux = lax.dot_general(own_flux, pick, NT, precision=HIGH)
    for k in range(sources):
        wide_ref[k] = jnp.broadcast_to(flux[:, k : k + 1], (cl, LANES))
    for g in range(groups):
        part = jnp.sum(flux[:, g * per_group : (g + 1) * per_group], axis=1, keepdims=True)
        base_ref[g] = jnp.broadcast_to(part, (cl, LANES))
    freq = jnp.sum(channel * freq_ref[...], axis=1, keepdims=True)
    base_ref[groups] = jnp.broadcast_to(freq, (cl, LANES))

    lane = iota((owners, LANES), 1)
    row = iota((owners, LANES), 0)
    station_total = gain_ref.shape[3]
    for g in range(groups):
        for z in range(2):
            table_ref[g, z] = gain_ref[0, g * cl : (g + 1) * cl, z, :]
    for chunk in range(chunks):
        lanes = pl.ds(chunk * LANES, LANES)
        where_from = jnp.where((chunk * LANES + lane) // block_len == row, block_of, 0.0)
        where_from = (jnp.sum(where_from, axis=0, keepdims=True) + 0.5).astype(jnp.int32)
        source = where_from * block_len + (chunk * LANES + iota((1, LANES), 1)) % block_len
        source = jnp.broadcast_to(source, (cl, LANES))
        looked = []
        for which in range(2):
            ids = jnp.zeros((cl, LANES), jnp.int32)
            for part in range(chunks):
                table = ids_ref[which : which + 1, part * LANES : (part + 1) * LANES]
                table = jnp.broadcast_to(table, (cl, LANES))
                ids = jnp.where((source >> 7) == part, take(table, source & (LANES - 1)), ids)
            low, high = ids & (LANES - 1), ids >> 7
            rows = []
            for g in range(groups):
                for z in range(2):
                    total = jnp.zeros((cl, LANES), jnp.float32)
                    for part in range(station_total // LANES):
                        table = table_ref[g, z, :, pl.ds(part * LANES, LANES)]
                        total = jnp.where(high == part, take(table, low), total)
                    rows.append(total)
            looked.append(rows)
        first, second = looked
        for g in range(groups):
            ar, ai, br, bi = first[2 * g], first[2 * g + 1], second[2 * g], second[2 * g + 1]
            pair_ref[g, 0, :, lanes] = ar * br + ai * bi
            pair_ref[g, 1, :, lanes] = ai * br - ar * bi

    rows_all = jnp.right_shift(jnp.full(exps_ref.shape, time, jnp.int32), exps_ref[...])
    rows_all = rows_all.astype(jnp.float32)
    to_owner = jnp.zeros((owners, 1), jnp.float32)
    for k in range(owners):
        count = jnp.sum(rows_all[:, k * block_len : (k + 1) * block_len], axis=1, keepdims=True)
        to_owner = to_owner + jnp.where(plan_ref[:, k : k + 1] == p, count, 0.0)
    starts = jnp.sum(jnp.where(row < lane, to_owner, 0.0), axis=0, keepdims=True)
    start_ref[...] = (starts + 0.5).astype(jnp.int32)

    exps = []
    for t in range(block_tiles):
        source = (block_of + 0.5).astype(jnp.int32) * block_len + t * per_tile + lane // time
        found = jnp.zeros((owners, LANES), jnp.int32)
        for part in range(chunks):
            table = ids_ref[2:3, part * LANES : (part + 1) * LANES]
            table = jnp.broadcast_to(table, (owners, LANES))
            if owners > 8:
                got = jnp.concatenate(
                    [take(table[i : i + 8], source[i : i + 8] & (LANES - 1)) for i in range(0, owners, 8)]
                )
            else:
                got = take(table, source & (LANES - 1))
            found = jnp.where((source >> 7) == part, got, found)
        exps.append(found)
    exps = jnp.concatenate(exps, axis=1)

    def put(index, values):
        for t in range(block_tiles):
            mask_ref[index, t] = values[:, t * LANES : (t + 1) * LANES]

    position = iota((owners, slots), 1)
    width = jnp.left_shift(jnp.ones_like(exps), exps)
    valid = ((position & (width - 1)) == 0).astype(jnp.int32)
    prefix = valid
    shift = 1
    while shift < slots:
        prefix = prefix + jnp.where(position >= shift, pltpu.roll(prefix, shift, 1), 0)
        shift *= 2
    count = jnp.max(prefix, axis=1, keepdims=True)
    move = position - (prefix - valid)
    scale = jnp.ones((owners, slots), jnp.float32)
    for s in range(log_time):
        scale = jnp.where(exps > s, scale * 0.5, scale)
        put(s, (exps > s).astype(jnp.float32))
    bits = int(math.log2(slots))
    held = jnp.where(valid == 1, move, 0)
    for b in range(bits):
        here = (held >> b) & 1
        moved = pltpu.roll(held, slots - (1 << b), 1)
        come = (moved >> b) & 1
        put(log_time + b, come.astype(jnp.float32))
        held = jnp.where(come == 1, moved, jnp.where(here == 1, 0, held))
    put(log_time + bits, (position < count).astype(jnp.float32))
    put(log_time + bits + 1, scale)


def predict_kernel(
    groups,
    owners,
    time,
    tiles,
    sky_ref,
    wide_ref,
    base_ref,
    order_ref,
    pair_ref,
    mask_ref,
    piece_ref,
    q_ref,
    sum_ref,
    early_ref,
    send_ref,
    gather_ref,
    gain_send,
    gain_recv,
    piece_send,
    piece_recv,
):
    d = lax.axis_index("dir")
    p = lax.axis_index("bl")
    sources, cl, _ = wide_ref.shape
    per_group = sources // groups
    slots = order_ref.shape[2]
    block_len = slots // time
    block_tiles = slots // LANES
    per_tile = LANES // time
    log_time = int(math.log2(time))
    bits = int(math.log2(slots))

    barrier = pltpu.get_barrier_semaphore()
    for axis, me, size in (("dir", d, groups), ("bl", p, owners)):
        for step in range(1, size):
            pl.semaphore_signal(
                barrier, inc=1, device_id={axis: lax.rem(me + step, size)}, device_id_type=MESH
            )

    def gain_copy(step):
        other = lax.rem(d + step, groups)
        return pltpu.make_async_remote_copy(
            src_ref=pair_ref.at[other],
            dst_ref=gather_ref.at[d],
            send_sem=gain_send.at[step - 1],
            recv_sem=gain_recv.at[step - 1],
            device_id={"dir": other},
            device_id_type=MESH,
        )

    def piece_copy(step):
        return pltpu.make_async_remote_copy(
            src_ref=send_ref.at[step],
            dst_ref=piece_ref.at[p],
            send_sem=piece_send.at[step],
            recv_sem=piece_recv.at[step],
            device_id={"bl": lax.rem(p + 1 + step, owners)},
            device_id_type=MESH,
        )

    gather_ref[d] = pair_ref[d]
    freq = base_ref[groups]
    flux_sum = [base_ref[g] for g in range(groups)]
    lane = iota((cl, LANES), 1)
    steps = block_tiles // tiles

    def owner_of(turn):
        return lax.rem(p + 1 + turn, owners)

    def add_sources(owner, step, keep_ref):
        for t in range(tiles):
            ln = pl.ds(pl.multiple_of((step * tiles + t) * LANES, LANES), LANES)
            u = order_ref[owner, 0:1, ln]
            v = order_ref[owner, 1:2, ln]
            w = order_ref[owner, 2:3, ln]
            q_ref[t] = sky_ref[0] * u + sky_ref[1] * v + sky_ref[2] * w
        for g in range(groups):

            def source(i, acc):
                acc = list(acc)
                index = g * per_group + i
                amount = wide_ref[index]
                for t in range(tiles):
                    turns = freq * q_ref[t, pl.ds(index, cl, stride=0), :]
                    x = turns - jnp.round(turns)
                    z = x * x
                    m = (z + P0) * z
                    s = x * (m + P1)
                    weighted = amount * s
                    acc[2 * t] = acc[2 * t] + weighted * s
                    acc[2 * t + 1] = acc[2 * t + 1] + weighted * ((m + P2) * (m + P3))
                return tuple(acc)

            acc = tuple(jnp.zeros((cl, LANES), jnp.float32) for _ in range(2 * tiles))
            acc = lax.fori_loop(0, per_group, source, acc, unroll=UNROLL)
            for t in range(tiles):
                keep_ref[step * tiles + t, 2 * g] = K0 * flux_sum[g] + K1 * acc[2 * t]
                keep_ref[step * tiles + t, 2 * g + 1] = -K2 * acc[2 * t + 1]

    def finish(turn, keep_ref):
        owner = owner_of(turn)
        model = ([], [])
        for t in range(block_tiles):
            first_bl = owner * block_len + t * per_tile
            chunk = pl.multiple_of((first_bl // LANES) * LANES, LANES)
            index = first_bl % LANES + lane // time
            model_r = jnp.zeros((cl, LANES), jnp.float32)
            model_i = jnp.zeros((cl, LANES), jnp.float32)
            for g in range(groups):
                gr = take(gather_ref[g, 0, :, pl.ds(chunk, LANES)], index)
                gi = take(gather_ref[g, 1, :, pl.ds(chunk, LANES)], index)
                real, imag = keep_ref[t, 2 * g], keep_ref[t, 2 * g + 1]
                model_r = model_r + (real * gr - imag * gi)
                model_i = model_i + (real * gi + imag * gr)
            model[0].append(model_r)
            model[1].append(model_i)

        def wide(index):
            return jnp.concatenate(
                [mask_ref[index, t, pl.ds(owner, cl, stride=0), :] for t in range(block_tiles)], axis=1
            )

        scale = wide(log_time + bits + 1)
        both = [jnp.concatenate(model[z], axis=1) * scale for z in range(2)]
        for s in range(log_time):
            mask = wide(s)
            both = [x + mask * pltpu.roll(x, slots - (1 << s), 1) for x in both]
        for b in range(bits):
            mask = wide(log_time + b) > 0.5
            both = [jnp.where(mask, pltpu.roll(x, slots - (1 << b), 1), x) for x in both]
        mask = wide(log_time + bits) > 0.5
        return [jnp.where(mask, x, 0.0) for x in both]

    def send(turn, done):
        for z in range(2):
            send_ref[turn, z] = done[z]

    def early(index, carry):
        turn = index // steps

        @pl.when(index == steps)
        def _():
            pl.semaphore_wait(barrier, groups - 1 + owners - 1)
            for step in range(1, groups):
                gain_copy(step).start()

        add_sources(owner_of(turn), lax.rem(index, steps), early_ref.at[turn])
        return carry

    lax.fori_loop(0, 2 * steps, early, 0)
    for step in range(1, groups):
        gain_copy(step).wait()
    for step in range(steps):
        done = [turn for turn in range(2) if min(turn, steps - 1) == step]
        for turn in done:
            send(turn, finish(turn, early_ref.at[turn]))
        add_sources(owner_of(2), step, sum_ref)
        for turn in done:
            piece_copy(turn).start()

    def block_body(turn, carry):
        for step in range(steps):
            if step == 0:
                send(turn - 1, finish(turn - 1, sum_ref))
            add_sources(owner_of(turn), step, sum_ref)
            if step == 0:
                piece_copy(turn - 1).start()
        return carry

    lax.fori_loop(3, owners, block_body, 0)
    done = finish(owners - 1, sum_ref)
    for z in range(2):
        piece_ref[p, z] = done[z]
    for step in range(owners - 1):
        piece_copy(step).wait()


def place_kernel(start_ref, piece_ref, observed_ref, out_ref, total_ref):
    owners, _, cl, slots = piece_ref.shape
    capacity = observed_ref.shape[2]
    total_ref[...] = jnp.zeros_like(total_ref)
    position = iota((cl, LANES), 1)
    for index in range(owners):
        start = start_ref[0, index]
        low = start & (LANES - 1)
        base = pl.multiple_of(start - low, LANES)
        for z in range(2):
            spun = [
                pltpu.roll(piece_ref[index, z, :, pl.ds(t * LANES, LANES)], low, 1)
                for t in range(slots // LANES)
            ]
            for t in range(slots // LANES + 1):
                lanes = pl.ds(pl.multiple_of(base + t * LANES, LANES), LANES)
                if t == 0:
                    value = jnp.where(position >= low, spun[t], total_ref[z, :, lanes])
                elif t < slots // LANES:
                    value = jnp.where(position >= low, spun[t], spun[t - 1])
                else:
                    value = jnp.where(position >= low, 0.0, spun[t - 1])
                total_ref[z, :, lanes] = value
    for z in range(2):
        out_ref[:, z, :] = observed_ref[:, z, :] - total_ref[z, :, pl.ds(0, capacity)]


def on_device(
    observed,
    baseline_uvw_rows,
    frequencies,
    source_offset,
    source_flux,
    source_group,
    direction_gain,
    station_first,
    station_second,
    average_exponent,
    owner_plan,
):
    owners = lax.axis_size("bl")
    groups = lax.axis_size("dir")
    cl, _, capacity = observed.shape
    bl_dev = station_first.shape[0] // owners
    rows = baseline_uvw_rows.shape[1]
    time = rows // bl_dev
    slots = rows // owners
    tiles = slots // LANES
    sources = source_group.shape[0]
    ids = jnp.stack([station_first, station_second, average_exponent])
    ids = lax.dynamic_slice_in_dim(ids, lax.axis_index("bl") * bl_dev, bl_dev, 1)
    vmem = pl.BlockSpec(memory_space=pltpu.VMEM)
    smem = pl.BlockSpec(memory_space=pltpu.SMEM)
    masks = int(math.log2(time)) + int(math.log2(slots)) + 2
    f32 = jnp.float32
    shape = jax.ShapeDtypeStruct
    *prepared, starts = pl.pallas_call(
        functools.partial(prepare_kernel, groups, owners, time),
        out_shape=(
            shape((3, sources, LANES), f32),
            shape((sources, cl, LANES), f32),
            shape((groups + 1, cl, LANES), f32),
            shape((owners, 3, slots), f32),
            shape((groups, 2, cl, bl_dev), f32),
            shape((masks, tiles, owners, LANES), f32),
            shape((1, LANES), jnp.int32),
        ),
        in_specs=[vmem] * 9 + [smem],
        out_specs=(vmem,) * 7,
        scratch_shapes=[pltpu.VMEM((groups, 2, cl, direction_gain.shape[3]), f32)],
        compiler_params=pltpu.CompilerParams(vmem_limit_bytes=32 << 20),
        name="prepare",
    )(
        baseline_uvw_rows,
        frequencies.reshape(1, -1),
        source_offset,
        source_flux,
        source_group.reshape(1, -1),
        direction_gain,
        ids,
        average_exponent.reshape(owners, bl_dev),
        owner_plan,
        owner_plan,
    )
    dma = pltpu.SemaphoreType.DMA
    pieces = pl.pallas_call(
        functools.partial(predict_kernel, groups, owners, time, min(4, tiles)),
        out_shape=shape((owners, 2, cl, slots), f32),
        in_specs=[vmem] * 6,
        out_specs=vmem,
        scratch_shapes=[
            pltpu.VMEM((min(4, tiles), sources, LANES), f32),
            pltpu.VMEM((tiles, 2 * groups, cl, LANES), f32),
            pltpu.VMEM((2, tiles, 2 * groups, cl, LANES), f32),
            pltpu.VMEM((owners - 1, 2, cl, slots), f32),
            pltpu.VMEM((groups, 2, cl, bl_dev), f32),
            dma((groups - 1,)),
            dma((groups - 1,)),
            dma((owners - 1,)),
            dma((owners - 1,)),
        ],
        compiler_params=pltpu.CompilerParams(
            vmem_limit_bytes=32 << 20, collective_id=0, has_side_effects=True
        ),
        name="predict",
    )(*prepared)
    return pl.pallas_call(
        place_kernel,
        out_shape=jax.ShapeDtypeStruct(observed.shape, f32),
        in_specs=[smem, vmem, vmem],
        out_specs=vmem,
        scratch_shapes=[pltpu.VMEM((2, cl, capacity + slots + LANES), f32)],
        compiler_params=pltpu.CompilerParams(vmem_limit_bytes=32 << 20),
        name="place",
    )(starts, pieces, observed)


def solution(mesh):
    placed = (
        P("dir", None, "bl"),
        P(None, "bl"),
        P(),
        P(),
        P(),
        P(),
        P("dir", None, None, None),
        P(),
        P(),
        P(),
        P(),
    )
    return jax.shard_map(
        on_device, mesh=mesh, in_specs=placed, out_specs=P("dir", None, "bl"), check_vma=False
    )
```

```python
import functools
import math

import jax
import jax.numpy as jnp
from jax import lax
from jax.experimental import pallas as pl
from jax.experimental.pallas import tpu as pltpu
from jax.sharding import PartitionSpec as P

LANES = 128
UNROLL = 32
EARLY = 3
MESH = pl.DeviceIdType.MESH
HIGH = lax.Precision.HIGHEST
NT = (((1,), (1,)), ((), ()))
P0, P1, P2, P3 = -2.2636507847492298, 1.3870216243251186, 4.937789609959605, 0.5033641130059734
K0, K1, K2 = 0.9997897140197886, -10.245898871410082, 1.823099221649536


def iota(shape, axis):
    return lax.broadcasted_iota(jnp.int32, shape, axis)


def flip(a, b, size):
    bits = range(int(math.log2(size)))
    return sum(((a // 2**i + b // 2**i) % 2) * 2**i for i in bits)


def take(values, index):
    return jnp.take_along_axis(values, index, axis=1, mode="promise_in_bounds")


def prepare_kernel(
    groups,
    owners,
    time,
    *refs,
):
    inputs = refs[:11]
    (
    sky_ref,
    wide_ref,
    base_ref,
    order_ref,
    pair_ref,
    mask_ref,
    start_ref,
    table_ref,
    uvw_ref,
    freq_ref,
    offs_ref,
    flux_ref,
    group_ref,
    gain_ref,
    first_ref,
    second_ref,
    exps_ref,
    plan_ref,
    plan_smem,
    sem,
    ) = refs[11:]
    d = lax.axis_index("dir")
    p = lax.axis_index("bl")
    cl = wide_ref.shape[1]
    sources = offs_ref.shape[1]
    per_group = sources // groups
    bl_dev = first_ref.shape[1]
    own = pl.ds(pl.multiple_of(p * bl_dev, bl_dev), bl_dev)
    held = refs[19:30]
    copies = {}
    for index in (4, 2, 3, 1, 9, 10, 0, 5, 6, 7, 8):
        source = inputs[index].at[:, own] if index in (6, 7) else inputs[index]
        copies[index] = pltpu.make_async_copy(source, held[index], sem.at[index])
        copies[index].start()

    def arrive(*indices):
        for index in indices:
            copies[index].wait()

    block_len = bl_dev // owners
    slots = block_len * time
    block_tiles = slots // LANES
    per_tile = LANES // time
    log_time = int(math.log2(time))
    chunks = bl_dev // LANES

    arrive(4, 2, 3, 1)
    member_row = group_ref[...].astype(jnp.float32)
    eye = (iota((sources, sources), 0) == iota((sources, sources), 1)).astype(jnp.float32)
    member_col = lax.dot_general(eye, member_row, NT, precision=HIGH)
    earlier = iota((sources, sources), 0) < iota((sources, sources), 1)
    same = (jnp.abs(member_col - member_row) < 0.5) & earlier
    rank = jnp.sum(same.astype(jnp.float32), axis=0, keepdims=True)
    place = (member_row * per_group + rank + 0.5).astype(jnp.int32)
    pick = (iota((sources, sources), 0) == place).astype(jnp.float32)
    offs = lax.dot_general(pick, offs_ref[...], NT, precision=HIGH)
    east, north = offs[:, 0:1], offs[:, 1:2]
    depth = jnp.sqrt(1.0 - east * east - north * north) - 1.0
    sky_ref[0] = jnp.broadcast_to(east, sky_ref.shape[1:])
    sky_ref[1] = jnp.broadcast_to(north, sky_ref.shape[1:])
    sky_ref[2] = jnp.broadcast_to(depth, sky_ref.shape[1:])
    channel = iota((cl, flux_ref.shape[0]), 1) == d * cl + iota((cl, flux_ref.shape[0]), 0)
    channel = channel.astype(jnp.float32)
    own_flux = jnp.dot(channel, flux_ref[...], precision=HIGH)
    flux = lax.dot_general(own_flux, pick, NT, precision=HIGH)
    for k in range(sources):
        wide_ref[k] = jnp.broadcast_to(flux[:, k : k + 1], (cl, LANES))
    for g in range(groups):
        part = jnp.sum(flux[:, g * per_group : (g + 1) * per_group], axis=1, keepdims=True)
        base_ref[g] = jnp.broadcast_to(part, (cl, LANES))
    freq = jnp.sum(channel * freq_ref[...], axis=1, keepdims=True)
    base_ref[groups] = jnp.broadcast_to(freq, (cl, LANES))

    arrive(9, 10, 0)
    for k in range(owners):
        order_ref[plan_smem[p, k]] = uvw_ref[:, k * slots : (k + 1) * slots]
    plan = plan_ref[...].astype(jnp.float32)
    own_plan = jnp.sum(
        jnp.where(iota((owners, owners), 0) == p, plan, 0.0), axis=0, keepdims=True
    )
    held_by = jnp.abs(own_plan - iota((owners, owners), 0).astype(jnp.float32)) < 0.5
    block_of = jnp.sum(
        jnp.where(held_by, iota((owners, owners), 1).astype(jnp.float32), 0.0), axis=1, keepdims=True
    )

    arrive(5, 6, 7, 8)
    lane = iota((owners, LANES), 1)
    row = iota((owners, LANES), 0)
    station_total = gain_ref.shape[3]
    for g in range(groups):
        for z in range(2):
            table_ref[g, z] = gain_ref[0, g * cl : (g + 1) * cl, z, :]
    for chunk in range(chunks):
        lanes = pl.ds(chunk * LANES, LANES)
        where_from = jnp.where((chunk * LANES + lane) // block_len == row, block_of, 0.0)
        where_from = (jnp.sum(where_from, axis=0, keepdims=True) + 0.5).astype(jnp.int32)
        source = where_from * block_len + (chunk * LANES + iota((1, LANES), 1)) % block_len
        source = jnp.broadcast_to(source, (cl, LANES))
        looked = []
        for which in range(2):
            ids = jnp.zeros((cl, LANES), jnp.int32)
            for part in range(chunks):
                table = (first_ref, second_ref)[which][:, part * LANES : (part + 1) * LANES]
                table = jnp.broadcast_to(table, (cl, LANES))
                ids = jnp.where((source >> 7) == part, take(table, source & (LANES - 1)), ids)
            low, high = ids & (LANES - 1), ids >> 7
            rows = []
            for g in range(groups):
                for z in range(2):
                    total = jnp.zeros((cl, LANES), jnp.float32)
                    for part in range(station_total // LANES):
                        table = table_ref[g, z, :, pl.ds(part * LANES, LANES)]
                        total = jnp.where(high == part, take(table, low), total)
                    rows.append(total)
            looked.append(rows)
        first, second = looked
        for g in range(groups):
            ar, ai, br, bi = first[2 * g], first[2 * g + 1], second[2 * g], second[2 * g + 1]
            pair_ref[g, 0, :, lanes] = ar * br + ai * bi
            pair_ref[g, 1, :, lanes] = ai * br - ar * bi

    exps_all = jnp.concatenate(
        [exps_ref[:, i * bl_dev : (i + 1) * bl_dev] for i in range(owners)], axis=0
    )
    rows_all = jnp.right_shift(jnp.full(exps_all.shape, time, jnp.int32), exps_all)
    rows_all = rows_all.astype(jnp.float32)
    to_owner = jnp.zeros((owners, 1), jnp.float32)
    for k in range(owners):
        count = jnp.sum(rows_all[:, k * block_len : (k + 1) * block_len], axis=1, keepdims=True)
        to_owner = to_owner + jnp.where(plan_ref[:, k : k + 1] == p, count, 0.0)
    starts = jnp.sum(jnp.where(row < lane, to_owner, 0.0), axis=0, keepdims=True)
    start_ref[...] = (starts + 0.5).astype(jnp.int32)

    exps = []
    for t in range(block_tiles):
        source = (block_of + 0.5).astype(jnp.int32) * block_len + t * per_tile + lane // time
        found = jnp.zeros((owners, LANES), jnp.int32)
        for part in range(chunks):
            begin = pl.multiple_of(p * bl_dev + part * LANES, LANES)
            table = exps_ref[:, pl.ds(begin, LANES)]
            table = jnp.broadcast_to(table, (owners, LANES))
            if owners > 8:
                got = jnp.concatenate(
                    [take(table[i : i + 8], source[i : i + 8] & (LANES - 1)) for i in range(0, owners, 8)]
                )
            else:
                got = take(table, source & (LANES - 1))
            found = jnp.where((source >> 7) == part, got, found)
        exps.append(found)
    exps = jnp.concatenate(exps, axis=1)

    def put(index, values):
        for t in range(block_tiles):
            mask_ref[index, t] = values[:, t * LANES : (t + 1) * LANES]

    position = iota((owners, slots), 1)
    width = jnp.left_shift(jnp.ones_like(exps), exps)
    valid = ((position & (width - 1)) == 0).astype(jnp.int32)
    prefix = valid
    shift = 1
    while shift < slots:
        prefix = prefix + jnp.where(position >= shift, pltpu.roll(prefix, shift, 1), 0)
        shift *= 2
    count = jnp.max(prefix, axis=1, keepdims=True)
    move = position - (prefix - valid)
    scale = jnp.ones((owners, slots), jnp.float32)
    for s in range(log_time):
        scale = jnp.where(exps > s, scale * 0.5, scale)
        put(s, (exps > s).astype(jnp.float32))
    bits = int(math.log2(slots))
    held = jnp.where(valid == 1, move, 0)
    for b in range(bits):
        here = (held >> b) & 1
        moved = pltpu.roll(held, slots - (1 << b), 1)
        come = (moved >> b) & 1
        put(log_time + b, come.astype(jnp.float32))
        held = jnp.where(come == 1, moved, jnp.where(here == 1, 0, held))
    put(log_time + bits, (position < count).astype(jnp.float32))
    put(log_time + bits + 1, scale)


def predict_kernel(
    groups,
    owners,
    time,
    tiles,
    sky_ref,
    wide_ref,
    base_ref,
    order_ref,
    pair_ref,
    mask_ref,
    piece_ref,
    q_ref,
    sum_ref,
    early_ref,
    send_ref,
    gather_ref,
    gain_send,
    gain_recv,
    piece_send,
    piece_recv,
):
    d = lax.axis_index("dir")
    p = lax.axis_index("bl")
    sources, cl, _ = wide_ref.shape
    per_group = sources // groups
    slots = order_ref.shape[2]
    block_len = slots // time
    block_tiles = slots // LANES
    per_tile = LANES // time
    log_time = int(math.log2(time))
    bits = int(math.log2(slots))

    barrier = pltpu.get_barrier_semaphore()
    for axis, me, size in (("dir", d, groups), ("bl", p, owners)):
        for step in range(1, size):
            pl.semaphore_signal(
                barrier, inc=1, device_id={axis: lax.rem(me + step, size)}, device_id_type=MESH
            )

    def owner_of(turn):
        return flip(p, owners - 1 - turn, owners)

    def gain_copy(step):
        other = lax.rem(d + step, groups)
        return pltpu.make_async_remote_copy(
            src_ref=pair_ref.at[other],
            dst_ref=gather_ref.at[d],
            send_sem=gain_send.at[step - 1],
            recv_sem=gain_recv.at[step - 1],
            device_id={"dir": other},
            device_id_type=MESH,
        )

    def piece_copy(step):
        return pltpu.make_async_remote_copy(
            src_ref=send_ref.at[step],
            dst_ref=piece_ref.at[p],
            send_sem=piece_send.at[step],
            recv_sem=piece_recv.at[step],
            device_id={"bl": owner_of(step)},
            device_id_type=MESH,
        )

    gather_ref[d] = pair_ref[d]
    freq = base_ref[groups]
    flux_sum = [base_ref[g] for g in range(groups)]
    lane = iota((cl, LANES), 1)
    steps = block_tiles // tiles

    def add_sources(owner, step, keep_ref, sent=()):
        for t in range(tiles):
            ln = pl.ds(pl.multiple_of((step * tiles + t) * LANES, LANES), LANES)
            u = order_ref[owner, 0:1, ln]
            v = order_ref[owner, 1:2, ln]
            w = order_ref[owner, 2:3, ln]
            q_ref[t] = sky_ref[0] * u + sky_ref[1] * v + sky_ref[2] * w
        for g in range(groups):

            def source(i, acc):
                acc = list(acc)
                index = g * per_group + i
                amount = wide_ref[index]
                for t in range(tiles):
                    turns = freq * q_ref[t, pl.ds(index, cl, stride=0), :]
                    x = turns - jnp.round(turns)
                    z = x * x
                    m = (z + P0) * z
                    s = x * (m + P1)
                    weighted = amount * s
                    acc[2 * t] = acc[2 * t] + weighted * s
                    acc[2 * t + 1] = acc[2 * t + 1] + weighted * ((m + P2) * (m + P3))
                return tuple(acc)

            acc = tuple(jnp.zeros((cl, LANES), jnp.float32) for _ in range(2 * tiles))
            acc = lax.fori_loop(0, per_group, source, acc, unroll=UNROLL)
            for t in range(tiles):
                keep_ref[step * tiles + t, 2 * g] = K0 * flux_sum[g] + K1 * acc[2 * t]
                keep_ref[step * tiles + t, 2 * g + 1] = -K2 * acc[2 * t + 1]
            if g == groups // 2 - 1:
                for done in sent:
                    piece_copy(done).start()

    def finish(turn, keep_ref):
        owner = owner_of(turn)
        model = ([], [])
        for t in range(block_tiles):
            first_bl = owner * block_len + t * per_tile
            chunk = pl.multiple_of((first_bl // LANES) * LANES, LANES)
            index = first_bl % LANES + lane // time
            model_r = jnp.zeros((cl, LANES), jnp.float32)
            model_i = jnp.zeros((cl, LANES), jnp.float32)
            for g in range(groups):
                gr = take(gather_ref[g, 0, :, pl.ds(chunk, LANES)], index)
                gi = take(gather_ref[g, 1, :, pl.ds(chunk, LANES)], index)
                real, imag = keep_ref[t, 2 * g], keep_ref[t, 2 * g + 1]
                model_r = model_r + (real * gr - imag * gi)
                model_i = model_i + (real * gi + imag * gr)
            model[0].append(model_r)
            model[1].append(model_i)

        def wide(index):
            return jnp.concatenate(
                [mask_ref[index, t, pl.ds(owner, cl, stride=0), :] for t in range(block_tiles)], axis=1
            )

        scale = wide(log_time + bits + 1)
        both = [jnp.concatenate(model[z], axis=1) * scale for z in range(2)]
        for s in range(log_time):
            mask = wide(s)
            both = [x + mask * pltpu.roll(x, slots - (1 << s), 1) for x in both]
        for b in range(bits):
            mask = wide(log_time + b) > 0.5
            both = [jnp.where(mask, pltpu.roll(x, slots - (1 << b), 1), x) for x in both]
        mask = wide(log_time + bits) > 0.5
        return [jnp.where(mask, x, 0.0) for x in both]

    def send(turn, done):
        for z in range(2):
            send_ref[turn, z] = done[z]

    def early(index, carry):
        turn = index // steps

        @pl.when(index == steps)
        def _():
            pl.semaphore_wait(barrier, groups - 1 + owners - 1)
            for step in range(1, groups):
                gain_copy(step).start()

        add_sources(owner_of(turn), lax.rem(index, steps), early_ref.at[turn])
        return carry

    lax.fori_loop(0, EARLY * steps, early, 0)
    for step in range(1, groups):
        gain_copy(step).wait()
    turn, ready, quota = EARLY, 0, 2 // steps if steps < 2 else 1
    kept = {turn: early_ref.at[turn] for turn in range(EARLY)}
    while ready < turn - 1:
        last = ready + quota * steps >= turn
        kept[turn] = sum_ref if last else early_ref.at[turn]
        for step in range(steps):
            now = list(range(ready, min(ready + quota, turn)))
            for done in now:
                send(done, finish(done, kept[done]))
            add_sources(owner_of(turn), step, kept[turn], now)
            ready += len(now)
        turn += 1

    def block_body(turn, carry):
        send(turn - 1, finish(turn - 1, sum_ref))
        add_sources(owner_of(turn), 0, sum_ref, [turn - 1])
        for step in range(1, steps):
            add_sources(owner_of(turn), step, sum_ref)
        return carry

    lax.fori_loop(turn, owners, block_body, 0)
    done = finish(owners - 1, sum_ref)
    for z in range(2):
        piece_ref[p, z] = done[z]
    for step in range(owners - 1):
        piece_copy(step).wait()


def place_kernel(start_ref, piece_ref, observed_ref, out_ref, total_ref):
    owners, _, cl, slots = piece_ref.shape
    capacity = observed_ref.shape[2]
    total_ref[...] = jnp.zeros_like(total_ref)
    position = iota((cl, LANES), 1)
    for index in range(owners):
        start = start_ref[0, index]
        low = start & (LANES - 1)
        base = pl.multiple_of(start - low, LANES)
        for z in range(2):
            spun = [
                pltpu.roll(piece_ref[index, z, :, pl.ds(t * LANES, LANES)], low, 1)
                for t in range(slots // LANES)
            ]
            for t in range(slots // LANES + 1):
                lanes = pl.ds(pl.multiple_of(base + t * LANES, LANES), LANES)
                if t == 0:
                    value = jnp.where(position >= low, spun[t], total_ref[z, :, lanes])
                elif t < slots // LANES:
                    value = jnp.where(position >= low, spun[t], spun[t - 1])
                else:
                    value = jnp.where(position >= low, 0.0, spun[t - 1])
                total_ref[z, :, lanes] = value
    for z in range(2):
        out_ref[:, z, :] = observed_ref[:, z, :] - total_ref[z, :, pl.ds(0, capacity)]


def on_device(
    observed,
    baseline_uvw_rows,
    frequencies,
    source_offset,
    source_flux,
    source_group,
    direction_gain,
    station_first,
    station_second,
    average_exponent,
    owner_plan,
):
    owners = lax.axis_size("bl")
    groups = lax.axis_size("dir")
    cl, _, capacity = observed.shape
    bl_dev = station_first.shape[0] // owners
    rows = baseline_uvw_rows.shape[1]
    time = rows // bl_dev
    slots = rows // owners
    tiles = slots // LANES
    sources = source_group.shape[0]
    vmem = pl.BlockSpec(memory_space=pltpu.VMEM)
    smem = pl.BlockSpec(memory_space=pltpu.SMEM)
    masks = int(math.log2(time)) + int(math.log2(slots)) + 2
    f32 = jnp.float32
    shape = jax.ShapeDtypeStruct
    *prepared, starts = pl.pallas_call(
        functools.partial(prepare_kernel, groups, owners, time),
        out_shape=(
            shape((3, sources, LANES), f32),
            shape((sources, cl, LANES), f32),
            shape((groups + 1, cl, LANES), f32),
            shape((owners, 3, slots), f32),
            shape((groups, 2, cl, bl_dev), f32),
            shape((masks, tiles, owners, LANES), f32),
            shape((1, LANES), jnp.int32),
        ),
        in_specs=[pl.BlockSpec(memory_space=pltpu.HBM)] * 11,
        out_specs=(vmem,) * 7,
        scratch_shapes=[
            pltpu.VMEM((groups, 2, cl, direction_gain.shape[3]), f32),
            pltpu.VMEM(baseline_uvw_rows.shape, f32),
            pltpu.VMEM((1, frequencies.shape[0]), f32),
            pltpu.VMEM(source_offset.shape, f32),
            pltpu.VMEM(source_flux.shape, f32),
            pltpu.VMEM((1, sources), jnp.int32),
            pltpu.VMEM(direction_gain.shape, f32),
            pltpu.VMEM((1, bl_dev), jnp.int32),
            pltpu.VMEM((1, bl_dev), jnp.int32),
            pltpu.VMEM((1, average_exponent.shape[0]), jnp.int32),
            pltpu.VMEM(owner_plan.shape, jnp.int32),
            pltpu.SMEM(owner_plan.shape, jnp.int32),
            pltpu.SemaphoreType.DMA((11,)),
        ],
        compiler_params=pltpu.CompilerParams(vmem_limit_bytes=32 << 20),
        name="prepare",
    )(
        *[
            pltpu.with_memory_space_constraint(array, pltpu.HBM)
            for array in (
                baseline_uvw_rows,
                frequencies.reshape(1, -1),
                source_offset,
                source_flux,
                source_group.reshape(1, -1),
                direction_gain,
                station_first.reshape(1, -1),
                station_second.reshape(1, -1),
                average_exponent.reshape(1, -1),
                owner_plan,
                owner_plan,
            )
        ]
    )
    dma = pltpu.SemaphoreType.DMA
    pieces = pl.pallas_call(
        functools.partial(predict_kernel, groups, owners, time, min(4, tiles)),
        out_shape=shape((owners, 2, cl, slots), f32),
        in_specs=[vmem] * 6,
        out_specs=vmem,
        scratch_shapes=[
            pltpu.VMEM((min(4, tiles), sources, LANES), f32),
            pltpu.VMEM((tiles, 2 * groups, cl, LANES), f32),
            pltpu.VMEM((EARLY + 1, tiles, 2 * groups, cl, LANES), f32),
            pltpu.VMEM((owners - 1, 2, cl, slots), f32),
            pltpu.VMEM((groups, 2, cl, bl_dev), f32),
            dma((groups - 1,)),
            dma((groups - 1,)),
            dma((owners - 1,)),
            dma((owners - 1,)),
        ],
        compiler_params=pltpu.CompilerParams(
            vmem_limit_bytes=32 << 20, collective_id=0, has_side_effects=True
        ),
        name="predict",
    )(*prepared)
    return pl.pallas_call(
        place_kernel,
        out_shape=jax.ShapeDtypeStruct(observed.shape, f32),
        in_specs=[smem, vmem, vmem],
        out_specs=vmem,
        scratch_shapes=[pltpu.VMEM((2, cl, capacity + slots + LANES), f32)],
        compiler_params=pltpu.CompilerParams(vmem_limit_bytes=32 << 20),
        name="place",
    )(starts, pieces, observed)


def solution(mesh):
    placed = (
        P("dir", None, "bl"),
        P(None, "bl"),
        P(),
        P(),
        P(),
        P(),
        P("dir", None, None, None),
        P(),
        P(),
        P(),
        P(),
    )
    return jax.shard_map(
        on_device, mesh=mesh, in_specs=placed, out_specs=P("dir", None, "bl"), check_vma=False
    )
```

```python
import functools
import math

import jax
import jax.numpy as jnp
from jax import lax
from jax.experimental import pallas as pl
from jax.experimental.pallas import tpu as pltpu
from jax.sharding import PartitionSpec as P

LANES = 128
UNROLL = 32
EARLY = 4
START = 3
MESH = pl.DeviceIdType.MESH
HIGH = lax.Precision.HIGHEST
NT = (((1,), (1,)), ((), ()))
P0, P1, P2, P3 = -2.2636507847492298, 1.3870216243251186, 4.937789609959605, 0.5033641130059734
K0, K1, K2 = 0.9997897140197886, -10.245898871410082, 1.823099221649536


def iota(shape, axis):
    return lax.broadcasted_iota(jnp.int32, shape, axis)


def flip(a, b, size):
    bits = range(int(math.log2(size)))
    return sum(((a // 2**i + b // 2**i) % 2) * 2**i for i in bits)


def take(values, index):
    return jnp.take_along_axis(values, index, axis=1, mode="promise_in_bounds")


def thirds(value):
    high = value.astype(jnp.bfloat16).astype(jnp.float32)
    rest = value - high
    mid = rest.astype(jnp.bfloat16).astype(jnp.float32)
    return high, mid, rest - mid


def prepare_kernel(
    groups,
    owners,
    time,
    *refs,
):
    inputs = refs[:11]
    (
    sky_ref,
    wide_ref,
    base_ref,
    order_ref,
    pair_ref,
    mask_ref,
    start_ref,
    table_ref,
    spread_ref,
    uvw_ref,
    freq_ref,
    offs_ref,
    flux_ref,
    group_ref,
    gain_ref,
    first_ref,
    second_ref,
    exps_ref,
    plan_ref,
    plan_smem,
    sem,
    ) = refs[11:]
    d = lax.axis_index("dir")
    p = lax.axis_index("bl")
    cl = wide_ref.shape[1]
    sources = offs_ref.shape[1]
    per_group = sources // groups
    bl_dev = first_ref.shape[1]
    own = pl.ds(pl.multiple_of(p * bl_dev, bl_dev), bl_dev)
    held = refs[20:31]
    copies = {}
    for index in (4, 2, 3, 1, 9, 10, 0, 5, 6, 7, 8):
        source = inputs[index].at[:, own] if index in (6, 7) else inputs[index]
        copies[index] = pltpu.make_async_copy(source, held[index], sem.at[index])
        copies[index].start()

    def arrive(*indices):
        for index in indices:
            copies[index].wait()

    block_len = bl_dev // owners
    slots = block_len * time
    block_tiles = slots // LANES
    per_tile = LANES // time
    log_time = int(math.log2(time))
    chunks = bl_dev // LANES

    arrive(4, 2, 3, 1)
    member_row = group_ref[...].astype(jnp.float32)
    eye = (iota((sources, sources), 0) == iota((sources, sources), 1)).astype(jnp.float32)
    member_col = lax.dot_general(eye, member_row, NT, precision=HIGH)
    earlier = iota((sources, sources), 0) < iota((sources, sources), 1)
    same = (jnp.abs(member_col - member_row) < 0.5) & earlier
    rank = jnp.sum(same.astype(jnp.float32), axis=0, keepdims=True)
    place = (member_row * per_group + rank + 0.5).astype(jnp.int32)
    pick = (iota((sources, sources), 0) == place).astype(jnp.float32)
    offs = lax.dot_general(pick, offs_ref[...], NT, precision=HIGH)
    east, north = offs[:, 0:1], offs[:, 1:2]
    depth = jnp.sqrt(1.0 - east * east - north * north) - 1.0
    depth_of = sky_ref.shape[1]
    kind = iota((sources, depth_of), 1) % 8
    spread_ref[...] = jnp.where(
        kind == 0, east, jnp.where(kind == 1, north, jnp.where(kind == 2, depth, 0.0))
    )
    high_rows = sky_ref.shape[0] // sources
    turn_channel = iota((high_rows, flux_ref.shape[0]), 1) == d * cl + iota((high_rows, flux_ref.shape[0]), 0)
    turn_freq = jnp.sum(turn_channel.astype(jnp.float32) * freq_ref[...], axis=1, keepdims=True)
    turn_freq = jnp.broadcast_to(turn_freq, (high_rows, depth_of))
    term = iota((high_rows, depth_of), 1) // 8
    pair_rows = max(1, 16 // high_rows)
    for k in range(0, sources, pair_rows):
        rows = []
        for i in range(pair_rows):
            high, mid, low = thirds(turn_freq * spread_ref[pl.ds(k + i, high_rows, stride=0), :])
            rows.append(jnp.where((term == 2) | (term == 3), mid, jnp.where(term == 5, low, high)))
        rows = jnp.concatenate(rows, axis=0).astype(jnp.bfloat16)
        sky_ref[k * high_rows : (k + pair_rows) * high_rows, :] = rows
    channel = iota((cl, flux_ref.shape[0]), 1) == d * cl + iota((cl, flux_ref.shape[0]), 0)
    channel = channel.astype(jnp.float32)
    own_flux = jnp.dot(channel, flux_ref[...], precision=HIGH)
    flux = lax.dot_general(own_flux, pick, NT, precision=HIGH)
    for k in range(sources):
        wide_ref[k] = jnp.broadcast_to(flux[:, k : k + 1], (cl, LANES))
    for g in range(groups):
        part = jnp.sum(flux[:, g * per_group : (g + 1) * per_group], axis=1, keepdims=True)
        base_ref[g] = jnp.broadcast_to(part, (cl, LANES))

    arrive(9, 10, 0)
    for k in range(owners):
        rows = uvw_ref[:, k * slots : (k + 1) * slots]
        rows = jnp.concatenate([rows, jnp.zeros((8 - rows.shape[0], slots), jnp.float32)], axis=0)
        high, mid, low = thirds(rows)
        rows = jnp.concatenate([high, mid, high, mid, low, high], axis=0)
        order_ref[plan_smem[p, k]] = rows.astype(jnp.bfloat16)
    plan = plan_ref[...].astype(jnp.float32)
    own_plan = jnp.sum(
        jnp.where(iota((owners, owners), 0) == p, plan, 0.0), axis=0, keepdims=True
    )
    held_by = jnp.abs(own_plan - iota((owners, owners), 0).astype(jnp.float32)) < 0.5
    block_of = jnp.sum(
        jnp.where(held_by, iota((owners, owners), 1).astype(jnp.float32), 0.0), axis=1, keepdims=True
    )

    arrive(5, 6, 7, 8)
    lane = iota((owners, LANES), 1)
    row = iota((owners, LANES), 0)
    station_total = gain_ref.shape[3]
    for g in range(groups):
        for z in range(2):
            table_ref[g, z] = gain_ref[0, g * cl : (g + 1) * cl, z, :]
    for chunk in range(chunks):
        lanes = pl.ds(chunk * LANES, LANES)
        where_from = jnp.where((chunk * LANES + lane) // block_len == row, block_of, 0.0)
        where_from = (jnp.sum(where_from, axis=0, keepdims=True) + 0.5).astype(jnp.int32)
        source = where_from * block_len + (chunk * LANES + iota((1, LANES), 1)) % block_len
        source = jnp.broadcast_to(source, (cl, LANES))
        looked = []
        for which in range(2):
            ids = jnp.zeros((cl, LANES), jnp.int32)
            for part in range(chunks):
                table = (first_ref, second_ref)[which][:, part * LANES : (part + 1) * LANES]
                table = jnp.broadcast_to(table, (cl, LANES))
                ids = jnp.where((source >> 7) == part, take(table, source & (LANES - 1)), ids)
            low, high = ids & (LANES - 1), ids >> 7
            rows = []
            for g in range(groups):
                for z in range(2):
                    total = jnp.zeros((cl, LANES), jnp.float32)
                    for part in range(station_total // LANES):
                        table = table_ref[g, z, :, pl.ds(part * LANES, LANES)]
                        total = jnp.where(high == part, take(table, low), total)
                    rows.append(total)
            looked.append(rows)
        first, second = looked
        for g in range(groups):
            ar, ai, br, bi = first[2 * g], first[2 * g + 1], second[2 * g], second[2 * g + 1]
            pair_ref[g, 0, :, lanes] = ar * br + ai * bi
            pair_ref[g, 1, :, lanes] = ai * br - ar * bi

    exps_all = jnp.concatenate(
        [exps_ref[:, i * bl_dev : (i + 1) * bl_dev] for i in range(owners)], axis=0
    )
    rows_all = jnp.right_shift(jnp.full(exps_all.shape, time, jnp.int32), exps_all)
    rows_all = rows_all.astype(jnp.float32)
    to_owner = jnp.zeros((owners, 1), jnp.float32)
    for k in range(owners):
        count = jnp.sum(rows_all[:, k * block_len : (k + 1) * block_len], axis=1, keepdims=True)
        to_owner = to_owner + jnp.where(plan_ref[:, k : k + 1] == p, count, 0.0)
    starts = jnp.sum(jnp.where(row < lane, to_owner, 0.0), axis=0, keepdims=True)
    start_ref[...] = (starts + 0.5).astype(jnp.int32)

    exps = []
    for t in range(block_tiles):
        source = (block_of + 0.5).astype(jnp.int32) * block_len + t * per_tile + lane // time
        found = jnp.zeros((owners, LANES), jnp.int32)
        for part in range(chunks):
            begin = pl.multiple_of(p * bl_dev + part * LANES, LANES)
            table = exps_ref[:, pl.ds(begin, LANES)]
            table = jnp.broadcast_to(table, (owners, LANES))
            if owners > 8:
                got = jnp.concatenate(
                    [take(table[i : i + 8], source[i : i + 8] & (LANES - 1)) for i in range(0, owners, 8)]
                )
            else:
                got = take(table, source & (LANES - 1))
            found = jnp.where((source >> 7) == part, got, found)
        exps.append(found)
    exps = jnp.concatenate(exps, axis=1)

    def put(index, values):
        for t in range(block_tiles):
            mask_ref[index, t] = values[:, t * LANES : (t + 1) * LANES]

    position = iota((owners, slots), 1)
    width = jnp.left_shift(jnp.ones_like(exps), exps)
    valid = ((position & (width - 1)) == 0).astype(jnp.int32)
    prefix = valid
    shift = 1
    while shift < slots:
        prefix = prefix + jnp.where(position >= shift, pltpu.roll(prefix, shift, 1), 0)
        shift *= 2
    count = jnp.max(prefix, axis=1, keepdims=True)
    move = position - (prefix - valid)
    scale = jnp.ones((owners, slots), jnp.float32)
    for s in range(log_time):
        scale = jnp.where(exps > s, scale * 0.5, scale)
        put(s, (exps > s).astype(jnp.float32))
    bits = int(math.log2(slots))
    held = jnp.where(valid == 1, move, 0)
    for b in range(bits):
        here = (held >> b) & 1
        moved = pltpu.roll(held, slots - (1 << b), 1)
        come = (moved >> b) & 1
        put(log_time + b, come.astype(jnp.float32))
        held = jnp.where(come == 1, moved, jnp.where(here == 1, 0, held))
    put(log_time + bits, (position < count).astype(jnp.float32))
    put(log_time + bits + 1, scale)


def predict_kernel(
    groups,
    owners,
    time,
    tiles,
    sky_ref,
    wide_ref,
    base_ref,
    order_ref,
    pair_ref,
    mask_ref,
    piece_ref,
    turns_ref,
    kept_ref,
    send_ref,
    gather_ref,
    gain_send,
    gain_recv,
    piece_send,
    piece_recv,
):
    d = lax.axis_index("dir")
    p = lax.axis_index("bl")
    sources, cl, _ = wide_ref.shape
    per_group = sources // groups
    slots = order_ref.shape[2]
    block_len = slots // time
    block_tiles = slots // LANES
    per_tile = LANES // time
    log_time = int(math.log2(time))
    bits = int(math.log2(slots))

    barrier = pltpu.get_barrier_semaphore()
    for axis, me, size in (("dir", d, groups), ("bl", p, owners)):
        for step in range(1, size):
            pl.semaphore_signal(
                barrier, inc=1, device_id={axis: lax.rem(me + step, size)}, device_id_type=MESH
            )

    def owner_of(turn):
        return flip(p, owners - 1 - turn, owners)

    def gain_copy(step):
        other = lax.rem(d + step, groups)
        return pltpu.make_async_remote_copy(
            src_ref=pair_ref.at[other],
            dst_ref=gather_ref.at[d],
            send_sem=gain_send.at[step - 1],
            recv_sem=gain_recv.at[step - 1],
            device_id={"dir": other},
            device_id_type=MESH,
        )

    def piece_copy(step):
        return pltpu.make_async_remote_copy(
            src_ref=send_ref.at[step],
            dst_ref=piece_ref.at[p],
            send_sem=piece_send.at[step],
            recv_sem=piece_recv.at[step],
            device_id={"bl": owner_of(step)},
            device_id_type=MESH,
        )

    gather_ref[d] = pair_ref[d]
    flux_sum = [base_ref[g] for g in range(groups)]
    lane = iota((cl, LANES), 1)
    steps = block_tiles // tiles

    def fill(turn, step, g):
        ln = pl.ds(pl.multiple_of(step * tiles * LANES, LANES), tiles * LANES)
        rows = per_group * turns_ref.shape[2]
        turns = jnp.dot(
            sky_ref[g * rows : (g + 1) * rows, :],
            order_ref[owner_of(turn), :, ln],
            preferred_element_type=jnp.float32,
        )
        turns_ref[g] = turns.reshape(turns_ref.shape[1:])

    def add_sources(turn, step, sent=()):
        for g in range(groups):
            if g + 1 < groups:
                fill(turn, step, g + 1)
            else:
                fill(lax.rem(turn + (step + 1) // steps, owners), lax.rem(step + 1, steps), 0)

            def source(i, acc):
                acc = list(acc)
                index = g * per_group + i
                amount = wide_ref[index]
                for t in range(tiles):
                    turns = turns_ref[g, i, 0:cl, t * LANES : (t + 1) * LANES]
                    x = turns - jnp.round(turns)
                    z = x * x
                    m = (z + P0) * z
                    s = x * (m + P1)
                    weighted = amount * s
                    acc[2 * t] = acc[2 * t] + weighted * s
                    acc[2 * t + 1] = acc[2 * t + 1] + weighted * ((m + P2) * (m + P3))
                return tuple(acc)

            acc = tuple(jnp.zeros((cl, LANES), jnp.float32) for _ in range(2 * tiles))
            acc = lax.fori_loop(0, per_group, source, acc, unroll=UNROLL)
            for t in range(tiles):
                kept_ref[turn, step * tiles + t, 2 * g] = K0 * flux_sum[g] + K1 * acc[2 * t]
                kept_ref[turn, step * tiles + t, 2 * g + 1] = -K2 * acc[2 * t + 1]
            if g == groups // 2 - 1:
                for done in sent:
                    piece_copy(done).start()

    def finish(turn):
        owner = owner_of(turn)
        model = ([], [])
        for t in range(block_tiles):
            first_bl = owner * block_len + t * per_tile
            chunk = pl.multiple_of((first_bl // LANES) * LANES, LANES)
            index = first_bl % LANES + lane // time
            model_r = jnp.zeros((cl, LANES), jnp.float32)
            model_i = jnp.zeros((cl, LANES), jnp.float32)
            for g in range(groups):
                gr = take(gather_ref[g, 0, :, pl.ds(chunk, LANES)], index)
                gi = take(gather_ref[g, 1, :, pl.ds(chunk, LANES)], index)
                real, imag = kept_ref[turn, t, 2 * g], kept_ref[turn, t, 2 * g + 1]
                model_r = model_r + (real * gr - imag * gi)
                model_i = model_i + (real * gi + imag * gr)
            model[0].append(model_r)
            model[1].append(model_i)

        def wide(index):
            return jnp.concatenate(
                [mask_ref[index, t, pl.ds(owner, cl, stride=0), :] for t in range(block_tiles)], axis=1
            )

        scale = wide(log_time + bits + 1)
        both = [jnp.concatenate(model[z], axis=1) * scale for z in range(2)]
        for s in range(log_time):
            mask = wide(s)
            both = [x + mask * pltpu.roll(x, slots - (1 << s), 1) for x in both]
        for b in range(bits):
            mask = wide(log_time + b) > 0.5
            both = [jnp.where(mask, pltpu.roll(x, slots - (1 << b), 1), x) for x in both]
        mask = wide(log_time + bits) > 0.5
        return [jnp.where(mask, x, 0.0) for x in both]

    def send(turn, done):
        for z in range(2):
            send_ref[turn, z] = done[z]

    def early(index, carry):
        @pl.when(index == START)
        def _():
            pl.semaphore_wait(barrier, groups - 1 + owners - 1)
            for step in range(1, groups):
                gain_copy(step).start()

        add_sources(index // steps, lax.rem(index, steps))
        return carry

    fill(0, 0, 0)
    lax.fori_loop(0, EARLY * steps, early, 0)
    for step in range(1, groups):
        gain_copy(step).wait()

    def catch_up(index, carry):
        for step in range(steps):
            first = 2 * index + (step if steps > 1 else 0)
            now = [first] if 0 < steps - 1 else [first, first + 1]
            now = now if step < 2 else []
            for done in now:
                send(done, finish(done))
            add_sources(EARLY + index, step, now)
        return carry

    lax.fori_loop(0, EARLY - 1, catch_up, 0)

    def block_body(turn, carry):
        send(turn - 1, finish(turn - 1))
        add_sources(turn, 0, [turn - 1])
        for step in range(1, steps):
            add_sources(turn, step)
        return carry

    lax.fori_loop(2 * EARLY - 1, owners, block_body, 0)
    done = finish(owners - 1)
    for z in range(2):
        piece_ref[p, z] = done[z]
    for step in range(owners - 1):
        piece_copy(step).wait()


def place_kernel(start_ref, piece_ref, observed_ref, out_ref, total_ref):
    owners, _, cl, slots = piece_ref.shape
    capacity = observed_ref.shape[2]
    total_ref[...] = jnp.zeros_like(total_ref)
    position = iota((cl, LANES), 1)
    for index in range(owners):
        start = start_ref[0, index]
        low = start & (LANES - 1)
        base = pl.multiple_of(start - low, LANES)
        for z in range(2):
            spun = [
                pltpu.roll(piece_ref[index, z, :, pl.ds(t * LANES, LANES)], low, 1)
                for t in range(slots // LANES)
            ]
            for t in range(slots // LANES + 1):
                lanes = pl.ds(pl.multiple_of(base + t * LANES, LANES), LANES)
                if t == 0:
                    value = jnp.where(position >= low, spun[t], total_ref[z, :, lanes])
                elif t < slots // LANES:
                    value = jnp.where(position >= low, spun[t], spun[t - 1])
                else:
                    value = jnp.where(position >= low, 0.0, spun[t - 1])
                total_ref[z, :, lanes] = value
    for z in range(2):
        out_ref[:, z, :] = observed_ref[:, z, :] - total_ref[z, :, pl.ds(0, capacity)]


def on_device(
    observed,
    baseline_uvw_rows,
    frequencies,
    source_offset,
    source_flux,
    source_group,
    direction_gain,
    station_first,
    station_second,
    average_exponent,
    owner_plan,
):
    owners = lax.axis_size("bl")
    groups = lax.axis_size("dir")
    cl, _, capacity = observed.shape
    bl_dev = station_first.shape[0] // owners
    rows = baseline_uvw_rows.shape[1]
    time = rows // bl_dev
    slots = rows // owners
    tiles = slots // LANES
    sources = source_group.shape[0]
    vmem = pl.BlockSpec(memory_space=pltpu.VMEM)
    smem = pl.BlockSpec(memory_space=pltpu.SMEM)
    masks = int(math.log2(time)) + int(math.log2(slots)) + 2
    rows_per = max(8, cl)
    f32 = jnp.float32
    shape = jax.ShapeDtypeStruct
    *prepared, starts = pl.pallas_call(
        functools.partial(prepare_kernel, groups, owners, time),
        out_shape=(
            shape((sources * rows_per, 48), jnp.bfloat16),
            shape((sources, cl, LANES), f32),
            shape((groups, cl, LANES), f32),
            shape((owners, 48, slots), jnp.bfloat16),
            shape((groups, 2, cl, bl_dev), f32),
            shape((masks, tiles, owners, LANES), f32),
            shape((1, LANES), jnp.int32),
        ),
        in_specs=[pl.BlockSpec(memory_space=pltpu.HBM)] * 11,
        out_specs=(vmem,) * 7,
        scratch_shapes=[
            pltpu.VMEM((groups, 2, cl, direction_gain.shape[3]), f32),
            pltpu.VMEM((sources, 48), f32),
            pltpu.VMEM(baseline_uvw_rows.shape, f32),
            pltpu.VMEM((1, frequencies.shape[0]), f32),
            pltpu.VMEM(source_offset.shape, f32),
            pltpu.VMEM(source_flux.shape, f32),
            pltpu.VMEM((1, sources), jnp.int32),
            pltpu.VMEM(direction_gain.shape, f32),
            pltpu.VMEM((1, bl_dev), jnp.int32),
            pltpu.VMEM((1, bl_dev), jnp.int32),
            pltpu.VMEM((1, average_exponent.shape[0]), jnp.int32),
            pltpu.VMEM(owner_plan.shape, jnp.int32),
            pltpu.SMEM(owner_plan.shape, jnp.int32),
            pltpu.SemaphoreType.DMA((11,)),
        ],
        compiler_params=pltpu.CompilerParams(vmem_limit_bytes=32 << 20),
        name="prepare",
    )(
        *[
            pltpu.with_memory_space_constraint(array, pltpu.HBM)
            for array in (
                baseline_uvw_rows,
                frequencies.reshape(1, -1),
                source_offset,
                source_flux,
                source_group.reshape(1, -1),
                direction_gain,
                station_first.reshape(1, -1),
                station_second.reshape(1, -1),
                average_exponent.reshape(1, -1),
                owner_plan,
                owner_plan,
            )
        ]
    )
    dma = pltpu.SemaphoreType.DMA
    pieces = pl.pallas_call(
        functools.partial(predict_kernel, groups, owners, time, min(4, tiles)),
        out_shape=shape((owners, 2, cl, slots), f32),
        in_specs=[vmem] * 6,
        out_specs=vmem,
        scratch_shapes=[
            pltpu.VMEM((groups, sources // groups, rows_per, min(4, tiles) * LANES), f32),
            pltpu.VMEM((owners, tiles, 2 * groups, cl, LANES), f32),
            pltpu.VMEM((owners - 1, 2, cl, slots), f32),
            pltpu.VMEM((groups, 2, cl, bl_dev), f32),
            dma((groups - 1,)),
            dma((groups - 1,)),
            dma((owners - 1,)),
            dma((owners - 1,)),
        ],
        compiler_params=pltpu.CompilerParams(
            vmem_limit_bytes=32 << 20, collective_id=0, has_side_effects=True
        ),
        name="predict",
    )(*prepared)
    return pl.pallas_call(
        place_kernel,
        out_shape=jax.ShapeDtypeStruct(observed.shape, f32),
        in_specs=[smem, vmem, vmem],
        out_specs=vmem,
        scratch_shapes=[pltpu.VMEM((2, cl, capacity + slots + LANES), f32)],
        compiler_params=pltpu.CompilerParams(vmem_limit_bytes=32 << 20),
        name="place",
    )(starts, pieces, observed)


def solution(mesh):
    placed = (
        P("dir", None, "bl"),
        P(None, "bl"),
        P(),
        P(),
        P(),
        P(),
        P("dir", None, None, None),
        P(),
        P(),
        P(),
        P(),
    )
    return jax.shard_map(
        on_device, mesh=mesh, in_specs=placed, out_specs=P("dir", None, "bl"), check_vma=False
    )
```

```python
import functools
import math

import jax
import jax.numpy as jnp
from jax import lax
from jax.experimental import pallas as pl
from jax.experimental.pallas import tpu as pltpu
from jax.sharding import PartitionSpec as P

LANES = 128
CHUNK = 8
PACE = 4
EARLY = 4
START = 3
MESH = pl.DeviceIdType.MESH
HIGH = lax.Precision.HIGHEST
NT = (((1,), (1,)), ((), ()))
P0, P1, P2, P3 = -2.2636507847492298, 1.3870216243251186, 4.937789609959605, 0.5033641130059734
K0, K1, K2 = 0.9997897140197886, -10.245898871410082, 1.823099221649536


def iota(shape, axis):
    return lax.broadcasted_iota(jnp.int32, shape, axis)


def flip(a, b, size):
    total = 0
    for i in range(int(math.log2(size))):
        total = total + lax.rem(lax.div(a, 2**i) + lax.div(b, 2**i), 2) * 2**i
    return total


def take(values, index):
    return jnp.take_along_axis(values, index, axis=1, mode="promise_in_bounds")


def thirds(value):
    high = value.astype(jnp.bfloat16).astype(jnp.float32)
    rest = value - high
    mid = rest.astype(jnp.bfloat16).astype(jnp.float32)
    return high, mid, rest - mid


def prepare_kernel(
    groups,
    owners,
    time,
    *refs,
):
    inputs = refs[:11]
    (
    sky_ref,
    wide_ref,
    base_ref,
    order_ref,
    pair_ref,
    mask_ref,
    start_ref,
    table_ref,
    spread_ref,
    uvw_ref,
    freq_ref,
    offs_ref,
    flux_ref,
    group_ref,
    gain_ref,
    first_ref,
    second_ref,
    exps_ref,
    plan_ref,
    plan_smem,
    sem,
    ) = refs[11:]
    d = lax.axis_index("dir")
    p = lax.axis_index("bl")
    cl = wide_ref.shape[1]
    sources = offs_ref.shape[1]
    per_group = sources // groups
    bl_dev = first_ref.shape[1]
    own = pl.ds(pl.multiple_of(p * bl_dev, bl_dev), bl_dev)
    held = refs[20:31]
    copies = {}
    for index in (4, 2, 3, 1, 9, 10, 0, 5, 6, 7, 8):
        source = inputs[index].at[:, own] if index in (6, 7) else inputs[index]
        copies[index] = pltpu.make_async_copy(source, held[index], sem.at[index])
        copies[index].start()

    def arrive(*indices):
        for index in indices:
            copies[index].wait()

    block_len = bl_dev // owners
    slots = block_len * time
    block_tiles = slots // LANES
    per_tile = LANES // time
    log_time = int(math.log2(time))
    chunks = bl_dev // LANES

    arrive(4, 2, 3, 1)
    member_row = group_ref[...].astype(jnp.float32)
    eye = (iota((sources, sources), 0) == iota((sources, sources), 1)).astype(jnp.float32)
    member_col = lax.dot_general(eye, member_row, NT, precision=HIGH)
    earlier = iota((sources, sources), 0) < iota((sources, sources), 1)
    same = (jnp.abs(member_col - member_row) < 0.5) & earlier
    rank = jnp.sum(same.astype(jnp.float32), axis=0, keepdims=True)
    place = (member_row * per_group + rank + 0.5).astype(jnp.int32)
    pick = (iota((sources, sources), 0) == place).astype(jnp.float32)
    offs = lax.dot_general(pick, offs_ref[...], NT, precision=HIGH)
    east, north = offs[:, 0:1], offs[:, 1:2]
    depth = jnp.sqrt(1.0 - east * east - north * north) - 1.0
    depth_of = sky_ref.shape[1]
    kind = iota((sources, depth_of), 1) % 8
    spread_ref[...] = jnp.where(
        kind == 0, east, jnp.where(kind == 1, north, jnp.where(kind == 2, depth, 0.0))
    )
    high_rows = sky_ref.shape[0] // sources
    turn_channel = iota((high_rows, flux_ref.shape[0]), 1) == d * cl + iota((high_rows, flux_ref.shape[0]), 0)
    turn_freq = jnp.sum(turn_channel.astype(jnp.float32) * freq_ref[...], axis=1, keepdims=True)
    turn_freq = jnp.broadcast_to(turn_freq, (high_rows, depth_of))
    term = iota((high_rows, depth_of), 1) // 8
    pair_rows = max(1, 16 // high_rows)
    for k in range(0, sources, pair_rows):
        rows = []
        for i in range(pair_rows):
            high, mid, low = thirds(turn_freq * spread_ref[pl.ds(k + i, high_rows, stride=0), :])
            rows.append(jnp.where((term == 2) | (term == 3), mid, jnp.where(term == 5, low, high)))
        rows = jnp.concatenate(rows, axis=0).astype(jnp.bfloat16)
        sky_ref[k * high_rows : (k + pair_rows) * high_rows, :] = rows
    channel = iota((cl, flux_ref.shape[0]), 1) == d * cl + iota((cl, flux_ref.shape[0]), 0)
    channel = channel.astype(jnp.float32)
    own_flux = jnp.dot(channel, flux_ref[...], precision=HIGH)
    flux = lax.dot_general(own_flux, pick, NT, precision=HIGH)
    for k in range(sources):
        wide_ref[k] = jnp.broadcast_to(flux[:, k : k + 1], (cl, LANES))
    for g in range(groups):
        part = jnp.sum(flux[:, g * per_group : (g + 1) * per_group], axis=1, keepdims=True)
        base_ref[g] = jnp.broadcast_to(part, (cl, LANES))

    arrive(9, 10, 0)
    for k in range(owners):
        rows = uvw_ref[:, k * slots : (k + 1) * slots]
        rows = jnp.concatenate([rows, jnp.zeros((8 - rows.shape[0], slots), jnp.float32)], axis=0)
        high, mid, low = thirds(rows)
        rows = jnp.concatenate([high, mid, high, mid, low, high], axis=0)
        order_ref[plan_smem[p, k]] = rows.astype(jnp.bfloat16)
    plan = plan_ref[...].astype(jnp.float32)
    own_plan = jnp.sum(
        jnp.where(iota((owners, owners), 0) == p, plan, 0.0), axis=0, keepdims=True
    )
    held_by = jnp.abs(own_plan - iota((owners, owners), 0).astype(jnp.float32)) < 0.5
    block_of = jnp.sum(
        jnp.where(held_by, iota((owners, owners), 1).astype(jnp.float32), 0.0), axis=1, keepdims=True
    )

    arrive(5, 6, 7, 8)
    lane = iota((owners, LANES), 1)
    row = iota((owners, LANES), 0)
    station_total = gain_ref.shape[3]
    for g in range(groups):
        for z in range(2):
            table_ref[g, z] = gain_ref[0, g * cl : (g + 1) * cl, z, :]
    for chunk in range(chunks):
        lanes = pl.ds(chunk * LANES, LANES)
        where_from = jnp.where((chunk * LANES + lane) // block_len == row, block_of, 0.0)
        where_from = (jnp.sum(where_from, axis=0, keepdims=True) + 0.5).astype(jnp.int32)
        source = where_from * block_len + (chunk * LANES + iota((1, LANES), 1)) % block_len
        source = jnp.broadcast_to(source, (cl, LANES))
        looked = []
        for which in range(2):
            ids = jnp.zeros((cl, LANES), jnp.int32)
            for part in range(chunks):
                table = (first_ref, second_ref)[which][:, part * LANES : (part + 1) * LANES]
                table = jnp.broadcast_to(table, (cl, LANES))
                ids = jnp.where((source >> 7) == part, take(table, source & (LANES - 1)), ids)
            low, high = ids & (LANES - 1), ids >> 7
            rows = []
            for g in range(groups):
                for z in range(2):
                    total = jnp.zeros((cl, LANES), jnp.float32)
                    for part in range(station_total // LANES):
                        table = table_ref[g, z, :, pl.ds(part * LANES, LANES)]
                        total = jnp.where(high == part, take(table, low), total)
                    rows.append(total)
            looked.append(rows)
        first, second = looked
        for g in range(groups):
            ar, ai, br, bi = first[2 * g], first[2 * g + 1], second[2 * g], second[2 * g + 1]
            pair_ref[g, 0, :, lanes] = ar * br + ai * bi
            pair_ref[g, 1, :, lanes] = ai * br - ar * bi

    exps_all = jnp.concatenate(
        [exps_ref[:, i * bl_dev : (i + 1) * bl_dev] for i in range(owners)], axis=0
    )
    rows_all = jnp.right_shift(jnp.full(exps_all.shape, time, jnp.int32), exps_all)
    rows_all = rows_all.astype(jnp.float32)
    to_owner = jnp.zeros((owners, 1), jnp.float32)
    for k in range(owners):
        count = jnp.sum(rows_all[:, k * block_len : (k + 1) * block_len], axis=1, keepdims=True)
        to_owner = to_owner + jnp.where(plan_ref[:, k : k + 1] == p, count, 0.0)
    starts = jnp.sum(jnp.where(row < lane, to_owner, 0.0), axis=0, keepdims=True)
    start_ref[...] = (starts + 0.5).astype(jnp.int32)

    exps = []
    for t in range(block_tiles):
        source = (block_of + 0.5).astype(jnp.int32) * block_len + t * per_tile + lane // time
        found = jnp.zeros((owners, LANES), jnp.int32)
        for part in range(chunks):
            begin = pl.multiple_of(p * bl_dev + part * LANES, LANES)
            table = exps_ref[:, pl.ds(begin, LANES)]
            table = jnp.broadcast_to(table, (owners, LANES))
            if owners > 8:
                got = jnp.concatenate(
                    [take(table[i : i + 8], source[i : i + 8] & (LANES - 1)) for i in range(0, owners, 8)]
                )
            else:
                got = take(table, source & (LANES - 1))
            found = jnp.where((source >> 7) == part, got, found)
        exps.append(found)
    exps = jnp.concatenate(exps, axis=1)

    def put(index, values):
        for t in range(block_tiles):
            mask_ref[index, t] = values[:, t * LANES : (t + 1) * LANES]

    position = iota((owners, slots), 1)
    width = jnp.left_shift(jnp.ones_like(exps), exps)
    valid = ((position & (width - 1)) == 0).astype(jnp.int32)
    prefix = valid
    shift = 1
    while shift < slots:
        prefix = prefix + jnp.where(position >= shift, pltpu.roll(prefix, shift, 1), 0)
        shift *= 2
    count = jnp.max(prefix, axis=1, keepdims=True)
    move = position - (prefix - valid)
    scale = jnp.ones((owners, slots), jnp.float32)
    for s in range(log_time):
        scale = jnp.where(exps > s, scale * 0.5, scale)
        put(s, (exps > s).astype(jnp.float32))
    bits = int(math.log2(slots))
    held = jnp.where(valid == 1, move, 0)
    for b in range(bits):
        here = (held >> b) & 1
        moved = pltpu.roll(held, slots - (1 << b), 1)
        come = (moved >> b) & 1
        put(log_time + b, come.astype(jnp.float32))
        held = jnp.where(come == 1, moved, jnp.where(here == 1, 0, held))
    put(log_time + bits, (position < count).astype(jnp.float32))
    put(log_time + bits + 1, scale)


def predict_kernel(
    groups,
    owners,
    time,
    tiles,
    sky_ref,
    wide_ref,
    base_ref,
    order_ref,
    pair_ref,
    mask_ref,
    piece_ref,
    kept_ref,
    send_ref,
    gather_ref,
    gain_send,
    gain_recv,
    piece_send,
    piece_recv,
    *more_refs,
):
    states, turns_refs = more_refs[:2], more_refs[2:]
    d = lax.axis_index("dir")
    p = lax.axis_index("bl")
    sources, cl, _ = wide_ref.shape
    per_group = sources // groups
    slots = order_ref.shape[2]
    block_len = slots // time
    block_tiles = slots // LANES
    per_tile = LANES // time
    log_time = int(math.log2(time))
    bits = int(math.log2(slots))

    barrier = pltpu.get_barrier_semaphore()
    for axis, me, size in (("dir", d, groups), ("bl", p, owners)):
        for step in range(1, size):
            pl.semaphore_signal(
                barrier, inc=1, device_id={axis: lax.rem(me + step, size)}, device_id_type=MESH
            )

    def owner_of(turn):
        return flip(p, owners - 1 - turn, owners)

    def gain_copy(step):
        other = lax.rem(d + step, groups)
        return pltpu.make_async_remote_copy(
            src_ref=pair_ref.at[other],
            dst_ref=gather_ref.at[d],
            send_sem=gain_send.at[step - 1],
            recv_sem=gain_recv.at[step - 1],
            device_id={"dir": other},
            device_id_type=MESH,
        )

    def piece_copy(step):
        return pltpu.make_async_remote_copy(
            src_ref=send_ref.at[step],
            dst_ref=piece_ref.at[p],
            send_sem=piece_send.at[step],
            recv_sem=piece_recv.at[step],
            device_id={"bl": owner_of(step)},
            device_id_type=MESH,
        )

    gather_ref[d] = pair_ref[d]
    flux_sum = [base_ref[g] for g in range(groups)]
    lane = iota((cl, LANES), 1)
    steps = block_tiles // tiles

    def fill(turn, step, g):
        ln = pl.ds(pl.multiple_of(step * tiles * LANES, LANES), tiles * LANES)
        turns_ref = turns_refs[g]
        rows = per_group * turns_ref.shape[1]
        turns = jnp.dot(
            sky_ref[g * rows : (g + 1) * rows, :],
            order_ref[owner_of(turn), :, ln],
            preferred_element_type=jnp.float32,
        )
        turns_ref[...] = turns.reshape(turns_ref.shape)

    def add_sources(turn, step, work=(), pace=3):
        for g in range(groups):
            if g + 1 < groups:
                fill(turn, step, g + 1)
            else:
                ahead = step + 1
                fill(lax.rem(turn + lax.div(ahead, steps), owners), lax.rem(ahead, steps), 0)

            def source(i, acc):
                acc = list(acc)
                amount = wide_ref[g * per_group + i]
                for t in range(tiles):
                    turns = turns_refs[g][i, 0:cl, t * LANES : (t + 1) * LANES]
                    x = turns - jnp.round(turns)
                    z = x * x
                    m = (z + P0) * z
                    s = x * (m + P1)
                    weighted = amount * s
                    acc[2 * t] = acc[2 * t] + weighted * s
                    acc[2 * t + 1] = acc[2 * t + 1] + weighted * ((m + P2) * (m + P3))
                return tuple(acc)

            acc = tuple(jnp.zeros((cl, LANES), jnp.float32) for _ in range(2 * tiles))
            for begin in range(0, per_group, CHUNK):
                acc = lax.fori_loop(begin, begin + CHUNK, source, acc, unroll=CHUNK)
                for stage in list(work) * pace:
                    next(stage, None)
            for t in range(tiles):
                kept_ref[turn, step * tiles + t, 2 * g] = K0 * flux_sum[g] + K1 * acc[2 * t]
                kept_ref[turn, step * tiles + t, 2 * g + 1] = -K2 * acc[2 * t + 1]
        for stage in work:
            for _ in stage:
                pass

    def finish(turn, out_ref, where):
        owner = owner_of(turn)
        chunk = pl.multiple_of(lax.div(owner * block_len, LANES) * LANES, LANES)
        first_bl = lax.rem(owner * block_len, LANES) + (lane >> log_time)

        def wide(index, t):
            return mask_ref[index, t, pl.ds(owner, cl, stride=0), :]

        for t in range(block_tiles):
            index = first_bl + t * per_tile
            model_r = jnp.zeros((cl, LANES), jnp.float32)
            model_i = jnp.zeros((cl, LANES), jnp.float32)
            for g in range(groups):
                gr = take(gather_ref[g, 0, :, pl.ds(chunk, LANES)], index)
                gi = take(gather_ref[g, 1, :, pl.ds(chunk, LANES)], index)
                real, imag = kept_ref[turn, t, 2 * g], kept_ref[turn, t, 2 * g + 1]
                model_r = model_r + (real * gr - imag * gi)
                model_i = model_i + (real * gi + imag * gr)
            scale = wide(log_time + bits + 1, t)
            states[0][0, t] = model_r * scale
            states[0][1, t] = model_i * scale
            yield

        stages = log_time + bits
        for stage in range(stages):
            size = 1 << (stage if stage < log_time else stage - log_time)
            jump, size = size // LANES, size % LANES
            for z in range(2):
                old, new = states[stage % 2], states[1 - stage % 2]
                spun = [old[z, t] for t in range(block_tiles)]
                if size:
                    spun = [pltpu.roll(x, LANES - size, 1) for x in spun]
                for t in range(block_tiles):
                    near = spun[(t + jump) % block_tiles]
                    if size:
                        near = jnp.where(lane < LANES - size, near, spun[(t + 1) % block_tiles])
                    if stage < log_time:
                        value = old[z, t] + wide(stage, t) * near
                    else:
                        value = jnp.where(wide(stage, t) > 0.5, near, old[z, t])
                    if stage == stages - 1:
                        value = jnp.where(wide(stages, t) > 0.5, value, 0.0)
                        out_ref[where, z, :, t * LANES : (t + 1) * LANES] = value
                    else:
                        new[z, t] = value
                yield

    def send(turn):
        yield from finish(turn, send_ref, turn)
        yield
        piece_copy(turn).start()

    def early(index, carry):
        @pl.when(index == START)
        def _():
            pl.semaphore_wait(barrier, groups - 1 + owners - 1)
            for step in range(1, groups):
                gain_copy(step).start()

        add_sources(lax.div(index, steps), lax.rem(index, steps))
        return carry

    fill(0, 0, 0)
    lax.fori_loop(0, EARLY * steps, early, 0)
    for step in range(1, groups):
        gain_copy(step).wait()

    def catch_up(index, carry):
        for step in range(steps):
            first = 2 * index + (step if steps > 1 else 0)
            now = [first] if 0 < steps - 1 else [first, first + 1]
            now = now if step < 2 else []
            add_sources(EARLY + index, step, [send(done) for done in now])
        return carry

    lax.fori_loop(0, EARLY - 1, catch_up, 0)

    def block_body(turn, carry):
        add_sources(turn, 0, [send(turn - 1)], PACE)
        for step in range(1, steps):
            add_sources(turn, step)
        return carry

    lax.fori_loop(2 * EARLY - 1, owners, block_body, 0)

    for _ in finish(owners - 1, piece_ref, p):
        pass
    for step in range(owners - 1):
        piece_copy(step).wait()


def place_kernel(start_ref, piece_ref, observed_ref, out_ref, total_ref):
    owners, _, cl, slots = piece_ref.shape
    capacity = observed_ref.shape[2]
    total_ref[...] = jnp.zeros_like(total_ref)
    position = iota((cl, LANES), 1)
    for index in range(owners):
        start = start_ref[0, index]
        low = start & (LANES - 1)
        base = pl.multiple_of(start - low, LANES)
        for z in range(2):
            spun = [
                pltpu.roll(piece_ref[index, z, :, pl.ds(t * LANES, LANES)], low, 1)
                for t in range(slots // LANES)
            ]
            for t in range(slots // LANES + 1):
                lanes = pl.ds(pl.multiple_of(base + t * LANES, LANES), LANES)
                if t == 0:
                    value = jnp.where(position >= low, spun[t], total_ref[z, :, lanes])
                elif t < slots // LANES:
                    value = jnp.where(position >= low, spun[t], spun[t - 1])
                else:
                    value = jnp.where(position >= low, 0.0, spun[t - 1])
                total_ref[z, :, lanes] = value
    for z in range(2):
        out_ref[:, z, :] = observed_ref[:, z, :] - total_ref[z, :, pl.ds(0, capacity)]


def on_device(
    observed,
    baseline_uvw_rows,
    frequencies,
    source_offset,
    source_flux,
    source_group,
    direction_gain,
    station_first,
    station_second,
    average_exponent,
    owner_plan,
):
    owners = lax.axis_size("bl")
    groups = lax.axis_size("dir")
    cl, _, capacity = observed.shape
    bl_dev = station_first.shape[0] // owners
    rows = baseline_uvw_rows.shape[1]
    time = rows // bl_dev
    slots = rows // owners
    tiles = slots // LANES
    sources = source_group.shape[0]
    vmem = pl.BlockSpec(memory_space=pltpu.VMEM)
    smem = pl.BlockSpec(memory_space=pltpu.SMEM)
    masks = int(math.log2(time)) + int(math.log2(slots)) + 2
    rows_per = max(8, cl)
    f32 = jnp.float32
    shape = jax.ShapeDtypeStruct
    *prepared, starts = pl.pallas_call(
        functools.partial(prepare_kernel, groups, owners, time),
        out_shape=(
            shape((sources * rows_per, 48), jnp.bfloat16),
            shape((sources, cl, LANES), f32),
            shape((groups, cl, LANES), f32),
            shape((owners, 48, slots), jnp.bfloat16),
            shape((groups, 2, cl, bl_dev), f32),
            shape((masks, tiles, owners, LANES), f32),
            shape((1, LANES), jnp.int32),
        ),
        in_specs=[pl.BlockSpec(memory_space=pltpu.HBM)] * 11,
        out_specs=(vmem,) * 7,
        scratch_shapes=[
            pltpu.VMEM((groups, 2, cl, direction_gain.shape[3]), f32),
            pltpu.VMEM((sources, 48), f32),
            pltpu.VMEM(baseline_uvw_rows.shape, f32),
            pltpu.VMEM((1, frequencies.shape[0]), f32),
            pltpu.VMEM(source_offset.shape, f32),
            pltpu.VMEM(source_flux.shape, f32),
            pltpu.VMEM((1, sources), jnp.int32),
            pltpu.VMEM(direction_gain.shape, f32),
            pltpu.VMEM((1, bl_dev), jnp.int32),
            pltpu.VMEM((1, bl_dev), jnp.int32),
            pltpu.VMEM((1, average_exponent.shape[0]), jnp.int32),
            pltpu.VMEM(owner_plan.shape, jnp.int32),
            pltpu.SMEM(owner_plan.shape, jnp.int32),
            pltpu.SemaphoreType.DMA((11,)),
        ],
        compiler_params=pltpu.CompilerParams(vmem_limit_bytes=32 << 20),
        name="prepare",
    )(
        *[
            pltpu.with_memory_space_constraint(array, pltpu.HBM)
            for array in (
                baseline_uvw_rows,
                frequencies.reshape(1, -1),
                source_offset,
                source_flux,
                source_group.reshape(1, -1),
                direction_gain,
                station_first.reshape(1, -1),
                station_second.reshape(1, -1),
                average_exponent.reshape(1, -1),
                owner_plan,
                owner_plan,
            )
        ]
    )
    dma = pltpu.SemaphoreType.DMA
    pieces = pl.pallas_call(
        functools.partial(predict_kernel, groups, owners, time, min(4, tiles)),
        out_shape=shape((owners, 2, cl, slots), f32),
        in_specs=[vmem] * 6,
        out_specs=vmem,
        scratch_shapes=[
            pltpu.VMEM((owners, tiles, 2 * groups, cl, LANES), f32),
            pltpu.VMEM((owners - 1, 2, cl, slots), f32),
            pltpu.VMEM((groups, 2, cl, bl_dev), f32),
            dma((groups - 1,)),
            dma((groups - 1,)),
            dma((owners - 1,)),
            dma((owners - 1,)),
        ]
        + [pltpu.VMEM((2, tiles, cl, LANES), f32)] * 2
        + [pltpu.VMEM((sources // groups, rows_per, min(4, tiles) * LANES), f32)] * groups,
        compiler_params=pltpu.CompilerParams(
            vmem_limit_bytes=32 << 20, collective_id=0, has_side_effects=True
        ),
        name="predict",
    )(*prepared)
    return pl.pallas_call(
        place_kernel,
        out_shape=jax.ShapeDtypeStruct(observed.shape, f32),
        in_specs=[smem, vmem, vmem],
        out_specs=vmem,
        scratch_shapes=[pltpu.VMEM((2, cl, capacity + slots + LANES), f32)],
        compiler_params=pltpu.CompilerParams(vmem_limit_bytes=32 << 20),
        name="place",
    )(starts, pieces, observed)


def solution(mesh):
    placed = (
        P("dir", None, "bl"),
        P(None, "bl"),
        P(),
        P(),
        P(),
        P(),
        P("dir", None, None, None),
        P(),
        P(),
        P(),
        P(),
    )
    return jax.shard_map(
        on_device, mesh=mesh, in_specs=placed, out_specs=P("dir", None, "bl"), check_vma=False
    )
```

```python
import functools
import math

import jax
import jax.numpy as jnp
from jax import lax
from jax.experimental import pallas as pl
from jax.experimental.pallas import tpu as pltpu
from jax.sharding import PartitionSpec as P

LANES = 128
CHUNK = 8
PACE = 4
EARLY = 4
START = 3
FIRST = 2
BATCH = 16
MESH = pl.DeviceIdType.MESH
HIGH = lax.Precision.HIGHEST
NT = (((1,), (1,)), ((), ()))
P0, P1, P2, P3 = -2.2636507847492298, 1.3870216243251186, 4.937789609959605, 0.5033641130059734
K0, K1, K2 = 0.9997897140197886, -10.245898871410082, 1.823099221649536


def iota(shape, axis):
    return lax.broadcasted_iota(jnp.int32, shape, axis)


def flip(a, b, size):
    total = 0
    for i in range(int(math.log2(size))):
        total = total + lax.rem(lax.div(a, 2**i) + lax.div(b, 2**i), 2) * 2**i
    return total


def take(values, index):
    return jnp.take_along_axis(values, index, axis=1, mode="promise_in_bounds")


def thirds(value):
    high = value.astype(jnp.bfloat16).astype(jnp.float32)
    rest = value - high
    mid = rest.astype(jnp.bfloat16).astype(jnp.float32)
    return high, mid, rest - mid


def prepare_kernel(
    groups,
    owners,
    time,
    *refs,
):
    inputs = refs[:11]
    (
    sky_ref,
    wide_ref,
    base_ref,
    order_ref,
    table_ref,
    ids_ref,
    start_ref,
    spread_ref,
    uvw_ref,
    freq_ref,
    offs_ref,
    flux_ref,
    group_ref,
    gain_ref,
    first_ref,
    second_ref,
    exps_ref,
    plan_ref,
    plan_smem,
    sem,
    ) = refs[11:]
    d = lax.axis_index("dir")
    p = lax.axis_index("bl")
    cl = wide_ref.shape[1]
    sources = offs_ref.shape[1]
    per_group = sources // groups
    bl_dev = first_ref.shape[1]
    own = pl.ds(pl.multiple_of(p * bl_dev, bl_dev), bl_dev)
    held = refs[19:30]
    copies = {}
    for index in (4, 2, 3, 1, 9, 10, 0, 5, 6, 7, 8):
        source = inputs[index].at[:, own] if index in (6, 7) else inputs[index]
        copies[index] = pltpu.make_async_copy(source, held[index], sem.at[index])
        copies[index].start()

    def arrive(*indices):
        for index in indices:
            copies[index].wait()

    block_len = bl_dev // owners
    slots = block_len * time
    block_tiles = slots // LANES
    per_tile = LANES // time
    log_time = int(math.log2(time))
    chunks = bl_dev // LANES

    arrive(4, 2, 3, 1)
    member_row = group_ref[...].astype(jnp.float32)
    earlier = iota((sources, sources), 0) < iota((sources, sources), 1)
    equal = iota((sources, sources), 0) == iota((sources, sources), 1)
    member_col = jnp.sum(jnp.where(equal, member_row, 0.0), axis=1, keepdims=True)
    same = (jnp.abs(member_col - member_row) < 0.5) & earlier
    rank = jnp.sum(same.astype(jnp.float32), axis=0, keepdims=True)
    place = (member_row * per_group + rank + 0.5).astype(jnp.int32)
    pick = (iota((sources, sources), 0) == place).astype(jnp.float32).astype(jnp.bfloat16)

    def padded(rows):
        fill = jnp.zeros((8 - rows.shape[0], sources), jnp.float32)
        rows = jnp.concatenate([rows, fill], axis=0) if rows.shape[0] < 8 else rows
        return jnp.concatenate(thirds(rows), axis=0).astype(jnp.bfloat16)

    own_flux = jnp.zeros((cl, sources), jnp.float32)
    for i in range(groups):
        own_flux = own_flux + jnp.where(d == i, flux_ref[i * cl : (i + 1) * cl, :], 0.0)
    flux = lax.dot_general(padded(own_flux), pick, NT, preferred_element_type=jnp.float32)
    size = flux.shape[0] // 3
    flux = (flux[0:size] + flux[size : 2 * size] + flux[2 * size : 3 * size])[0:cl]
    offs = lax.dot_general(pick, padded(offs_ref[...]), NT, preferred_element_type=jnp.float32)
    east, north = [offs[:, i : i + 1] + offs[:, 8 + i : 9 + i] + offs[:, 16 + i : 17 + i] for i in range(2)]
    depth = jnp.sqrt(1.0 - east * east - north * north) - 1.0
    arrive(9, 10, 0, 5, 6, 7, 8)
    half = sources // 2
    kind = iota((sources, LANES), 1) % 8
    used = iota((sources, LANES), 1) % (LANES // 2) < 48
    spread = jnp.where(kind == 0, east, jnp.where(kind == 1, north, jnp.where(kind == 2, depth, 0.0)))
    spread = jnp.where(used, spread, 0.0)
    spread_ref[...] = jnp.where(iota((half, LANES), 1) < LANES // 2, spread[:half], spread[half:])
    high_rows = sky_ref.shape[0] // half
    turn_channel = iota((high_rows, flux_ref.shape[0]), 1) == d * cl + iota((high_rows, flux_ref.shape[0]), 0)
    turn_freq = jnp.sum(turn_channel.astype(jnp.float32) * freq_ref[...], axis=1, keepdims=True)
    turn_freq = jnp.broadcast_to(turn_freq, (high_rows, LANES))
    term = iota((high_rows, LANES), 1) % (LANES // 2) // 8
    mids, lows = (term == 2) | (term == 3), term == 5
    pair_rows = max(1, 16 // high_rows)
    share = [part.astype(jnp.float32) for part in thirds(own_flux)[:2]]
    if cl < 8:
        share = [jnp.concatenate([part, jnp.zeros((8 - cl, sources), jnp.float32)], axis=0) for part in share]
    order_row = jnp.broadcast_to(place, share[0].shape)
    ones = jnp.ones((2 * sources, LANES), jnp.float32).astype(jnp.bfloat16)
    for k in range(0, half, pair_rows):
        rows = []
        for i in range(pair_rows):
            high, mid, low = thirds(turn_freq * spread_ref[pl.ds(k + i, high_rows, stride=0), :])
            rows.append(jnp.where(mids, mid, jnp.where(lows, low, high)))
        rows = jnp.concatenate(rows, axis=0).astype(jnp.bfloat16)
        sky_ref[k * high_rows : (k + pair_rows) * high_rows, :] = rows
        if k % BATCH == 0:
            left = []
            for i in range(2 * k, 2 * k + 2 * BATCH):
                here = order_row == i
                left.append(jnp.concatenate([jnp.where(here, part, 0.0) for part in share], axis=1))
            left = jnp.concatenate(left, axis=0).astype(jnp.bfloat16)
            amounts = jnp.dot(left, ones, preferred_element_type=jnp.float32)
            amounts = amounts.reshape(2 * BATCH, share[0].shape[0], LANES)[:, 0:cl]
            wide_ref[2 * k : 2 * k + 2 * BATCH] = amounts
    for g in range(groups):
        part = jnp.sum(flux[:, g * per_group : (g + 1) * per_group], axis=1, keepdims=True)
        base_ref[g] = jnp.broadcast_to(part, (cl, LANES))

    for k in range(owners):
        rows = uvw_ref[:, k * slots : (k + 1) * slots]
        rows = jnp.concatenate([rows, jnp.zeros((8 - rows.shape[0], slots), jnp.float32)], axis=0)
        high, mid, low = thirds(rows)
        rows = jnp.concatenate([high, mid, high, mid, low, high], axis=0)
        order_ref[plan_smem[p, k]] = rows.astype(jnp.bfloat16)
    plan = plan_ref[...].astype(jnp.float32)
    own_plan = jnp.sum(
        jnp.where(iota((owners, owners), 0) == p, plan, 0.0), axis=0, keepdims=True
    )
    held_by = jnp.abs(own_plan - iota((owners, owners), 0).astype(jnp.float32)) < 0.5
    block_of = jnp.sum(
        jnp.where(held_by, iota((owners, owners), 1).astype(jnp.float32), 0.0), axis=1, keepdims=True
    )

    lane = iota((owners, LANES), 1)
    row = iota((owners, LANES), 0)
    for g in range(groups):
        for z in range(2):
            table_ref[g, z] = gain_ref[0, g * cl : (g + 1) * cl, z, :]
    for chunk in range(chunks):
        lanes = pl.ds(chunk * LANES, LANES)
        where_from = jnp.where((chunk * LANES + lane) // block_len == row, block_of, 0.0)
        where_from = (jnp.sum(where_from, axis=0, keepdims=True) + 0.5).astype(jnp.int32)
        source = where_from * block_len + (chunk * LANES + iota((1, LANES), 1)) % block_len
        source = jnp.broadcast_to(source, (cl, LANES))
        for which in range(3):
            ids = jnp.zeros((cl, LANES), jnp.int32)
            for part in range(chunks):
                begin = part * LANES
                if which == 2:
                    begin = pl.multiple_of(p * bl_dev + begin, LANES)
                table = (first_ref, second_ref, exps_ref)[which][:, pl.ds(begin, LANES)]
                table = jnp.broadcast_to(table, (cl, LANES))
                ids = jnp.where((source >> 7) == part, take(table, source & (LANES - 1)), ids)
            ids_ref[which : which + 1, lanes] = ids[0:1]

    exps_all = jnp.concatenate(
        [exps_ref[:, i * bl_dev : (i + 1) * bl_dev] for i in range(owners)], axis=0
    )
    rows_all = jnp.right_shift(jnp.full(exps_all.shape, time, jnp.int32), exps_all)
    rows_all = rows_all.astype(jnp.float32)
    to_owner = jnp.zeros((owners, 1), jnp.float32)
    for k in range(owners):
        count = jnp.sum(rows_all[:, k * block_len : (k + 1) * block_len], axis=1, keepdims=True)
        to_owner = to_owner + jnp.where(plan_ref[:, k : k + 1] == p, count, 0.0)
    starts = jnp.sum(jnp.where(row < lane, to_owner, 0.0), axis=0, keepdims=True)
    start_ref[...] = (starts + 0.5).astype(jnp.int32)


def predict_kernel(
    groups,
    owners,
    time,
    tiles,
    sky_ref,
    wide_ref,
    base_ref,
    order_ref,
    table_ref,
    ids_ref,
    piece_ref,
    pair_ref,
    mask_ref,
    kept_ref,
    send_ref,
    gather_ref,
    gain_send,
    gain_recv,
    piece_send,
    piece_recv,
    *more_refs,
):
    states, turns_refs = more_refs[:2], more_refs[2:]
    d = lax.axis_index("dir")
    p = lax.axis_index("bl")
    sources, cl, _ = wide_ref.shape
    per_group = sources // groups
    slots = order_ref.shape[2]
    block_len = slots // time
    block_tiles = slots // LANES
    per_tile = LANES // time
    log_time = int(math.log2(time))
    bits = int(math.log2(slots))

    barrier = pltpu.get_barrier_semaphore()
    for axis, me, size in (("dir", d, groups), ("bl", p, owners)):
        for step in range(1, size):
            pl.semaphore_signal(
                barrier, inc=1, device_id={axis: lax.rem(me + step, size)}, device_id_type=MESH
            )

    def owner_of(turn):
        return flip(p, owners - 1 - turn, owners)

    def gain_copy(step):
        other = lax.rem(d + step, groups)
        return pltpu.make_async_remote_copy(
            src_ref=pair_ref.at[other],
            dst_ref=gather_ref.at[d],
            send_sem=gain_send.at[step - 1],
            recv_sem=gain_recv.at[step - 1],
            device_id={"dir": other},
            device_id_type=MESH,
        )

    def piece_copy(step):
        return pltpu.make_async_remote_copy(
            src_ref=send_ref.at[step],
            dst_ref=piece_ref.at[p],
            send_sem=piece_send.at[step],
            recv_sem=piece_recv.at[step],
            device_id={"bl": owner_of(step)},
            device_id_type=MESH,
        )

    flux_sum = [base_ref[g] for g in range(groups)]
    lane = iota((cl, LANES), 1)
    steps = block_tiles // tiles

    def fill(turn, step, g):
        ln = pl.ds(pl.multiple_of(step * tiles * LANES, LANES), tiles * LANES)
        turns_ref = turns_refs[g]
        rows = per_group * turns_ref.shape[1]
        near = g % (groups // 2)
        right = order_ref[owner_of(turn), :, ln]
        fill_rows = LANES // 2 if g >= groups // 2 else LANES - right.shape[0]
        blank = jnp.zeros((fill_rows, tiles * LANES), jnp.bfloat16)
        if g >= groups // 2:
            rest = jnp.zeros((LANES // 2 - right.shape[0], tiles * LANES), jnp.bfloat16)
            right = jnp.concatenate([blank, right, rest], axis=0)
        else:
            right = jnp.concatenate([right, blank], axis=0)
        turns = jnp.dot(
            sky_ref[near * rows : (near + 1) * rows, :], right, preferred_element_type=jnp.float32
        )
        turns_ref[...] = turns.reshape(turns_ref.shape)

    def add_sources(turn, step, work=(), pace=3, drain=True):
        for g in range(groups):
            if g + 1 < groups:
                fill(turn, step, g + 1)
            else:
                ahead = step + 1
                fill(lax.rem(turn + lax.div(ahead, steps), owners), lax.rem(ahead, steps), 0)

            def source(i, acc):
                acc = list(acc)
                amount = wide_ref[g * per_group + i]
                for t in range(tiles):
                    turns = turns_refs[g][i, 0:cl, t * LANES : (t + 1) * LANES]
                    x = turns - jnp.round(turns)
                    z = x * x
                    m = (z + P0) * z
                    s = x * (m + P1)
                    weighted = amount * s
                    acc[2 * t] = acc[2 * t] + weighted * s
                    acc[2 * t + 1] = acc[2 * t + 1] + weighted * ((m + P2) * (m + P3))
                return tuple(acc)

            acc = tuple(jnp.zeros((cl, LANES), jnp.float32) for _ in range(2 * tiles))
            for begin in range(0, per_group, CHUNK):
                acc = lax.fori_loop(begin, begin + CHUNK, source, acc, unroll=CHUNK)
                for stage in list(work) * pace:
                    next(stage, None)
            for t in range(tiles):
                kept_ref[turn, step * tiles + t, 2 * g] = K0 * flux_sum[g] + K1 * acc[2 * t]
                kept_ref[turn, step * tiles + t, 2 * g + 1] = -K2 * acc[2 * t + 1]
        for stage in work if drain else ():
            for _ in stage:
                pass

    def finish(turn, out_ref, where):
        owner = owner_of(turn)
        chunk = pl.multiple_of(lax.div(owner * block_len, LANES) * LANES, LANES)
        first_bl = lax.rem(owner * block_len, LANES) + (lane >> log_time)

        def wide(index, t):
            return mask_ref[index, t, pl.ds(owner, cl, stride=0), :]

        for t in range(block_tiles):
            index = first_bl + t * per_tile
            model_r = jnp.zeros((cl, LANES), jnp.float32)
            model_i = jnp.zeros((cl, LANES), jnp.float32)
            for g in range(groups):
                gr = take(gather_ref[g, 0, :, pl.ds(chunk, LANES)], index)
                gi = take(gather_ref[g, 1, :, pl.ds(chunk, LANES)], index)
                real, imag = kept_ref[turn, t, 2 * g], kept_ref[turn, t, 2 * g + 1]
                model_r = model_r + (real * gr - imag * gi)
                model_i = model_i + (real * gi + imag * gr)
            scale = wide(log_time + bits + 1, t)
            states[0][0, t] = model_r * scale
            states[0][1, t] = model_i * scale
            yield

        stages = log_time + bits
        for stage in range(stages):
            size = 1 << (stage if stage < log_time else stage - log_time)
            jump, size = size // LANES, size % LANES
            for z in range(2):
                old, new = states[stage % 2], states[1 - stage % 2]
                spun = [old[z, t] for t in range(block_tiles)]
                if size:
                    spun = [pltpu.roll(x, LANES - size, 1) for x in spun]
                for t in range(block_tiles):
                    near = spun[(t + jump) % block_tiles]
                    if size:
                        near = jnp.where(lane < LANES - size, near, spun[(t + 1) % block_tiles])
                    if stage < log_time:
                        value = old[z, t] + wide(stage, t) * near
                    else:
                        value = jnp.where(wide(stage, t) > 0.5, near, old[z, t])
                    if stage == stages - 1:
                        value = jnp.where(wide(stages, t) > 0.5, value, 0.0)
                        out_ref[where, z, :, t * LANES : (t + 1) * LANES] = value
                    else:
                        new[z, t] = value
                yield

    def send(turn):
        yield from finish(turn, send_ref, turn)
        yield
        piece_copy(turn).start()

    def tables():
        station_total = table_ref.shape[3]
        chunks = ids_ref.shape[1] // LANES
        for chunk in range(chunks):
            lanes = pl.ds(chunk * LANES, LANES)
            looked = []
            for which in range(2):
                ids = jnp.broadcast_to(ids_ref[which : which + 1, lanes], (cl, LANES))
                low, high = ids & (LANES - 1), ids >> 7
                rows = []
                for g in range(groups):
                    for z in range(2):
                        total = jnp.zeros((cl, LANES), jnp.float32)
                        for part in range(station_total // LANES):
                            table = table_ref[g, z, :, pl.ds(part * LANES, LANES)]
                            total = jnp.where(high == part, take(table, low), total)
                        rows.append(total)
                looked.append(rows)
                yield
            first, second = looked
            for g in range(groups):
                ar, ai, br, bi = first[2 * g], first[2 * g + 1], second[2 * g], second[2 * g + 1]
                pair_ref[g, 0, :, lanes] = ar * br + ai * bi
                pair_ref[g, 1, :, lanes] = ai * br - ar * bi
        gather_ref[d] = pair_ref[d]

        exps = []
        wide_lane = iota((owners, LANES), 1)
        for t in range(block_tiles):
            source = iota((owners, LANES), 0) * block_len + t * per_tile + (wide_lane >> log_time)
            found = jnp.zeros((owners, LANES), jnp.int32)
            for part in range(chunks):
                table = ids_ref[2:3, part * LANES : (part + 1) * LANES]
                table = jnp.broadcast_to(table, (owners, LANES))
                got = [take(table[i : i + 8], source[i : i + 8] & (LANES - 1)) for i in range(0, owners, 8)]
                got = jnp.concatenate(got) if owners > 8 else got[0]
                found = jnp.where((source >> 7) == part, got, found)
            exps.append(found)
            if t % 2 == 1:
                yield
        exps = jnp.concatenate(exps, axis=1)

        def put(index, values):
            for t in range(block_tiles):
                mask_ref[index, t] = values[:, t * LANES : (t + 1) * LANES]

        position = iota((owners, slots), 1)
        width = jnp.left_shift(jnp.ones_like(exps), exps)
        valid = ((position & (width - 1)) == 0).astype(jnp.int32)
        scale = jnp.ones((owners, slots), jnp.float32)
        for s in range(log_time):
            scale = jnp.where(exps > s, scale * 0.5, scale)
            put(s, (exps > s).astype(jnp.float32))
        put(log_time + bits + 1, scale)
        yield
        prefix = valid
        for b in range(bits):
            prefix = prefix + jnp.where(position >= 1 << b, pltpu.roll(prefix, 1 << b, 1), 0)
            if b % 2 == 1:
                yield
        count = jnp.max(prefix, axis=1, keepdims=True)
        put(log_time + bits, (position < count).astype(jnp.float32))
        held = jnp.where(valid == 1, position - (prefix - valid), 0)
        for b in range(bits):
            here = (held >> b) & 1
            moved = pltpu.roll(held, slots - (1 << b), 1)
            come = (moved >> b) & 1
            put(log_time + b, come.astype(jnp.float32))
            held = jnp.where(come == 1, moved, jnp.where(here == 1, 0, held))
            yield

    def early(index, carry):
        @pl.when(index == START)
        def _():
            pl.semaphore_wait(barrier, groups - 1 + owners - 1)
            for step in range(1, groups):
                gain_copy(step).start()

        add_sources(lax.div(index, steps), lax.rem(index, steps))
        return carry

    fill(0, 0, 0)
    work = [tables()]
    for index in range(FIRST):
        add_sources(index // steps, index % steps, work, 1, index == FIRST - 1)
    lax.fori_loop(FIRST, EARLY * steps, early, 0)
    for step in range(1, groups):
        gain_copy(step).wait()

    def catch_up(index, carry):
        for step in range(steps):
            first = 2 * index + (step if steps > 1 else 0)
            now = [first] if 0 < steps - 1 else [first, first + 1]
            now = now if step < 2 else []
            add_sources(EARLY + index, step, [send(done) for done in now])
        return carry

    lax.fori_loop(0, EARLY - 1, catch_up, 0)

    def block_body(turn, carry):
        add_sources(turn, 0, [send(turn - 1)], PACE)
        for step in range(1, steps):
            add_sources(turn, step)
        return carry

    lax.fori_loop(2 * EARLY - 1, owners, block_body, 0)

    for _ in finish(owners - 1, piece_ref, p):
        pass
    for step in range(owners - 1):
        piece_copy(step).wait()


def place_kernel(start_ref, piece_ref, observed_ref, out_ref, total_ref):
    owners, _, cl, slots = piece_ref.shape
    capacity = observed_ref.shape[2]
    total_ref[...] = jnp.zeros_like(total_ref)
    position = iota((cl, LANES), 1)
    for index in range(owners):
        start = start_ref[0, index]
        low = start & (LANES - 1)
        base = pl.multiple_of(start - low, LANES)
        for z in range(2):
            spun = [
                pltpu.roll(piece_ref[index, z, :, pl.ds(t * LANES, LANES)], low, 1)
                for t in range(slots // LANES)
            ]
            for t in range(slots // LANES + 1):
                lanes = pl.ds(pl.multiple_of(base + t * LANES, LANES), LANES)
                if t == 0:
                    value = jnp.where(position >= low, spun[t], total_ref[z, :, lanes])
                elif t < slots // LANES:
                    value = jnp.where(position >= low, spun[t], spun[t - 1])
                else:
                    value = jnp.where(position >= low, 0.0, spun[t - 1])
                total_ref[z, :, lanes] = value
    for z in range(2):
        out_ref[:, z, :] = observed_ref[:, z, :] - total_ref[z, :, pl.ds(0, capacity)]


def on_device(
    observed,
    baseline_uvw_rows,
    frequencies,
    source_offset,
    source_flux,
    source_group,
    direction_gain,
    station_first,
    station_second,
    average_exponent,
    owner_plan,
):
    owners = lax.axis_size("bl")
    groups = lax.axis_size("dir")
    cl, _, capacity = observed.shape
    bl_dev = station_first.shape[0] // owners
    rows = baseline_uvw_rows.shape[1]
    time = rows // bl_dev
    slots = rows // owners
    tiles = slots // LANES
    sources = source_group.shape[0]
    vmem = pl.BlockSpec(memory_space=pltpu.VMEM)
    smem = pl.BlockSpec(memory_space=pltpu.SMEM)
    masks = int(math.log2(time)) + int(math.log2(slots)) + 2
    rows_per = max(8, cl)
    f32 = jnp.float32
    shape = jax.ShapeDtypeStruct
    *prepared, starts = pl.pallas_call(
        functools.partial(prepare_kernel, groups, owners, time),
        out_shape=(
            shape((sources // 2 * rows_per, LANES), jnp.bfloat16),
            shape((sources, cl, LANES), f32),
            shape((groups, cl, LANES), f32),
            shape((owners, 48, slots), jnp.bfloat16),
            shape((groups, 2, cl, direction_gain.shape[3]), f32),
            shape((8, bl_dev), jnp.int32),
            shape((1, LANES), jnp.int32),
        ),
        in_specs=[pl.BlockSpec(memory_space=pltpu.HBM)] * 11,
        out_specs=(vmem,) * 7,
        scratch_shapes=[
            pltpu.VMEM((sources // 2, LANES), f32),
            pltpu.VMEM(baseline_uvw_rows.shape, f32),
            pltpu.VMEM((1, frequencies.shape[0]), f32),
            pltpu.VMEM(source_offset.shape, f32),
            pltpu.VMEM(source_flux.shape, f32),
            pltpu.VMEM((1, sources), jnp.int32),
            pltpu.VMEM(direction_gain.shape, f32),
            pltpu.VMEM((1, bl_dev), jnp.int32),
            pltpu.VMEM((1, bl_dev), jnp.int32),
            pltpu.VMEM((1, average_exponent.shape[0]), jnp.int32),
            pltpu.VMEM(owner_plan.shape, jnp.int32),
            pltpu.SMEM(owner_plan.shape, jnp.int32),
            pltpu.SemaphoreType.DMA((11,)),
        ],
        compiler_params=pltpu.CompilerParams(vmem_limit_bytes=32 << 20),
        name="prepare",
    )(
        *[
            pltpu.with_memory_space_constraint(array, pltpu.HBM)
            for array in (
                baseline_uvw_rows,
                frequencies.reshape(1, -1),
                source_offset,
                source_flux,
                source_group.reshape(1, -1),
                direction_gain,
                station_first.reshape(1, -1),
                station_second.reshape(1, -1),
                average_exponent.reshape(1, -1),
                owner_plan,
                owner_plan,
            )
        ]
    )
    dma = pltpu.SemaphoreType.DMA
    pieces = pl.pallas_call(
        functools.partial(predict_kernel, groups, owners, time, min(4, tiles)),
        out_shape=shape((owners, 2, cl, slots), f32),
        in_specs=[vmem] * 6,
        out_specs=vmem,
        scratch_shapes=[
            pltpu.VMEM((groups, 2, cl, bl_dev), f32),
            pltpu.VMEM((masks, tiles, owners, LANES), f32),
            pltpu.VMEM((owners, tiles, 2 * groups, cl, LANES), f32),
            pltpu.VMEM((owners - 1, 2, cl, slots), f32),
            pltpu.VMEM((groups, 2, cl, bl_dev), f32),
            dma((groups - 1,)),
            dma((groups - 1,)),
            dma((owners - 1,)),
            dma((owners - 1,)),
        ]
        + [pltpu.VMEM((2, tiles, cl, LANES), f32)] * 2
        + [pltpu.VMEM((sources // groups, rows_per, min(4, tiles) * LANES), f32)] * groups,
        compiler_params=pltpu.CompilerParams(
            vmem_limit_bytes=32 << 20, collective_id=0, has_side_effects=True
        ),
        name="predict",
    )(*prepared)
    return pl.pallas_call(
        place_kernel,
        out_shape=jax.ShapeDtypeStruct(observed.shape, f32),
        in_specs=[smem, vmem, vmem],
        out_specs=vmem,
        scratch_shapes=[pltpu.VMEM((2, cl, capacity + slots + LANES), f32)],
        compiler_params=pltpu.CompilerParams(vmem_limit_bytes=32 << 20),
        name="place",
    )(starts, pieces, observed)


def solution(mesh):
    placed = (
        P("dir", None, "bl"),
        P(None, "bl"),
        P(),
        P(),
        P(),
        P(),
        P("dir", None, None, None),
        P(),
        P(),
        P(),
        P(),
    )
    return jax.shard_map(
        on_device, mesh=mesh, in_specs=placed, out_specs=P("dir", None, "bl"), check_vma=False
    )
```

```python
import functools
import math

import jax
import jax.numpy as jnp
from jax import lax
from jax.experimental import pallas as pl
from jax.experimental.pallas import tpu as pltpu
from jax.sharding import PartitionSpec as P

LANES = 128
CHUNK = 8
PACE = 4
EARLY = 4
START = 3
FIRST = 2
BATCH = 16
MESH = pl.DeviceIdType.MESH
HIGH = lax.Precision.HIGHEST
NT = (((1,), (1,)), ((), ()))
P0, P1, P2, P3 = -2.2636507847492298, 1.3870216243251186, 4.937789609959605, 0.5033641130059734
K0, K1, K2 = 0.9997897140197886, -10.245898871410082, 1.823099221649536


def iota(shape, axis):
    return lax.broadcasted_iota(jnp.int32, shape, axis)


def flip(a, b, size):
    total = 0
    for i in range(int(math.log2(size))):
        total = total + lax.rem(lax.div(a, 2**i) + lax.div(b, 2**i), 2) * 2**i
    return total


def take(values, index):
    return jnp.take_along_axis(values, index, axis=1, mode="promise_in_bounds")


def thirds(value):
    high = value.astype(jnp.bfloat16).astype(jnp.float32)
    rest = value - high
    mid = rest.astype(jnp.bfloat16).astype(jnp.float32)
    return high, mid, rest - mid


def prepare_kernel(
    groups,
    owners,
    time,
    *refs,
):
    inputs = refs[:11]
    (
    sky_ref,
    wide_ref,
    base_ref,
    order_ref,
    table_ref,
    ids_ref,
    start_ref,
    spread_ref,
    uvw_ref,
    freq_ref,
    offs_ref,
    flux_ref,
    group_ref,
    gain_ref,
    first_ref,
    second_ref,
    exps_ref,
    plan_ref,
    plan_smem,
    sem,
    ) = refs[11:]
    d = lax.axis_index("dir")
    p = lax.axis_index("bl")
    cl = wide_ref.shape[1]
    sources = offs_ref.shape[1]
    per_group = sources // groups
    bl_dev = first_ref.shape[1]
    own = pl.ds(pl.multiple_of(p * bl_dev, bl_dev), bl_dev)
    held = refs[19:30]
    copies = {}
    for index in (4, 2, 3, 1, 9, 10, 0, 5, 6, 7, 8):
        source = inputs[index].at[:, own] if index in (6, 7) else inputs[index]
        copies[index] = pltpu.make_async_copy(source, held[index], sem.at[index])
        copies[index].start()

    def arrive(*indices):
        for index in indices:
            copies[index].wait()

    block_len = bl_dev // owners
    slots = block_len * time
    block_tiles = slots // LANES
    per_tile = LANES // time
    log_time = int(math.log2(time))
    chunks = bl_dev // LANES

    arrive(4, 2, 3, 1)
    member_row = group_ref[...].astype(jnp.float32)
    earlier = iota((sources, sources), 0) < iota((sources, sources), 1)
    equal = iota((sources, sources), 0) == iota((sources, sources), 1)
    member_col = jnp.sum(jnp.where(equal, member_row, 0.0), axis=1, keepdims=True)
    same = (jnp.abs(member_col - member_row) < 0.5) & earlier
    rank = jnp.sum(same.astype(jnp.float32), axis=0, keepdims=True)
    place = (member_row * per_group + rank + 0.5).astype(jnp.int32)
    pick = (iota((sources, sources), 0) == place).astype(jnp.float32).astype(jnp.bfloat16)

    def padded(rows):
        fill = jnp.zeros((8 - rows.shape[0], sources), jnp.float32)
        rows = jnp.concatenate([rows, fill], axis=0) if rows.shape[0] < 8 else rows
        return jnp.concatenate(thirds(rows), axis=0).astype(jnp.bfloat16)

    own_flux = jnp.zeros((cl, sources), jnp.float32)
    for i in range(groups):
        own_flux = own_flux + jnp.where(d == i, flux_ref[i * cl : (i + 1) * cl, :], 0.0)
    flux = lax.dot_general(padded(own_flux), pick, NT, preferred_element_type=jnp.float32)
    size = flux.shape[0] // 3
    flux = (flux[0:size] + flux[size : 2 * size] + flux[2 * size : 3 * size])[0:cl]
    offs = lax.dot_general(pick, padded(offs_ref[...]), NT, preferred_element_type=jnp.float32)
    east, north = [offs[:, i : i + 1] + offs[:, 8 + i : 9 + i] + offs[:, 16 + i : 17 + i] for i in range(2)]
    depth = jnp.sqrt(1.0 - east * east - north * north) - 1.0
    arrive(9, 10, 0, 5, 6, 7, 8)
    half = sources // 2
    kind = iota((sources, LANES), 1) % 8
    used = iota((sources, LANES), 1) % (LANES // 2) < 48
    spread = jnp.where(kind == 0, east, jnp.where(kind == 1, north, jnp.where(kind == 2, depth, 0.0)))
    spread = jnp.where(used, spread, 0.0)
    spread_ref[...] = jnp.where(iota((half, LANES), 1) < LANES // 2, spread[:half], spread[half:])
    high_rows = sky_ref.shape[0] // half
    turn_channel = iota((high_rows, flux_ref.shape[0]), 1) == d * cl + iota((high_rows, flux_ref.shape[0]), 0)
    turn_freq = jnp.sum(turn_channel.astype(jnp.float32) * freq_ref[...], axis=1, keepdims=True)
    turn_freq = jnp.broadcast_to(turn_freq, (high_rows, LANES))
    term = iota((high_rows, LANES), 1) % (LANES // 2) // 8
    mids, lows = (term == 2) | (term == 3), term == 5
    pair_rows = max(1, 16 // high_rows)
    share = [part.astype(jnp.float32) for part in thirds(own_flux)[:2]]
    if cl < 8:
        share = [jnp.concatenate([part, jnp.zeros((8 - cl, sources), jnp.float32)], axis=0) for part in share]
    order_row = jnp.broadcast_to(place, share[0].shape)
    ones = jnp.ones((2 * sources, LANES), jnp.float32).astype(jnp.bfloat16)
    for k in range(0, half, pair_rows):
        rows = []
        for i in range(pair_rows):
            high, mid, low = thirds(turn_freq * spread_ref[pl.ds(k + i, high_rows, stride=0), :])
            rows.append(jnp.where(mids, mid, jnp.where(lows, low, high)))
        rows = jnp.concatenate(rows, axis=0).astype(jnp.bfloat16)
        sky_ref[k * high_rows : (k + pair_rows) * high_rows, :] = rows
        if k % BATCH == 0:
            left = []
            for i in range(2 * k, 2 * k + 2 * BATCH):
                here = order_row == i
                left.append(jnp.concatenate([jnp.where(here, part, 0.0) for part in share], axis=1))
            left = jnp.concatenate(left, axis=0).astype(jnp.bfloat16)
            amounts = jnp.dot(left, ones, preferred_element_type=jnp.float32)
            amounts = amounts.reshape(2 * BATCH, share[0].shape[0], LANES)[:, 0:cl]
            wide_ref[2 * k : 2 * k + 2 * BATCH] = amounts
    for g in range(groups):
        part = jnp.sum(flux[:, g * per_group : (g + 1) * per_group], axis=1, keepdims=True)
        base_ref[g] = jnp.broadcast_to(part, (cl, LANES))

    for k in range(owners):
        rows = uvw_ref[:, k * slots : (k + 1) * slots]
        rows = jnp.concatenate([rows, jnp.zeros((8 - rows.shape[0], slots), jnp.float32)], axis=0)
        high, mid, low = thirds(rows)
        rows = jnp.concatenate([high, mid, high, mid, low, high], axis=0)
        order_ref[plan_smem[p, k]] = rows.astype(jnp.bfloat16)
    plan = plan_ref[...].astype(jnp.float32)
    own_plan = jnp.sum(
        jnp.where(iota((owners, owners), 0) == p, plan, 0.0), axis=0, keepdims=True
    )
    held_by = jnp.abs(own_plan - iota((owners, owners), 0).astype(jnp.float32)) < 0.5
    block_of = jnp.sum(
        jnp.where(held_by, iota((owners, owners), 1).astype(jnp.float32), 0.0), axis=1, keepdims=True
    )

    lane = iota((owners, LANES), 1)
    row = iota((owners, LANES), 0)
    for g in range(groups):
        for z in range(2):
            table_ref[g, z] = gain_ref[0, g * cl : (g + 1) * cl, z, :]
    for chunk in range(chunks):
        lanes = pl.ds(chunk * LANES, LANES)
        where_from = jnp.where((chunk * LANES + lane) // block_len == row, block_of, 0.0)
        where_from = (jnp.sum(where_from, axis=0, keepdims=True) + 0.5).astype(jnp.int32)
        source = where_from * block_len + (chunk * LANES + iota((1, LANES), 1)) % block_len
        source = jnp.broadcast_to(source, (cl, LANES))
        for which in range(3):
            ids = jnp.zeros((cl, LANES), jnp.int32)
            for part in range(chunks):
                begin = part * LANES
                if which == 2:
                    begin = pl.multiple_of(p * bl_dev + begin, LANES)
                table = (first_ref, second_ref, exps_ref)[which][:, pl.ds(begin, LANES)]
                table = jnp.broadcast_to(table, (cl, LANES))
                ids = jnp.where((source >> 7) == part, take(table, source & (LANES - 1)), ids)
            ids_ref[which : which + 1, lanes] = ids[0:1]

    exps_all = jnp.concatenate(
        [exps_ref[:, i * bl_dev : (i + 1) * bl_dev] for i in range(owners)], axis=0
    )
    rows_all = jnp.right_shift(jnp.full(exps_all.shape, time, jnp.int32), exps_all)
    rows_all = rows_all.astype(jnp.float32)
    to_owner = jnp.zeros((owners, 1), jnp.float32)
    for k in range(owners):
        count = jnp.sum(rows_all[:, k * block_len : (k + 1) * block_len], axis=1, keepdims=True)
        to_owner = to_owner + jnp.where(plan_ref[:, k : k + 1] == p, count, 0.0)
    starts = jnp.sum(jnp.where(row < lane, to_owner, 0.0), axis=0, keepdims=True)
    start_ref[...] = (starts + 0.5).astype(jnp.int32)


def predict_kernel(
    groups,
    owners,
    time,
    tiles,
    sky_ref,
    wide_ref,
    base_ref,
    order_ref,
    table_ref,
    ids_ref,
    piece_ref,
    pair_ref,
    mask_ref,
    kept_ref,
    send_ref,
    gather_ref,
    gain_send,
    gain_recv,
    piece_send,
    piece_recv,
    *more_refs,
):
    states, turns_refs = more_refs[:2], more_refs[2:]
    d = lax.axis_index("dir")
    p = lax.axis_index("bl")
    sources, cl, _ = wide_ref.shape
    per_group = sources // groups
    slots = order_ref.shape[2]
    block_len = slots // time
    block_tiles = slots // LANES
    per_tile = LANES // time
    log_time = int(math.log2(time))
    bits = int(math.log2(slots))

    barrier = pltpu.get_barrier_semaphore()
    for axis, me, size in (("dir", d, groups), ("bl", p, owners)):
        for step in range(1, size):
            pl.semaphore_signal(
                barrier, inc=1, device_id={axis: lax.rem(me + step, size)}, device_id_type=MESH
            )

    def owner_of(turn):
        return flip(p, owners - 1 - turn, owners)

    chunks = ids_ref.shape[1] // LANES
    per_chunk = LANES // block_len

    def gain_copy(step, chunk):
        other = lax.rem(d + step, groups)
        first = flip(lax.div(p, per_chunk), chunks - 1 - chunk, chunks) * LANES
        lanes = pl.ds(pl.multiple_of(first, LANES), LANES)
        return pltpu.make_async_remote_copy(
            src_ref=pair_ref.at[other, :, :, lanes],
            dst_ref=gather_ref.at[d, :, :, lanes],
            send_sem=gain_send.at[step - 1, chunk],
            recv_sem=gain_recv.at[step - 1, chunk],
            device_id={"dir": other},
            device_id_type=MESH,
        )

    def gains_arrive(chunk):
        for step in range(1, groups):
            gain_copy(step, chunk).wait()

    def piece_copy(step):
        return pltpu.make_async_remote_copy(
            src_ref=send_ref.at[step],
            dst_ref=piece_ref.at[p],
            send_sem=piece_send.at[step],
            recv_sem=piece_recv.at[step],
            device_id={"bl": owner_of(step)},
            device_id_type=MESH,
        )

    flux_sum = [base_ref[g] for g in range(groups)]
    lane = iota((cl, LANES), 1)
    steps = block_tiles // tiles

    def fill(turn, step, g):
        ln = pl.ds(pl.multiple_of(step * tiles * LANES, LANES), tiles * LANES)
        turns_ref = turns_refs[g]
        rows = per_group * turns_ref.shape[1]
        near = g % (groups // 2)
        right = order_ref[owner_of(turn), :, ln]
        fill_rows = LANES // 2 if g >= groups // 2 else LANES - right.shape[0]
        blank = jnp.zeros((fill_rows, tiles * LANES), jnp.bfloat16)
        if g >= groups // 2:
            rest = jnp.zeros((LANES // 2 - right.shape[0], tiles * LANES), jnp.bfloat16)
            right = jnp.concatenate([blank, right, rest], axis=0)
        else:
            right = jnp.concatenate([right, blank], axis=0)
        turns = jnp.dot(
            sky_ref[near * rows : (near + 1) * rows, :], right, preferred_element_type=jnp.float32
        )
        turns_ref[...] = turns.reshape(turns_ref.shape)

    def add_sources(turn, step, work=(), pace=3, drain=True):
        for g in range(groups):
            if g + 1 < groups:
                fill(turn, step, g + 1)
            else:
                ahead = step + 1
                fill(lax.rem(turn + lax.div(ahead, steps), owners), lax.rem(ahead, steps), 0)

            def source(i, acc):
                acc = list(acc)
                amount = wide_ref[g * per_group + i]
                for t in range(tiles):
                    turns = turns_refs[g][i, 0:cl, t * LANES : (t + 1) * LANES]
                    x = turns - jnp.round(turns)
                    z = x * x
                    m = (z + P0) * z
                    s = x * (m + P1)
                    weighted = amount * s
                    acc[2 * t] = acc[2 * t] + weighted * s
                    acc[2 * t + 1] = acc[2 * t + 1] + weighted * ((m + P2) * (m + P3))
                return tuple(acc)

            acc = tuple(jnp.zeros((cl, LANES), jnp.float32) for _ in range(2 * tiles))
            for begin in range(0, per_group, CHUNK):
                acc = lax.fori_loop(begin, begin + CHUNK, source, acc, unroll=CHUNK)
                for stage in list(work) * pace:
                    next(stage, None)
            for t in range(tiles):
                kept_ref[turn, step * tiles + t, 2 * g] = K0 * flux_sum[g] + K1 * acc[2 * t]
                kept_ref[turn, step * tiles + t, 2 * g + 1] = -K2 * acc[2 * t + 1]
        for stage in work if drain else ():
            for _ in stage:
                pass

    def finish(turn, out_ref, where):
        owner = owner_of(turn)
        chunk = pl.multiple_of(lax.div(owner * block_len, LANES) * LANES, LANES)
        first_bl = lax.rem(owner * block_len, LANES) + (lane >> log_time)

        def wide(index, t):
            return mask_ref[index, t, pl.ds(owner, cl, stride=0), :]

        for t in range(block_tiles):
            index = first_bl + t * per_tile
            model_r = jnp.zeros((cl, LANES), jnp.float32)
            model_i = jnp.zeros((cl, LANES), jnp.float32)
            for g in range(groups):
                gr = take(gather_ref[g, 0, :, pl.ds(chunk, LANES)], index)
                gi = take(gather_ref[g, 1, :, pl.ds(chunk, LANES)], index)
                real, imag = kept_ref[turn, t, 2 * g], kept_ref[turn, t, 2 * g + 1]
                model_r = model_r + (real * gr - imag * gi)
                model_i = model_i + (real * gi + imag * gr)
            scale = wide(log_time + bits + 1, t)
            states[0][0, t] = model_r * scale
            states[0][1, t] = model_i * scale
            yield

        stages = log_time + bits
        for stage in range(stages):
            size = 1 << (stage if stage < log_time else stage - log_time)
            jump, size = size // LANES, size % LANES
            for z in range(2):
                old, new = states[stage % 2], states[1 - stage % 2]
                spun = [old[z, t] for t in range(block_tiles)]
                if size:
                    spun = [pltpu.roll(x, LANES - size, 1) for x in spun]
                for t in range(block_tiles):
                    near = spun[(t + jump) % block_tiles]
                    if size:
                        near = jnp.where(lane < LANES - size, near, spun[(t + 1) % block_tiles])
                    if stage < log_time:
                        value = old[z, t] + wide(stage, t) * near
                    else:
                        value = jnp.where(wide(stage, t) > 0.5, near, old[z, t])
                    if stage == stages - 1:
                        value = jnp.where(wide(stages, t) > 0.5, value, 0.0)
                        out_ref[where, z, :, t * LANES : (t + 1) * LANES] = value
                    else:
                        new[z, t] = value
                yield

    def send(turn):
        yield from finish(turn, send_ref, turn)
        yield
        piece_copy(turn).start()

    def tables():
        station_total = table_ref.shape[3]
        for chunk in range(chunks):
            lanes = pl.ds(chunk * LANES, LANES)
            looked = []
            for which in range(2):
                ids = jnp.broadcast_to(ids_ref[which : which + 1, lanes], (cl, LANES))
                low, high = ids & (LANES - 1), ids >> 7
                rows = []
                for g in range(groups):
                    for z in range(2):
                        total = jnp.zeros((cl, LANES), jnp.float32)
                        for part in range(station_total // LANES):
                            table = table_ref[g, z, :, pl.ds(part * LANES, LANES)]
                            total = jnp.where(high == part, take(table, low), total)
                        rows.append(total)
                looked.append(rows)
                yield
            first, second = looked
            for g in range(groups):
                ar, ai, br, bi = first[2 * g], first[2 * g + 1], second[2 * g], second[2 * g + 1]
                pair_ref[g, 0, :, lanes] = ar * br + ai * bi
                pair_ref[g, 1, :, lanes] = ai * br - ar * bi
        gather_ref[d] = pair_ref[d]

        exps = []
        wide_lane = iota((owners, LANES), 1)
        for t in range(block_tiles):
            source = iota((owners, LANES), 0) * block_len + t * per_tile + (wide_lane >> log_time)
            found = jnp.zeros((owners, LANES), jnp.int32)
            for part in range(chunks):
                table = ids_ref[2:3, part * LANES : (part + 1) * LANES]
                table = jnp.broadcast_to(table, (owners, LANES))
                got = [take(table[i : i + 8], source[i : i + 8] & (LANES - 1)) for i in range(0, owners, 8)]
                got = jnp.concatenate(got) if owners > 8 else got[0]
                found = jnp.where((source >> 7) == part, got, found)
            exps.append(found)
            if t % 2 == 1:
                yield
        exps = jnp.concatenate(exps, axis=1)

        def put(index, values):
            for t in range(block_tiles):
                mask_ref[index, t] = values[:, t * LANES : (t + 1) * LANES]

        position = iota((owners, slots), 1)
        width = jnp.left_shift(jnp.ones_like(exps), exps)
        valid = ((position & (width - 1)) == 0).astype(jnp.int32)
        scale = jnp.ones((owners, slots), jnp.float32)
        for s in range(log_time):
            scale = jnp.where(exps > s, scale * 0.5, scale)
            put(s, (exps > s).astype(jnp.float32))
        put(log_time + bits + 1, scale)
        yield
        prefix = valid
        for b in range(bits):
            prefix = prefix + jnp.where(position >= 1 << b, pltpu.roll(prefix, 1 << b, 1), 0)
            if b % 2 == 1:
                yield
        count = jnp.max(prefix, axis=1, keepdims=True)
        put(log_time + bits, (position < count).astype(jnp.float32))
        held = jnp.where(valid == 1, position - (prefix - valid), 0)
        for b in range(bits):
            here = (held >> b) & 1
            moved = pltpu.roll(held, slots - (1 << b), 1)
            come = (moved >> b) & 1
            put(log_time + b, come.astype(jnp.float32))
            held = jnp.where(come == 1, moved, jnp.where(here == 1, 0, held))
            yield

    def early(index, carry):
        @pl.when(index == START)
        def _():
            pl.semaphore_wait(barrier, groups - 1 + owners - 1)
            for chunk in range(chunks):
                for step in range(1, groups):
                    gain_copy(step, chunk).start()

        add_sources(lax.div(index, steps), lax.rem(index, steps))
        return carry

    fill(0, 0, 0)
    work = [tables()]
    for index in range(FIRST):
        add_sources(index // steps, index % steps, work, 1, index == FIRST - 1)
    lax.fori_loop(FIRST, EARLY * steps, early, 0)

    def catch_up(index, carry):
        @pl.when(lax.rem(2 * index, per_chunk) == 0)
        def _():
            gains_arrive(lax.div(2 * index, per_chunk))

        for step in range(steps):
            first = 2 * index + (step if steps > 1 else 0)
            now = [first] if 0 < steps - 1 else [first, first + 1]
            now = now if step < 2 else []
            add_sources(EARLY + index, step, [send(done) for done in now])
        return carry

    lax.fori_loop(0, EARLY - 1, catch_up, 0)
    for chunk in range(-(-2 * (EARLY - 1) // per_chunk), chunks):
        gains_arrive(chunk)

    def block_body(turn, carry):
        add_sources(turn, 0, [send(turn - 1)], PACE)
        for step in range(1, steps):
            add_sources(turn, step)
        return carry

    lax.fori_loop(2 * EARLY - 1, owners, block_body, 0)

    for _ in finish(owners - 1, piece_ref, p):
        pass
    for step in range(owners - 1):
        piece_copy(step).wait()


def place_kernel(start_ref, piece_ref, observed_ref, out_ref, total_ref):
    owners, _, cl, slots = piece_ref.shape
    capacity = observed_ref.shape[2]
    total_ref[...] = jnp.zeros_like(total_ref)
    position = iota((cl, LANES), 1)
    for index in range(owners):
        start = start_ref[0, index]
        low = start & (LANES - 1)
        base = pl.multiple_of(start - low, LANES)
        for z in range(2):
            spun = [
                pltpu.roll(piece_ref[index, z, :, pl.ds(t * LANES, LANES)], low, 1)
                for t in range(slots // LANES)
            ]
            for t in range(slots // LANES + 1):
                lanes = pl.ds(pl.multiple_of(base + t * LANES, LANES), LANES)
                if t == 0:
                    value = jnp.where(position >= low, spun[t], total_ref[z, :, lanes])
                elif t < slots // LANES:
                    value = jnp.where(position >= low, spun[t], spun[t - 1])
                else:
                    value = jnp.where(position >= low, 0.0, spun[t - 1])
                total_ref[z, :, lanes] = value
    for z in range(2):
        out_ref[:, z, :] = observed_ref[:, z, :] - total_ref[z, :, pl.ds(0, capacity)]


def on_device(
    observed,
    baseline_uvw_rows,
    frequencies,
    source_offset,
    source_flux,
    source_group,
    direction_gain,
    station_first,
    station_second,
    average_exponent,
    owner_plan,
):
    owners = lax.axis_size("bl")
    groups = lax.axis_size("dir")
    cl, _, capacity = observed.shape
    bl_dev = station_first.shape[0] // owners
    rows = baseline_uvw_rows.shape[1]
    time = rows // bl_dev
    slots = rows // owners
    tiles = slots // LANES
    sources = source_group.shape[0]
    vmem = pl.BlockSpec(memory_space=pltpu.VMEM)
    masks = int(math.log2(time)) + int(math.log2(slots)) + 2
    rows_per = max(8, cl)
    f32 = jnp.float32
    shape = jax.ShapeDtypeStruct
    *prepared, starts = pl.pallas_call(
        functools.partial(prepare_kernel, groups, owners, time),
        out_shape=(
            shape((sources // 2 * rows_per, LANES), jnp.bfloat16),
            shape((sources, cl, LANES), f32),
            shape((groups, cl, LANES), f32),
            shape((owners, 48, slots), jnp.bfloat16),
            shape((groups, 2, cl, direction_gain.shape[3]), f32),
            shape((8, bl_dev), jnp.int32),
            shape((1, LANES), jnp.int32),
        ),
        in_specs=[pl.BlockSpec(memory_space=pltpu.HBM)] * 11,
        out_specs=(vmem,) * 7,
        scratch_shapes=[
            pltpu.VMEM((sources // 2, LANES), f32),
            pltpu.VMEM(baseline_uvw_rows.shape, f32),
            pltpu.VMEM((1, frequencies.shape[0]), f32),
            pltpu.VMEM(source_offset.shape, f32),
            pltpu.VMEM(source_flux.shape, f32),
            pltpu.VMEM((1, sources), jnp.int32),
            pltpu.VMEM(direction_gain.shape, f32),
            pltpu.VMEM((1, bl_dev), jnp.int32),
            pltpu.VMEM((1, bl_dev), jnp.int32),
            pltpu.VMEM((1, average_exponent.shape[0]), jnp.int32),
            pltpu.VMEM(owner_plan.shape, jnp.int32),
            pltpu.SMEM(owner_plan.shape, jnp.int32),
            pltpu.SemaphoreType.DMA((11,)),
        ],
        compiler_params=pltpu.CompilerParams(vmem_limit_bytes=32 << 20),
        name="prepare",
    )(
        *[
            pltpu.with_memory_space_constraint(array, pltpu.HBM)
            for array in (
                baseline_uvw_rows,
                frequencies.reshape(1, -1),
                source_offset,
                source_flux,
                source_group.reshape(1, -1),
                direction_gain,
                station_first.reshape(1, -1),
                station_second.reshape(1, -1),
                average_exponent.reshape(1, -1),
                owner_plan,
                owner_plan,
            )
        ]
    )
    dma = pltpu.SemaphoreType.DMA
    pieces = pl.pallas_call(
        functools.partial(predict_kernel, groups, owners, time, min(4, tiles)),
        out_shape=shape((owners, 2, cl, slots), f32),
        in_specs=[vmem] * 6,
        out_specs=vmem,
        scratch_shapes=[
            pltpu.VMEM((groups, 2, cl, bl_dev), f32),
            pltpu.VMEM((masks, tiles, owners, LANES), f32),
            pltpu.VMEM((owners, tiles, 2 * groups, cl, LANES), f32),
            pltpu.VMEM((owners - 1, 2, cl, slots), f32),
            pltpu.VMEM((groups, 2, cl, bl_dev), f32),
            dma((groups - 1, bl_dev // LANES)),
            dma((groups - 1, bl_dev // LANES)),
            dma((owners - 1,)),
            dma((owners - 1,)),
        ]
        + [pltpu.VMEM((2, tiles, cl, LANES), f32)] * 2
        + [pltpu.VMEM((sources // groups, rows_per, min(4, tiles) * LANES), f32)] * groups,
        compiler_params=pltpu.CompilerParams(
            vmem_limit_bytes=32 << 20, collective_id=0, has_side_effects=True
        ),
        name="predict",
    )(*prepared)
    return pl.pallas_call(
        place_kernel,
        out_shape=jax.ShapeDtypeStruct(observed.shape, f32),
        in_specs=[vmem, vmem, vmem],
        out_specs=vmem,
        scratch_shapes=[pltpu.VMEM((2, cl, capacity + slots + LANES), f32)],
        compiler_params=pltpu.CompilerParams(vmem_limit_bytes=32 << 20),
        name="place",
    )(starts, pieces, observed)


def solution(mesh):
    placed = (
        P("dir", None, "bl"),
        P(None, "bl"),
        P(),
        P(),
        P(),
        P(),
        P("dir", None, None, None),
        P(),
        P(),
        P(),
        P(),
    )
    return jax.shard_map(
        on_device, mesh=mesh, in_specs=placed, out_specs=P("dir", None, "bl"), check_vma=False
    )
```

```python
import functools
import math

import jax
import jax.numpy as jnp
from jax import lax
from jax.experimental import pallas as pl
from jax.experimental.pallas import tpu as pltpu
from jax.sharding import PartitionSpec as P

LANES = 128
CHUNK = 8
PACE = 4
EARLY = 4
START = 3
FIRST = 2
BATCH = 16
MESH = pl.DeviceIdType.MESH
HIGH = lax.Precision.HIGHEST
NT = (((1,), (1,)), ((), ()))
P0, P1, P2, P3 = -2.2636507847492298, 1.3870216243251186, 4.937789609959605, 0.5033641130059734
K0, K1, K2 = 0.9997897140197886, -10.245898871410082, 1.823099221649536


def iota(shape, axis):
    return lax.broadcasted_iota(jnp.int32, shape, axis)


def flip(a, b, size):
    total = 0
    for i in range(int(math.log2(size))):
        total = total + lax.rem(lax.div(a, 2**i) + lax.div(b, 2**i), 2) * 2**i
    return total


def take(values, index):
    return jnp.take_along_axis(values, index, axis=1, mode="promise_in_bounds")


def thirds(value):
    high = value.astype(jnp.bfloat16).astype(jnp.float32)
    rest = value - high
    mid = rest.astype(jnp.bfloat16).astype(jnp.float32)
    return high, mid, rest - mid


def prepare_kernel(
    groups,
    owners,
    time,
    *refs,
):
    inputs = refs[:11]
    (
    sky_ref,
    wide_ref,
    base_ref,
    order_ref,
    table_ref,
    ids_ref,
    start_ref,
    spread_ref,
    uvw_ref,
    freq_ref,
    offs_ref,
    flux_ref,
    group_ref,
    gain_ref,
    first_ref,
    second_ref,
    exps_ref,
    plan_ref,
    plan_smem,
    sem,
    ) = refs[11:]
    d = lax.axis_index("dir")
    p = lax.axis_index("bl")
    cl = wide_ref.shape[1]
    sources = offs_ref.shape[1]
    per_group = sources // groups
    bl_dev = first_ref.shape[1]
    own = pl.ds(pl.multiple_of(p * bl_dev, bl_dev), bl_dev)
    held = refs[19:30]
    copies = {}
    for index in (4, 2, 3, 1, 9, 10, 0, 5, 6, 7, 8):
        source = inputs[index].at[:, own] if index in (6, 7) else inputs[index]
        copies[index] = pltpu.make_async_copy(source, held[index], sem.at[index])
        copies[index].start()

    def arrive(*indices):
        for index in indices:
            copies[index].wait()

    block_len = bl_dev // owners
    slots = block_len * time
    block_tiles = slots // LANES
    per_tile = LANES // time
    log_time = int(math.log2(time))
    chunks = bl_dev // LANES

    arrive(4, 2, 3, 1)
    member_row = group_ref[...].astype(jnp.float32)
    earlier = iota((sources, sources), 0) < iota((sources, sources), 1)
    equal = iota((sources, sources), 0) == iota((sources, sources), 1)
    member_col = jnp.sum(jnp.where(equal, member_row, 0.0), axis=1, keepdims=True)
    same = (jnp.abs(member_col - member_row) < 0.5) & earlier
    rank = jnp.sum(same.astype(jnp.float32), axis=0, keepdims=True)
    place = (member_row * per_group + rank + 0.5).astype(jnp.int32)
    pick = (iota((sources, sources), 0) == place).astype(jnp.float32).astype(jnp.bfloat16)

    def padded(rows):
        fill = jnp.zeros((8 - rows.shape[0], sources), jnp.float32)
        rows = jnp.concatenate([rows, fill], axis=0) if rows.shape[0] < 8 else rows
        return jnp.concatenate(thirds(rows), axis=0).astype(jnp.bfloat16)

    own_flux = jnp.zeros((cl, sources), jnp.float32)
    for i in range(groups):
        own_flux = own_flux + jnp.where(d == i, flux_ref[i * cl : (i + 1) * cl, :], 0.0)
    flux = lax.dot_general(padded(own_flux), pick, NT, preferred_element_type=jnp.float32)
    size = flux.shape[0] // 3
    flux = (flux[0:size] + flux[size : 2 * size] + flux[2 * size : 3 * size])[0:cl]
    offs = lax.dot_general(pick, padded(offs_ref[...]), NT, preferred_element_type=jnp.float32)
    east, north = [offs[:, i : i + 1] + offs[:, 8 + i : 9 + i] + offs[:, 16 + i : 17 + i] for i in range(2)]
    depth = jnp.sqrt(1.0 - east * east - north * north) - 1.0
    arrive(9, 10, 0, 5, 6, 7, 8)
    half = sources // 2
    kind = iota((sources, LANES), 1) % 8
    used = iota((sources, LANES), 1) % (LANES // 2) < 48
    spread = jnp.where(kind == 0, east, jnp.where(kind == 1, north, jnp.where(kind == 2, depth, 0.0)))
    spread = jnp.where(used, spread, 0.0)
    spread_ref[...] = jnp.where(iota((half, LANES), 1) < LANES // 2, spread[:half], spread[half:])
    high_rows = sky_ref.shape[0] // half
    turn_channel = iota((high_rows, flux_ref.shape[0]), 1) == d * cl + iota((high_rows, flux_ref.shape[0]), 0)
    turn_freq = jnp.sum(turn_channel.astype(jnp.float32) * freq_ref[...], axis=1, keepdims=True)
    turn_freq = jnp.broadcast_to(turn_freq, (high_rows, LANES))
    term = iota((high_rows, LANES), 1) % (LANES // 2) // 8
    mids, lows = (term == 2) | (term == 3), term == 5
    pair_rows = max(1, 16 // high_rows)
    share = [part.astype(jnp.float32) for part in thirds(own_flux)[:2]]
    if cl < 8:
        share = [jnp.concatenate([part, jnp.zeros((8 - cl, sources), jnp.float32)], axis=0) for part in share]
    order_row = jnp.broadcast_to(place, share[0].shape)
    ones = jnp.ones((2 * sources, LANES), jnp.float32).astype(jnp.bfloat16)
    for k in range(0, half, pair_rows):
        rows = []
        for i in range(pair_rows):
            high, mid, low = thirds(turn_freq * spread_ref[pl.ds(k + i, high_rows, stride=0), :])
            rows.append(jnp.where(mids, mid, jnp.where(lows, low, high)))
        rows = jnp.concatenate(rows, axis=0).astype(jnp.bfloat16)
        sky_ref[k * high_rows : (k + pair_rows) * high_rows, :] = rows
        if k % BATCH == 0:
            left = []
            for i in range(2 * k, 2 * k + 2 * BATCH):
                here = order_row == i
                left.append(jnp.concatenate([jnp.where(here, part, 0.0) for part in share], axis=1))
            left = jnp.concatenate(left, axis=0).astype(jnp.bfloat16)
            amounts = jnp.dot(left, ones, preferred_element_type=jnp.float32)
            amounts = amounts.reshape(2 * BATCH, share[0].shape[0], LANES)[:, 0:cl]
            wide_ref[2 * k : 2 * k + 2 * BATCH] = amounts
    for g in range(groups):
        part = jnp.sum(flux[:, g * per_group : (g + 1) * per_group], axis=1, keepdims=True)
        base_ref[g] = jnp.broadcast_to(part, (cl, LANES))

    for k in range(owners):
        rows = uvw_ref[:, k * slots : (k + 1) * slots]
        rows = jnp.concatenate([rows, jnp.zeros((8 - rows.shape[0], slots), jnp.float32)], axis=0)
        high, mid, low = thirds(rows)
        rows = jnp.concatenate([high, mid, high, mid, low, high], axis=0)
        order_ref[plan_smem[p, k]] = rows.astype(jnp.bfloat16)
    plan = plan_ref[...].astype(jnp.float32)
    own_plan = jnp.sum(
        jnp.where(iota((owners, owners), 0) == p, plan, 0.0), axis=0, keepdims=True
    )
    held_by = jnp.abs(own_plan - iota((owners, owners), 0).astype(jnp.float32)) < 0.5
    block_of = jnp.sum(
        jnp.where(held_by, iota((owners, owners), 1).astype(jnp.float32), 0.0), axis=1, keepdims=True
    )

    lane = iota((owners, LANES), 1)
    row = iota((owners, LANES), 0)
    for g in range(groups):
        for z in range(2):
            table_ref[g, z] = gain_ref[0, g * cl : (g + 1) * cl, z, :]
    for chunk in range(chunks):
        lanes = pl.ds(chunk * LANES, LANES)
        where_from = jnp.where((chunk * LANES + lane) // block_len == row, block_of, 0.0)
        where_from = (jnp.sum(where_from, axis=0, keepdims=True) + 0.5).astype(jnp.int32)
        source = where_from * block_len + (chunk * LANES + iota((1, LANES), 1)) % block_len
        source = jnp.broadcast_to(source, (cl, LANES))
        for which in range(3):
            ids = jnp.zeros((cl, LANES), jnp.int32)
            for part in range(chunks):
                begin = part * LANES
                if which == 2:
                    begin = pl.multiple_of(p * bl_dev + begin, LANES)
                table = (first_ref, second_ref, exps_ref)[which][:, pl.ds(begin, LANES)]
                table = jnp.broadcast_to(table, (cl, LANES))
                ids = jnp.where((source >> 7) == part, take(table, source & (LANES - 1)), ids)
            ids_ref[which : which + 1, lanes] = ids[0:1]

    exps_all = jnp.concatenate(
        [exps_ref[:, i * bl_dev : (i + 1) * bl_dev] for i in range(owners)], axis=0
    )
    rows_all = jnp.right_shift(jnp.full(exps_all.shape, time, jnp.int32), exps_all)
    rows_all = rows_all.astype(jnp.float32)
    to_owner = jnp.zeros((owners, 1), jnp.float32)
    for k in range(owners):
        count = jnp.sum(rows_all[:, k * block_len : (k + 1) * block_len], axis=1, keepdims=True)
        to_owner = to_owner + jnp.where(plan_ref[:, k : k + 1] == p, count, 0.0)
    starts = jnp.sum(jnp.where(row < lane, to_owner, 0.0), axis=0, keepdims=True)
    start_ref[...] = (starts + 0.5).astype(jnp.int32)


def predict_kernel(
    groups,
    owners,
    time,
    tiles,
    sky_ref,
    wide_ref,
    base_ref,
    order_ref,
    table_ref,
    ids_ref,
    piece_ref,
    pair_ref,
    mask_ref,
    kept_ref,
    send_ref,
    gather_ref,
    gain_send,
    gain_recv,
    piece_send,
    piece_recv,
    *more_refs,
):
    states, turns_refs = more_refs[:6], more_refs[6:]
    d = lax.axis_index("dir")
    p = lax.axis_index("bl")
    sources, cl, _ = wide_ref.shape
    per_group = sources // groups
    slots = order_ref.shape[2]
    block_len = slots // time
    block_tiles = slots // LANES
    per_tile = LANES // time
    log_time = int(math.log2(time))
    bits = int(math.log2(slots))

    barrier = pltpu.get_barrier_semaphore()
    for axis, me, size in (("dir", d, groups), ("bl", p, owners)):
        for step in range(1, size):
            pl.semaphore_signal(
                barrier, inc=1, device_id={axis: lax.rem(me + step, size)}, device_id_type=MESH
            )

    def owner_of(turn):
        return flip(p, owners - 1 - turn, owners)

    chunks = ids_ref.shape[1] // LANES
    per_chunk = LANES // block_len

    def gain_copy(step, chunk):
        other = lax.rem(d + step, groups)
        first = flip(lax.div(p, per_chunk), chunks - 1 - chunk, chunks) * LANES
        lanes = pl.ds(pl.multiple_of(first, LANES), LANES)
        return pltpu.make_async_remote_copy(
            src_ref=pair_ref.at[other, :, :, lanes],
            dst_ref=gather_ref.at[d, :, :, lanes],
            send_sem=gain_send.at[step - 1, chunk],
            recv_sem=gain_recv.at[step - 1, chunk],
            device_id={"dir": other},
            device_id_type=MESH,
        )

    def gains_arrive(chunk):
        for step in range(1, groups):
            gain_copy(step, chunk).wait()

    def piece_copy(step):
        return pltpu.make_async_remote_copy(
            src_ref=send_ref.at[step],
            dst_ref=piece_ref.at[p],
            send_sem=piece_send.at[step],
            recv_sem=piece_recv.at[step],
            device_id={"bl": owner_of(step)},
            device_id_type=MESH,
        )

    flux_sum = [base_ref[g] for g in range(groups)]
    lane = iota((cl, LANES), 1)
    steps = block_tiles // tiles

    def fill(turn, step, g):
        ln = pl.ds(pl.multiple_of(step * tiles * LANES, LANES), tiles * LANES)
        turns_ref = turns_refs[g]
        rows = per_group * turns_ref.shape[1]
        near = g % (groups // 2)
        right = order_ref[owner_of(turn), :, ln]
        fill_rows = LANES // 2 if g >= groups // 2 else LANES - right.shape[0]
        blank = jnp.zeros((fill_rows, tiles * LANES), jnp.bfloat16)
        if g >= groups // 2:
            rest = jnp.zeros((LANES // 2 - right.shape[0], tiles * LANES), jnp.bfloat16)
            right = jnp.concatenate([blank, right, rest], axis=0)
        else:
            right = jnp.concatenate([right, blank], axis=0)
        turns = jnp.dot(
            sky_ref[near * rows : (near + 1) * rows, :], right, preferred_element_type=jnp.float32
        )
        turns_ref[...] = turns.reshape(turns_ref.shape)

    def add_sources(turn, step, work=(), pace=3, drain=True):
        for g in range(groups):
            if g + 1 < groups:
                fill(turn, step, g + 1)
            else:
                ahead = step + 1
                fill(lax.rem(turn + lax.div(ahead, steps), owners), lax.rem(ahead, steps), 0)

            def source(i, acc):
                acc = list(acc)
                amount = wide_ref[g * per_group + i]
                for t in range(tiles):
                    turns = turns_refs[g][i, 0:cl, t * LANES : (t + 1) * LANES]
                    x = turns - jnp.round(turns)
                    z = x * x
                    m = (z + P0) * z
                    s = x * (m + P1)
                    weighted = amount * s
                    acc[2 * t] = acc[2 * t] + weighted * s
                    acc[2 * t + 1] = acc[2 * t + 1] + weighted * ((m + P2) * (m + P3))
                return tuple(acc)

            acc = tuple(jnp.zeros((cl, LANES), jnp.float32) for _ in range(2 * tiles))
            for begin in range(0, per_group, CHUNK):
                acc = lax.fori_loop(begin, begin + CHUNK, source, acc, unroll=CHUNK)
                for stage in list(work) * pace:
                    next(stage, None)
            for t in range(tiles):
                kept_ref[turn, step * tiles + t, 2 * g] = K0 * flux_sum[g] + K1 * acc[2 * t]
                kept_ref[turn, step * tiles + t, 2 * g + 1] = -K2 * acc[2 * t + 1]
        for stage in work if drain else ():
            for _ in stage:
                pass

    def finish(turn, out_ref, where, states):
        owner = owner_of(turn)
        chunk = pl.multiple_of(lax.div(owner * block_len, LANES) * LANES, LANES)
        first_bl = lax.rem(owner * block_len, LANES) + (lane >> log_time)

        def wide(index, t):
            return mask_ref[index, t, pl.ds(owner, cl, stride=0), :]

        for t in range(block_tiles):
            index = first_bl + t * per_tile
            model_r = jnp.zeros((cl, LANES), jnp.float32)
            model_i = jnp.zeros((cl, LANES), jnp.float32)
            for g in range(groups):
                gr = take(gather_ref[g, 0, :, pl.ds(chunk, LANES)], index)
                gi = take(gather_ref[g, 1, :, pl.ds(chunk, LANES)], index)
                real, imag = kept_ref[turn, t, 2 * g], kept_ref[turn, t, 2 * g + 1]
                model_r = model_r + (real * gr - imag * gi)
                model_i = model_i + (real * gi + imag * gr)
            scale = wide(log_time + bits + 1, t)
            states[0][0, t] = model_r * scale
            states[0][1, t] = model_i * scale
            yield

        stages = log_time + bits
        for stage in range(stages):
            size = 1 << (stage if stage < log_time else stage - log_time)
            jump, size = size // LANES, size % LANES
            for z in range(2):
                old, new = states[stage % 2], states[1 - stage % 2]
                spun = [old[z, t] for t in range(block_tiles)]
                if size:
                    spun = [pltpu.roll(x, LANES - size, 1) for x in spun]
                for t in range(block_tiles):
                    near = spun[(t + jump) % block_tiles]
                    if size:
                        near = jnp.where(lane < LANES - size, near, spun[(t + 1) % block_tiles])
                    if stage < log_time:
                        value = old[z, t] + wide(stage, t) * near
                    else:
                        value = jnp.where(wide(stage, t) > 0.5, near, old[z, t])
                    if stage == stages - 1:
                        value = jnp.where(wide(stages, t) > 0.5, value, 0.0)
                        out_ref[where, z, :, t * LANES : (t + 1) * LANES] = value
                    else:
                        new[z, t] = value
                yield

    def send(turn, which=0):
        yield from finish(turn, send_ref, turn, states[2 * which : 2 * which + 2])
        yield
        piece_copy(turn).start()

    def tables():
        station_total = table_ref.shape[3]
        for chunk in range(chunks):
            lanes = pl.ds(chunk * LANES, LANES)
            looked = []
            for which in range(2):
                ids = jnp.broadcast_to(ids_ref[which : which + 1, lanes], (cl, LANES))
                low, high = ids & (LANES - 1), ids >> 7
                rows = []
                for g in range(groups):
                    for z in range(2):
                        total = jnp.zeros((cl, LANES), jnp.float32)
                        for part in range(station_total // LANES):
                            table = table_ref[g, z, :, pl.ds(part * LANES, LANES)]
                            total = jnp.where(high == part, take(table, low), total)
                        rows.append(total)
                looked.append(rows)
                yield
            first, second = looked
            for g in range(groups):
                ar, ai, br, bi = first[2 * g], first[2 * g + 1], second[2 * g], second[2 * g + 1]
                pair_ref[g, 0, :, lanes] = ar * br + ai * bi
                pair_ref[g, 1, :, lanes] = ai * br - ar * bi
        gather_ref[d] = pair_ref[d]

        exps = []
        wide_lane = iota((owners, LANES), 1)
        for t in range(block_tiles):
            source = iota((owners, LANES), 0) * block_len + t * per_tile + (wide_lane >> log_time)
            found = jnp.zeros((owners, LANES), jnp.int32)
            for part in range(chunks):
                table = ids_ref[2:3, part * LANES : (part + 1) * LANES]
                table = jnp.broadcast_to(table, (owners, LANES))
                got = [take(table[i : i + 8], source[i : i + 8] & (LANES - 1)) for i in range(0, owners, 8)]
                got = jnp.concatenate(got) if owners > 8 else got[0]
                found = jnp.where((source >> 7) == part, got, found)
            exps.append(found)
            if t % 2 == 1:
                yield
        exps = jnp.concatenate(exps, axis=1)

        def put(index, values):
            for t in range(block_tiles):
                mask_ref[index, t] = values[:, t * LANES : (t + 1) * LANES]

        position = iota((owners, slots), 1)
        width = jnp.left_shift(jnp.ones_like(exps), exps)
        valid = ((position & (width - 1)) == 0).astype(jnp.int32)
        scale = jnp.ones((owners, slots), jnp.float32)
        for s in range(log_time):
            scale = jnp.where(exps > s, scale * 0.5, scale)
            put(s, (exps > s).astype(jnp.float32))
        put(log_time + bits + 1, scale)
        yield
        prefix = valid
        for b in range(bits):
            prefix = prefix + jnp.where(position >= 1 << b, pltpu.roll(prefix, 1 << b, 1), 0)
            if b % 2 == 1:
                yield
        count = jnp.max(prefix, axis=1, keepdims=True)
        put(log_time + bits, (position < count).astype(jnp.float32))
        held = jnp.where(valid == 1, position - (prefix - valid), 0)
        for b in range(bits):
            here = (held >> b) & 1
            moved = pltpu.roll(held, slots - (1 << b), 1)
            come = (moved >> b) & 1
            put(log_time + b, come.astype(jnp.float32))
            held = jnp.where(come == 1, moved, jnp.where(here == 1, 0, held))
            yield

    def early(index, carry):
        @pl.when(index == START)
        def _():
            pl.semaphore_wait(barrier, groups - 1 + owners - 1)
            for chunk in range(chunks):
                for step in range(1, groups):
                    gain_copy(step, chunk).start()

        add_sources(lax.div(index, steps), lax.rem(index, steps))
        return carry

    fill(0, 0, 0)
    work = [tables()]
    for index in range(FIRST):
        add_sources(index // steps, index % steps, work, 1, index == FIRST - 1)
    lax.fori_loop(FIRST, EARLY * steps, early, 0)

    seen = 0
    ready = 0
    for turn in (EARLY, EARLY + 1):
        batch = list(range(ready, ready + EARLY + EARLY - turn - 1))
        batch = batch if len(batch) < turn - ready else list(range(ready, turn))
        ready += len(batch)
        while seen * per_chunk < ready:
            gains_arrive(seen)
            seen += 1
        halves = [batch] if steps == 1 else [batch[:1], batch[1:]]
        for step in range(steps):
            now = halves[step] if step < len(halves) else []
            add_sources(turn, step, [send(done, which) for which, done in enumerate(now)])
    for chunk in range(seen, chunks):
        gains_arrive(chunk)

    def block_body(turn, carry):
        add_sources(turn, 0, [send(turn - 1)], PACE)
        for step in range(1, steps):
            add_sources(turn, step)
        return carry

    lax.fori_loop(EARLY + 2, owners, block_body, 0)

    for _ in finish(owners - 1, piece_ref, p, states):
        pass
    for step in range(owners - 1):
        piece_copy(step).wait()


def place_kernel(start_ref, piece_ref, observed_ref, out_ref, total_ref):
    owners, _, cl, slots = piece_ref.shape
    capacity = observed_ref.shape[2]
    total_ref[...] = jnp.zeros_like(total_ref)
    position = iota((cl, LANES), 1)
    for index in range(owners):
        start = start_ref[0, index]
        low = start & (LANES - 1)
        base = pl.multiple_of(start - low, LANES)
        for z in range(2):
            spun = [
                pltpu.roll(piece_ref[index, z, :, pl.ds(t * LANES, LANES)], low, 1)
                for t in range(slots // LANES)
            ]
            for t in range(slots // LANES + 1):
                lanes = pl.ds(pl.multiple_of(base + t * LANES, LANES), LANES)
                if t == 0:
                    value = jnp.where(position >= low, spun[t], total_ref[z, :, lanes])
                elif t < slots // LANES:
                    value = jnp.where(position >= low, spun[t], spun[t - 1])
                else:
                    value = jnp.where(position >= low, 0.0, spun[t - 1])
                total_ref[z, :, lanes] = value
    for z in range(2):
        out_ref[:, z, :] = observed_ref[:, z, :] - total_ref[z, :, pl.ds(0, capacity)]


def on_device(
    observed,
    baseline_uvw_rows,
    frequencies,
    source_offset,
    source_flux,
    source_group,
    direction_gain,
    station_first,
    station_second,
    average_exponent,
    owner_plan,
):
    owners = lax.axis_size("bl")
    groups = lax.axis_size("dir")
    cl, _, capacity = observed.shape
    bl_dev = station_first.shape[0] // owners
    rows = baseline_uvw_rows.shape[1]
    time = rows // bl_dev
    slots = rows // owners
    tiles = slots // LANES
    sources = source_group.shape[0]
    vmem = pl.BlockSpec(memory_space=pltpu.VMEM)
    masks = int(math.log2(time)) + int(math.log2(slots)) + 2
    rows_per = max(8, cl)
    f32 = jnp.float32
    shape = jax.ShapeDtypeStruct
    *prepared, starts = pl.pallas_call(
        functools.partial(prepare_kernel, groups, owners, time),
        out_shape=(
            shape((sources // 2 * rows_per, LANES), jnp.bfloat16),
            shape((sources, cl, LANES), f32),
            shape((groups, cl, LANES), f32),
            shape((owners, 48, slots), jnp.bfloat16),
            shape((groups, 2, cl, direction_gain.shape[3]), f32),
            shape((8, bl_dev), jnp.int32),
            shape((1, LANES), jnp.int32),
        ),
        in_specs=[pl.BlockSpec(memory_space=pltpu.HBM)] * 11,
        out_specs=(vmem,) * 7,
        scratch_shapes=[
            pltpu.VMEM((sources // 2, LANES), f32),
            pltpu.VMEM(baseline_uvw_rows.shape, f32),
            pltpu.VMEM((1, frequencies.shape[0]), f32),
            pltpu.VMEM(source_offset.shape, f32),
            pltpu.VMEM(source_flux.shape, f32),
            pltpu.VMEM((1, sources), jnp.int32),
            pltpu.VMEM(direction_gain.shape, f32),
            pltpu.VMEM((1, bl_dev), jnp.int32),
            pltpu.VMEM((1, bl_dev), jnp.int32),
            pltpu.VMEM((1, average_exponent.shape[0]), jnp.int32),
            pltpu.VMEM(owner_plan.shape, jnp.int32),
            pltpu.SMEM(owner_plan.shape, jnp.int32),
            pltpu.SemaphoreType.DMA((11,)),
        ],
        compiler_params=pltpu.CompilerParams(vmem_limit_bytes=32 << 20),
        name="prepare",
    )(
        *[
            pltpu.with_memory_space_constraint(array, pltpu.HBM)
            for array in (
                baseline_uvw_rows,
                frequencies.reshape(1, -1),
                source_offset,
                source_flux,
                source_group.reshape(1, -1),
                direction_gain,
                station_first.reshape(1, -1),
                station_second.reshape(1, -1),
                average_exponent.reshape(1, -1),
                owner_plan,
                owner_plan,
            )
        ]
    )
    dma = pltpu.SemaphoreType.DMA
    pieces = pl.pallas_call(
        functools.partial(predict_kernel, groups, owners, time, min(4, tiles)),
        out_shape=shape((owners, 2, cl, slots), f32),
        in_specs=[vmem] * 6,
        out_specs=vmem,
        scratch_shapes=[
            pltpu.VMEM((groups, 2, cl, bl_dev), f32),
            pltpu.VMEM((masks, tiles, owners, LANES), f32),
            pltpu.VMEM((owners, tiles, 2 * groups, cl, LANES), f32),
            pltpu.VMEM((owners - 1, 2, cl, slots), f32),
            pltpu.VMEM((groups, 2, cl, bl_dev), f32),
            dma((groups - 1, bl_dev // LANES)),
            dma((groups - 1, bl_dev // LANES)),
            dma((owners - 1,)),
            dma((owners - 1,)),
        ]
        + [pltpu.VMEM((2, tiles, cl, LANES), f32)] * 6
        + [pltpu.VMEM((sources // groups, rows_per, min(4, tiles) * LANES), f32)] * groups,
        compiler_params=pltpu.CompilerParams(
            vmem_limit_bytes=32 << 20, collective_id=0, has_side_effects=True
        ),
        name="predict",
    )(*prepared)
    return pl.pallas_call(
        place_kernel,
        out_shape=jax.ShapeDtypeStruct(observed.shape, f32),
        in_specs=[vmem, vmem, vmem],
        out_specs=vmem,
        scratch_shapes=[pltpu.VMEM((2, cl, capacity + slots + LANES), f32)],
        compiler_params=pltpu.CompilerParams(vmem_limit_bytes=32 << 20),
        name="place",
    )(starts, pieces, observed)


def solution(mesh):
    placed = (
        P("dir", None, "bl"),
        P(None, "bl"),
        P(),
        P(),
        P(),
        P(),
        P("dir", None, None, None),
        P(),
        P(),
        P(),
        P(),
    )
    return jax.shard_map(
        on_device, mesh=mesh, in_specs=placed, out_specs=P("dir", None, "bl"), check_vma=False
    )
```

```python
import functools
import math

import jax
import jax.numpy as jnp
from jax import lax
from jax.experimental import pallas as pl
from jax.experimental.pallas import tpu as pltpu
from jax.sharding import PartitionSpec as P

LANES = 128
CHUNK = 8
PACE = 4
EARLY = 4
START = 3
FIRST = 2
BATCH = 16
MESH = pl.DeviceIdType.MESH
HIGH = lax.Precision.HIGHEST
NT = (((1,), (1,)), ((), ()))
P0, P1, P2, P3 = -2.2636507847492298, 1.3870216243251186, 4.937789609959605, 0.5033641130059734
K0, K1, K2 = 0.9997897140197886, -10.245898871410082, 1.823099221649536


def iota(shape, axis):
    return lax.broadcasted_iota(jnp.int32, shape, axis)


def flip(a, b, size):
    total = 0
    for i in range(int(math.log2(size))):
        total = total + lax.rem(lax.div(a, 2**i) + lax.div(b, 2**i), 2) * 2**i
    return total


def take(values, index):
    return jnp.take_along_axis(values, index, axis=1, mode="promise_in_bounds")


def thirds(value):
    high = value.astype(jnp.bfloat16).astype(jnp.float32)
    rest = value - high
    mid = rest.astype(jnp.bfloat16).astype(jnp.float32)
    return high, mid, rest - mid


def prepare_kernel(
    groups,
    owners,
    time,
    *refs,
):
    inputs = refs[:11]
    (
    sky_ref,
    wide_ref,
    base_ref,
    order_ref,
    table_ref,
    ids_ref,
    start_ref,
    spread_ref,
    uvw_ref,
    freq_ref,
    offs_ref,
    flux_ref,
    group_ref,
    gain_ref,
    first_ref,
    second_ref,
    exps_ref,
    plan_ref,
    plan_smem,
    sem,
    ) = refs[11:]
    d = lax.axis_index("dir")
    p = lax.axis_index("bl")
    cl = wide_ref.shape[1]
    sources = offs_ref.shape[1]
    per_group = sources // groups
    bl_dev = first_ref.shape[1]
    own = pl.ds(pl.multiple_of(p * bl_dev, bl_dev), bl_dev)
    held = refs[19:30]
    copies = {}
    for index in (4, 2, 3, 1, 9, 10, 0, 5, 6, 7, 8):
        source = inputs[index].at[:, own] if index in (6, 7) else inputs[index]
        copies[index] = pltpu.make_async_copy(source, held[index], sem.at[index])
        copies[index].start()

    def arrive(*indices):
        for index in indices:
            copies[index].wait()

    block_len = bl_dev // owners
    slots = block_len * time
    block_tiles = slots // LANES
    per_tile = LANES // time
    log_time = int(math.log2(time))
    chunks = bl_dev // LANES

    arrive(4, 2, 3, 1)
    member_row = group_ref[...].astype(jnp.float32)
    earlier = iota((sources, sources), 0) < iota((sources, sources), 1)
    equal = iota((sources, sources), 0) == iota((sources, sources), 1)
    member_col = jnp.sum(jnp.where(equal, member_row, 0.0), axis=1, keepdims=True)
    same = (jnp.abs(member_col - member_row) < 0.5) & earlier
    rank = jnp.sum(same.astype(jnp.float32), axis=0, keepdims=True)
    place = (member_row * per_group + rank + 0.5).astype(jnp.int32)
    pick = (iota((sources, sources), 0) == place).astype(jnp.float32).astype(jnp.bfloat16)

    def padded(rows):
        fill = jnp.zeros((8 - rows.shape[0], sources), jnp.float32)
        rows = jnp.concatenate([rows, fill], axis=0) if rows.shape[0] < 8 else rows
        return jnp.concatenate(thirds(rows), axis=0).astype(jnp.bfloat16)

    own_flux = jnp.zeros((cl, sources), jnp.float32)
    for i in range(groups):
        own_flux = own_flux + jnp.where(d == i, flux_ref[i * cl : (i + 1) * cl, :], 0.0)
    flux = lax.dot_general(padded(own_flux), pick, NT, preferred_element_type=jnp.float32)
    size = flux.shape[0] // 3
    flux = (flux[0:size] + flux[size : 2 * size] + flux[2 * size : 3 * size])[0:cl]
    offs = lax.dot_general(pick, padded(offs_ref[...]), NT, preferred_element_type=jnp.float32)
    east, north = [offs[:, i : i + 1] + offs[:, 8 + i : 9 + i] + offs[:, 16 + i : 17 + i] for i in range(2)]
    depth = jnp.sqrt(1.0 - east * east - north * north) - 1.0
    arrive(9, 10, 0, 5, 6, 7, 8)
    half = sources // 2
    kind = iota((sources, LANES), 1) % 8
    used = iota((sources, LANES), 1) % (LANES // 2) < 48
    spread = jnp.where(kind == 0, east, jnp.where(kind == 1, north, jnp.where(kind == 2, depth, 0.0)))
    spread = jnp.where(used, spread, 0.0)
    spread_ref[...] = jnp.where(iota((half, LANES), 1) < LANES // 2, spread[:half], spread[half:])
    high_rows = sky_ref.shape[0] // half
    turn_channel = iota((high_rows, flux_ref.shape[0]), 1) == d * cl + iota((high_rows, flux_ref.shape[0]), 0)
    turn_freq = jnp.sum(turn_channel.astype(jnp.float32) * freq_ref[...], axis=1, keepdims=True)
    turn_freq = jnp.broadcast_to(turn_freq, (high_rows, LANES))
    term = iota((high_rows, LANES), 1) % (LANES // 2) // 8
    mids, lows = (term == 2) | (term == 3), term == 5
    pair_rows = max(1, 16 // high_rows)
    share = [part.astype(jnp.float32) for part in thirds(own_flux)[:2]]
    if cl < 8:
        share = [jnp.concatenate([part, jnp.zeros((8 - cl, sources), jnp.float32)], axis=0) for part in share]
    order_row = jnp.broadcast_to(place, share[0].shape)
    ones = jnp.ones((2 * sources, LANES), jnp.float32).astype(jnp.bfloat16)
    for k in range(0, half, pair_rows):
        rows = []
        for i in range(pair_rows):
            high, mid, low = thirds(turn_freq * spread_ref[pl.ds(k + i, high_rows, stride=0), :])
            rows.append(jnp.where(mids, mid, jnp.where(lows, low, high)))
        rows = jnp.concatenate(rows, axis=0).astype(jnp.bfloat16)
        sky_ref[k * high_rows : (k + pair_rows) * high_rows, :] = rows
        if k % BATCH == 0:
            left = []
            for i in range(2 * k, 2 * k + 2 * BATCH):
                here = order_row == i
                left.append(jnp.concatenate([jnp.where(here, part, 0.0) for part in share], axis=1))
            left = jnp.concatenate(left, axis=0).astype(jnp.bfloat16)
            amounts = jnp.dot(left, ones, preferred_element_type=jnp.float32)
            amounts = amounts.reshape(2 * BATCH, share[0].shape[0], LANES)[:, 0:cl]
            wide_ref[2 * k : 2 * k + 2 * BATCH] = amounts
    for g in range(groups):
        part = jnp.sum(flux[:, g * per_group : (g + 1) * per_group], axis=1, keepdims=True)
        base_ref[g] = jnp.broadcast_to(part, (cl, LANES))

    for k in range(owners):
        rows = uvw_ref[:, k * slots : (k + 1) * slots]
        rows = jnp.concatenate([rows, jnp.zeros((8 - rows.shape[0], slots), jnp.float32)], axis=0)
        high, mid, low = thirds(rows)
        rows = jnp.concatenate([high, mid, high, mid, low, high], axis=0)
        order_ref[plan_smem[p, k]] = rows.astype(jnp.bfloat16)
    plan = plan_ref[...].astype(jnp.float32)
    own_plan = jnp.sum(
        jnp.where(iota((owners, owners), 0) == p, plan, 0.0), axis=0, keepdims=True
    )
    held_by = jnp.abs(own_plan - iota((owners, owners), 0).astype(jnp.float32)) < 0.5
    block_of = jnp.sum(
        jnp.where(held_by, iota((owners, owners), 1).astype(jnp.float32), 0.0), axis=1, keepdims=True
    )

    lane = iota((owners, LANES), 1)
    row = iota((owners, LANES), 0)
    for g in range(groups):
        for z in range(2):
            table_ref[g, z] = gain_ref[0, g * cl : (g + 1) * cl, z, :]
    for chunk in range(chunks):
        lanes = pl.ds(chunk * LANES, LANES)
        where_from = jnp.where((chunk * LANES + lane) // block_len == row, block_of, 0.0)
        where_from = (jnp.sum(where_from, axis=0, keepdims=True) + 0.5).astype(jnp.int32)
        source = where_from * block_len + (chunk * LANES + iota((1, LANES), 1)) % block_len
        source = jnp.broadcast_to(source, (cl, LANES))
        for which in range(3):
            ids = jnp.zeros((cl, LANES), jnp.int32)
            for part in range(chunks):
                begin = part * LANES
                if which == 2:
                    begin = pl.multiple_of(p * bl_dev + begin, LANES)
                table = (first_ref, second_ref, exps_ref)[which][:, pl.ds(begin, LANES)]
                table = jnp.broadcast_to(table, (cl, LANES))
                ids = jnp.where((source >> 7) == part, take(table, source & (LANES - 1)), ids)
            ids_ref[which : which + 1, lanes] = ids[0:1]

    exps_all = jnp.concatenate(
        [exps_ref[:, i * bl_dev : (i + 1) * bl_dev] for i in range(owners)], axis=0
    )
    rows_all = jnp.right_shift(jnp.full(exps_all.shape, time, jnp.int32), exps_all)
    rows_all = rows_all.astype(jnp.float32)
    to_owner = jnp.zeros((owners, 1), jnp.float32)
    for k in range(owners):
        count = jnp.sum(rows_all[:, k * block_len : (k + 1) * block_len], axis=1, keepdims=True)
        to_owner = to_owner + jnp.where(plan_ref[:, k : k + 1] == p, count, 0.0)
    starts = jnp.sum(jnp.where(row < lane, to_owner, 0.0), axis=0, keepdims=True)
    start_ref[...] = (starts + 0.5).astype(jnp.int32)


def predict_kernel(
    groups,
    owners,
    time,
    tiles,
    sky_ref,
    wide_ref,
    base_ref,
    order_ref,
    table_ref,
    ids_ref,
    piece_ref,
    pair_ref,
    mask_ref,
    kept_ref,
    send_ref,
    gather_ref,
    gain_send,
    gain_recv,
    piece_send,
    piece_recv,
    *more_refs,
):
    states, turns_refs = more_refs[:4], more_refs[4:]
    d = lax.axis_index("dir")
    p = lax.axis_index("bl")
    sources, cl, _ = wide_ref.shape
    per_group = sources // groups
    slots = order_ref.shape[2]
    block_len = slots // time
    block_tiles = slots // LANES
    per_tile = LANES // time
    log_time = int(math.log2(time))
    bits = int(math.log2(slots))

    barrier = pltpu.get_barrier_semaphore()
    for axis, me, size in (("dir", d, groups), ("bl", p, owners)):
        for step in range(1, size):
            pl.semaphore_signal(
                barrier, inc=1, device_id={axis: lax.rem(me + step, size)}, device_id_type=MESH
            )

    def owner_of(turn):
        return flip(p, owners - 1 - turn, owners)

    chunks = ids_ref.shape[1] // LANES
    per_chunk = LANES // block_len

    def gain_copy(step, chunk):
        other = lax.rem(d + step, groups)
        first = flip(lax.div(p, per_chunk), chunks - 1 - chunk, chunks) * LANES
        lanes = pl.ds(pl.multiple_of(first, LANES), LANES)
        return pltpu.make_async_remote_copy(
            src_ref=pair_ref.at[other, :, :, lanes],
            dst_ref=gather_ref.at[d, :, :, lanes],
            send_sem=gain_send.at[step - 1, chunk],
            recv_sem=gain_recv.at[step - 1, chunk],
            device_id={"dir": other},
            device_id_type=MESH,
        )

    def gains_arrive(chunk):
        for step in range(1, groups):
            gain_copy(step, chunk).wait()

    def piece_copy(step):
        return pltpu.make_async_remote_copy(
            src_ref=send_ref.at[step],
            dst_ref=piece_ref.at[p],
            send_sem=piece_send.at[step],
            recv_sem=piece_recv.at[step],
            device_id={"bl": owner_of(step)},
            device_id_type=MESH,
        )

    flux_sum = [base_ref[g] for g in range(groups)]
    lane = iota((cl, LANES), 1)
    steps = block_tiles // tiles

    def fill(turn, step, g):
        ln = pl.ds(pl.multiple_of(step * tiles * LANES, LANES), tiles * LANES)
        turns_ref = turns_refs[g]
        rows = per_group * turns_ref.shape[1]
        near = g % (groups // 2)
        right = order_ref[owner_of(turn), :, ln]
        fill_rows = LANES // 2 if g >= groups // 2 else LANES - right.shape[0]
        blank = jnp.zeros((fill_rows, tiles * LANES), jnp.bfloat16)
        if g >= groups // 2:
            rest = jnp.zeros((LANES // 2 - right.shape[0], tiles * LANES), jnp.bfloat16)
            right = jnp.concatenate([blank, right, rest], axis=0)
        else:
            right = jnp.concatenate([right, blank], axis=0)
        turns = jnp.dot(
            sky_ref[near * rows : (near + 1) * rows, :], right, preferred_element_type=jnp.float32
        )
        turns_ref[...] = turns.reshape(turns_ref.shape)

    def add_sources(turn, step, work=(), pace=3, drain=True, middle=None):
        for g in range(groups):
            if g + 1 < groups:
                fill(turn, step, g + 1)
            else:
                ahead = step + 1
                fill(lax.rem(turn + lax.div(ahead, steps), owners), lax.rem(ahead, steps), 0)

            def source(i, acc):
                acc = list(acc)
                amount = wide_ref[g * per_group + i]
                for t in range(tiles):
                    turns = turns_refs[g][i, 0:cl, t * LANES : (t + 1) * LANES]
                    x = turns - jnp.round(turns)
                    z = x * x
                    m = (z + P0) * z
                    s = x * (m + P1)
                    weighted = amount * s
                    acc[2 * t] = acc[2 * t] + weighted * s
                    acc[2 * t + 1] = acc[2 * t + 1] + weighted * ((m + P2) * (m + P3))
                return tuple(acc)

            acc = tuple(jnp.zeros((cl, LANES), jnp.float32) for _ in range(2 * tiles))
            for begin in range(0, per_group, CHUNK):
                acc = lax.fori_loop(begin, begin + CHUNK, source, acc, unroll=CHUNK)
                for stage in list(work) * pace:
                    next(stage, None)
            for t in range(tiles):
                kept_ref[turn, step * tiles + t, 2 * g] = K0 * flux_sum[g] + K1 * acc[2 * t]
                kept_ref[turn, step * tiles + t, 2 * g + 1] = -K2 * acc[2 * t + 1]
            if middle is not None and g == groups // 2 - 1:
                middle()
        for stage in work if drain else ():
            for _ in stage:
                pass

    def finish(turn, out_ref, where, states):
        owner = owner_of(turn)
        chunk = pl.multiple_of(lax.div(owner * block_len, LANES) * LANES, LANES)
        first_bl = lax.rem(owner * block_len, LANES) + (lane >> log_time)

        def wide(index, t):
            return mask_ref[index, t, pl.ds(owner, cl, stride=0), :]

        for t in range(block_tiles):
            index = first_bl + t * per_tile
            model_r = jnp.zeros((cl, LANES), jnp.float32)
            model_i = jnp.zeros((cl, LANES), jnp.float32)
            for g in range(groups):
                gr = take(gather_ref[g, 0, :, pl.ds(chunk, LANES)], index)
                gi = take(gather_ref[g, 1, :, pl.ds(chunk, LANES)], index)
                real, imag = kept_ref[turn, t, 2 * g], kept_ref[turn, t, 2 * g + 1]
                model_r = model_r + (real * gr - imag * gi)
                model_i = model_i + (real * gi + imag * gr)
            scale = wide(log_time + bits + 1, t)
            states[0][0, t] = model_r * scale
            states[0][1, t] = model_i * scale
            yield

        stages = log_time + bits
        for stage in range(stages):
            size = 1 << (stage if stage < log_time else stage - log_time)
            jump, size = size // LANES, size % LANES
            for z in range(2):
                old, new = states[stage % 2], states[1 - stage % 2]
                spun = [old[z, t] for t in range(block_tiles)]
                if size:
                    spun = [pltpu.roll(x, LANES - size, 1) for x in spun]
                for t in range(block_tiles):
                    near = spun[(t + jump) % block_tiles]
                    if size:
                        near = jnp.where(lane < LANES - size, near, spun[(t + 1) % block_tiles])
                    if stage < log_time:
                        value = old[z, t] + wide(stage, t) * near
                    else:
                        value = jnp.where(wide(stage, t) > 0.5, near, old[z, t])
                    if stage == stages - 1:
                        value = jnp.where(wide(stages, t) > 0.5, value, 0.0)
                        out_ref[where, z, :, t * LANES : (t + 1) * LANES] = value
                    else:
                        new[z, t] = value
                yield

    def send(turn, which=0):
        yield from finish(turn, send_ref, turn, states[2 * which : 2 * which + 2])
        yield
        piece_copy(turn).start()

    def tables():
        station_total = table_ref.shape[3]
        for chunk in range(chunks):
            lanes = pl.ds(chunk * LANES, LANES)
            looked = []
            for which in range(2):
                ids = jnp.broadcast_to(ids_ref[which : which + 1, lanes], (cl, LANES))
                low, high = ids & (LANES - 1), ids >> 7
                rows = []
                for g in range(groups):
                    for z in range(2):
                        total = jnp.zeros((cl, LANES), jnp.float32)
                        for part in range(station_total // LANES):
                            table = table_ref[g, z, :, pl.ds(part * LANES, LANES)]
                            total = jnp.where(high == part, take(table, low), total)
                        rows.append(total)
                looked.append(rows)
                yield
            first, second = looked
            for g in range(groups):
                ar, ai, br, bi = first[2 * g], first[2 * g + 1], second[2 * g], second[2 * g + 1]
                pair_ref[g, 0, :, lanes] = ar * br + ai * bi
                pair_ref[g, 1, :, lanes] = ai * br - ar * bi
        gather_ref[d] = pair_ref[d]

        exps = []
        wide_lane = iota((owners, LANES), 1)
        for t in range(block_tiles):
            source = iota((owners, LANES), 0) * block_len + t * per_tile + (wide_lane >> log_time)
            found = jnp.zeros((owners, LANES), jnp.int32)
            for part in range(chunks):
                table = ids_ref[2:3, part * LANES : (part + 1) * LANES]
                table = jnp.broadcast_to(table, (owners, LANES))
                got = [take(table[i : i + 8], source[i : i + 8] & (LANES - 1)) for i in range(0, owners, 8)]
                got = jnp.concatenate(got) if owners > 8 else got[0]
                found = jnp.where((source >> 7) == part, got, found)
            exps.append(found)
            if t % 2 == 1:
                yield
        exps = jnp.concatenate(exps, axis=1)

        def put(index, values):
            for t in range(block_tiles):
                mask_ref[index, t] = values[:, t * LANES : (t + 1) * LANES]

        position = iota((owners, slots), 1)
        width = jnp.left_shift(jnp.ones_like(exps), exps)
        valid = ((position & (width - 1)) == 0).astype(jnp.int32)
        scale = jnp.ones((owners, slots), jnp.float32)
        for s in range(log_time):
            scale = jnp.where(exps > s, scale * 0.5, scale)
            put(s, (exps > s).astype(jnp.float32))
        put(log_time + bits + 1, scale)
        yield
        prefix = valid
        for b in range(bits):
            prefix = prefix + jnp.where(position >= 1 << b, pltpu.roll(prefix, 1 << b, 1), 0)
            if b % 2 == 1:
                yield
        count = jnp.max(prefix, axis=1, keepdims=True)
        put(log_time + bits, (position < count).astype(jnp.float32))
        held = jnp.where(valid == 1, position - (prefix - valid), 0)
        for b in range(bits):
            here = (held >> b) & 1
            moved = pltpu.roll(held, slots - (1 << b), 1)
            come = (moved >> b) & 1
            put(log_time + b, come.astype(jnp.float32))
            held = jnp.where(come == 1, moved, jnp.where(here == 1, 0, held))
            yield

    def early(index, carry):
        def middle():
            @pl.when(index == START)
            def _():
                pl.semaphore_wait(barrier, groups - 1 + owners - 1)
                for chunk in range(chunks):
                    for step in range(1, groups):
                        gain_copy(step, chunk).start()

        add_sources(lax.div(index, steps), lax.rem(index, steps), middle=middle)
        return carry

    fill(0, 0, 0)
    work = [tables()]
    for index in range(FIRST):
        add_sources(index // steps, index % steps, work, 1, index == FIRST - 1)
    lax.fori_loop(FIRST, EARLY * steps, early, 0)

    def catch_up(index, carry):
        @pl.when(lax.rem(2 * index, per_chunk) == 0)
        def _():
            gains_arrive(lax.div(2 * index, per_chunk))

        for step in range(steps):
            first = 2 * index + (step if steps > 1 else 0)
            now = [first] if 0 < steps - 1 else [first, first + 1]
            now = now if step < 2 else []
            add_sources(EARLY + index, step, [send(done, which) for which, done in enumerate(now)])
        return carry

    lax.fori_loop(0, EARLY - 1, catch_up, 0)
    for chunk in range(-(-2 * (EARLY - 1) // per_chunk), chunks):
        gains_arrive(chunk)

    def block_body(turn, carry):
        add_sources(turn, 0, [send(turn - 1)], PACE)
        for step in range(1, steps):
            add_sources(turn, step)
        return carry

    lax.fori_loop(2 * EARLY - 1, owners, block_body, 0)

    for _ in finish(owners - 1, piece_ref, p, states):
        pass
    for step in range(owners - 1):
        piece_copy(step).wait()


def place_kernel(start_ref, piece_ref, observed_ref, out_ref, total_ref):
    owners, _, cl, slots = piece_ref.shape
    capacity = observed_ref.shape[2]
    total_ref[...] = jnp.zeros_like(total_ref)
    position = iota((cl, LANES), 1)
    for index in range(owners):
        start = start_ref[0, index]
        low = start & (LANES - 1)
        base = pl.multiple_of(start - low, LANES)
        for z in range(2):
            spun = [
                pltpu.roll(piece_ref[index, z, :, pl.ds(t * LANES, LANES)], low, 1)
                for t in range(slots // LANES)
            ]
            for t in range(slots // LANES + 1):
                lanes = pl.ds(pl.multiple_of(base + t * LANES, LANES), LANES)
                if t == 0:
                    value = jnp.where(position >= low, spun[t], total_ref[z, :, lanes])
                elif t < slots // LANES:
                    value = jnp.where(position >= low, spun[t], spun[t - 1])
                else:
                    value = jnp.where(position >= low, 0.0, spun[t - 1])
                total_ref[z, :, lanes] = value
    for z in range(2):
        out_ref[:, z, :] = observed_ref[:, z, :] - total_ref[z, :, pl.ds(0, capacity)]


def on_device(
    observed,
    baseline_uvw_rows,
    frequencies,
    source_offset,
    source_flux,
    source_group,
    direction_gain,
    station_first,
    station_second,
    average_exponent,
    owner_plan,
):
    owners = lax.axis_size("bl")
    groups = lax.axis_size("dir")
    cl, _, capacity = observed.shape
    bl_dev = station_first.shape[0] // owners
    rows = baseline_uvw_rows.shape[1]
    time = rows // bl_dev
    slots = rows // owners
    tiles = slots // LANES
    sources = source_group.shape[0]
    vmem = pl.BlockSpec(memory_space=pltpu.VMEM)
    masks = int(math.log2(time)) + int(math.log2(slots)) + 2
    rows_per = max(8, cl)
    f32 = jnp.float32
    shape = jax.ShapeDtypeStruct
    *prepared, starts = pl.pallas_call(
        functools.partial(prepare_kernel, groups, owners, time),
        out_shape=(
            shape((sources // 2 * rows_per, LANES), jnp.bfloat16),
            shape((sources, cl, LANES), f32),
            shape((groups, cl, LANES), f32),
            shape((owners, 48, slots), jnp.bfloat16),
            shape((groups, 2, cl, direction_gain.shape[3]), f32),
            shape((8, bl_dev), jnp.int32),
            shape((1, LANES), jnp.int32),
        ),
        in_specs=[pl.BlockSpec(memory_space=pltpu.HBM)] * 11,
        out_specs=(vmem,) * 7,
        scratch_shapes=[
            pltpu.VMEM((sources // 2, LANES), f32),
            pltpu.VMEM(baseline_uvw_rows.shape, f32),
            pltpu.VMEM((1, frequencies.shape[0]), f32),
            pltpu.VMEM(source_offset.shape, f32),
            pltpu.VMEM(source_flux.shape, f32),
            pltpu.VMEM((1, sources), jnp.int32),
            pltpu.VMEM(direction_gain.shape, f32),
            pltpu.VMEM((1, bl_dev), jnp.int32),
            pltpu.VMEM((1, bl_dev), jnp.int32),
            pltpu.VMEM((1, average_exponent.shape[0]), jnp.int32),
            pltpu.VMEM(owner_plan.shape, jnp.int32),
            pltpu.SMEM(owner_plan.shape, jnp.int32),
            pltpu.SemaphoreType.DMA((11,)),
        ],
        compiler_params=pltpu.CompilerParams(vmem_limit_bytes=32 << 20),
        name="prepare",
    )(
        *[
            pltpu.with_memory_space_constraint(array, pltpu.HBM)
            for array in (
                baseline_uvw_rows,
                frequencies.reshape(1, -1),
                source_offset,
                source_flux,
                source_group.reshape(1, -1),
                direction_gain,
                station_first.reshape(1, -1),
                station_second.reshape(1, -1),
                average_exponent.reshape(1, -1),
                owner_plan,
                owner_plan,
            )
        ]
    )
    dma = pltpu.SemaphoreType.DMA
    pieces = pl.pallas_call(
        functools.partial(predict_kernel, groups, owners, time, min(4, tiles)),
        out_shape=shape((owners, 2, cl, slots), f32),
        in_specs=[vmem] * 6,
        out_specs=vmem,
        scratch_shapes=[
            pltpu.VMEM((groups, 2, cl, bl_dev), f32),
            pltpu.VMEM((masks, tiles, owners, LANES), f32),
            pltpu.VMEM((owners, tiles, 2 * groups, cl, LANES), f32),
            pltpu.VMEM((owners - 1, 2, cl, slots), f32),
            pltpu.VMEM((groups, 2, cl, bl_dev), f32),
            dma((groups - 1, bl_dev // LANES)),
            dma((groups - 1, bl_dev // LANES)),
            dma((owners - 1,)),
            dma((owners - 1,)),
        ]
        + [pltpu.VMEM((2, tiles, cl, LANES), f32)] * 4
        + [pltpu.VMEM((sources // groups, rows_per, min(4, tiles) * LANES), f32)] * groups,
        compiler_params=pltpu.CompilerParams(
            vmem_limit_bytes=32 << 20, collective_id=0, has_side_effects=True
        ),
        name="predict",
    )(*prepared)
    return pl.pallas_call(
        place_kernel,
        out_shape=jax.ShapeDtypeStruct(observed.shape, f32),
        in_specs=[vmem, vmem, vmem],
        out_specs=vmem,
        scratch_shapes=[pltpu.VMEM((2, cl, capacity + slots + LANES), f32)],
        compiler_params=pltpu.CompilerParams(vmem_limit_bytes=32 << 20),
        name="place",
    )(starts, pieces, observed)


def solution(mesh):
    placed = (
        P("dir", None, "bl"),
        P(None, "bl"),
        P(),
        P(),
        P(),
        P(),
        P("dir", None, None, None),
        P(),
        P(),
        P(),
        P(),
    )
    return jax.shard_map(
        on_device, mesh=mesh, in_specs=placed, out_specs=P("dir", None, "bl"), check_vma=False
    )
```

```python
import functools
import math

import jax
import jax.numpy as jnp
from jax import lax
from jax.experimental import pallas as pl
from jax.experimental.pallas import tpu as pltpu
from jax.sharding import PartitionSpec as P

LANES = 128
CHUNK = 8
PACE = 4
EARLY = 4
START = 3
FIRST = 2
BATCH = 16
MESH = pl.DeviceIdType.MESH
HIGH = lax.Precision.HIGHEST
NT = (((1,), (1,)), ((), ()))
P0, P1, P2, P3 = -2.2636507847492298, 1.3870216243251186, 4.937789609959605, 0.5033641130059734
K0, K1, K2 = 0.9997897140197886, -10.245898871410082, 1.823099221649536


def iota(shape, axis):
    return lax.broadcasted_iota(jnp.int32, shape, axis)


def flip(a, b, size):
    total = 0
    for i in range(int(math.log2(size))):
        total = total + lax.rem(lax.div(a, 2**i) + lax.div(b, 2**i), 2) * 2**i
    return total


def take(values, index):
    return jnp.take_along_axis(values, index, axis=1, mode="promise_in_bounds")


def thirds(value):
    high = value.astype(jnp.bfloat16).astype(jnp.float32)
    rest = value - high
    mid = rest.astype(jnp.bfloat16).astype(jnp.float32)
    return high, mid, rest - mid


def prepare_kernel(
    groups,
    owners,
    time,
    *refs,
):
    inputs = refs[:11]
    (
    sky_ref,
    wide_ref,
    base_ref,
    order_ref,
    table_ref,
    ids_ref,
    start_ref,
    spread_ref,
    uvw_ref,
    freq_ref,
    offs_ref,
    flux_ref,
    group_ref,
    gain_ref,
    first_ref,
    second_ref,
    exps_ref,
    plan_ref,
    plan_smem,
    sem,
    ) = refs[11:]
    d = lax.axis_index("dir")
    p = lax.axis_index("bl")
    cl = wide_ref.shape[1]
    sources = offs_ref.shape[1]
    per_group = sources // groups
    bl_dev = first_ref.shape[1]
    own = pl.ds(pl.multiple_of(p * bl_dev, bl_dev), bl_dev)
    held = refs[19:30]
    copies = {}
    for index in (4, 2, 3, 1, 9, 10, 0, 5, 6, 7, 8):
        source = inputs[index].at[:, own] if index in (6, 7) else inputs[index]
        copies[index] = pltpu.make_async_copy(source, held[index], sem.at[index])
        copies[index].start()

    def arrive(*indices):
        for index in indices:
            copies[index].wait()

    block_len = bl_dev // owners
    slots = block_len * time
    block_tiles = slots // LANES
    per_tile = LANES // time
    log_time = int(math.log2(time))
    chunks = bl_dev // LANES

    arrive(4, 2, 3, 1)
    member_row = group_ref[...].astype(jnp.float32)
    earlier = iota((sources, sources), 0) < iota((sources, sources), 1)
    equal = iota((sources, sources), 0) == iota((sources, sources), 1)
    member_col = jnp.sum(jnp.where(equal, member_row, 0.0), axis=1, keepdims=True)
    same = (jnp.abs(member_col - member_row) < 0.5) & earlier
    rank = jnp.sum(same.astype(jnp.float32), axis=0, keepdims=True)
    place = (member_row * per_group + rank + 0.5).astype(jnp.int32)
    pick = (iota((sources, sources), 0) == place).astype(jnp.float32).astype(jnp.bfloat16)

    def padded(rows):
        fill = jnp.zeros((8 - rows.shape[0], sources), jnp.float32)
        rows = jnp.concatenate([rows, fill], axis=0) if rows.shape[0] < 8 else rows
        return jnp.concatenate(thirds(rows), axis=0).astype(jnp.bfloat16)

    own_flux = jnp.zeros((cl, sources), jnp.float32)
    for i in range(groups):
        own_flux = own_flux + jnp.where(d == i, flux_ref[i * cl : (i + 1) * cl, :], 0.0)
    flux = lax.dot_general(padded(own_flux), pick, NT, preferred_element_type=jnp.float32)
    size = flux.shape[0] // 3
    flux = (flux[0:size] + flux[size : 2 * size] + flux[2 * size : 3 * size])[0:cl]
    offs = lax.dot_general(pick, padded(offs_ref[...]), NT, preferred_element_type=jnp.float32)
    east, north = [offs[:, i : i + 1] + offs[:, 8 + i : 9 + i] + offs[:, 16 + i : 17 + i] for i in range(2)]
    depth = jnp.sqrt(1.0 - east * east - north * north) - 1.0
    arrive(9, 10, 0, 5, 6, 7, 8)
    half = sources // 2
    kind = iota((sources, LANES), 1) % 8
    used = iota((sources, LANES), 1) % (LANES // 2) < 48
    spread = jnp.where(kind == 0, east, jnp.where(kind == 1, north, jnp.where(kind == 2, depth, 0.0)))
    spread = jnp.where(used, spread, 0.0)
    spread_ref[...] = jnp.where(iota((half, LANES), 1) < LANES // 2, spread[:half], spread[half:])
    high_rows = sky_ref.shape[0] // half
    turn_channel = iota((high_rows, flux_ref.shape[0]), 1) == d * cl + iota((high_rows, flux_ref.shape[0]), 0)
    turn_freq = jnp.sum(turn_channel.astype(jnp.float32) * freq_ref[...], axis=1, keepdims=True)
    turn_freq = jnp.broadcast_to(turn_freq, (high_rows, LANES))
    term = iota((high_rows, LANES), 1) % (LANES // 2) // 8
    mids, lows = (term == 2) | (term == 3), term == 5
    pair_rows = max(1, 16 // high_rows)
    share = [part.astype(jnp.float32) for part in thirds(own_flux)[:2]]
    if cl < 8:
        share = [jnp.concatenate([part, jnp.zeros((8 - cl, sources), jnp.float32)], axis=0) for part in share]
    order_row = jnp.broadcast_to(place, share[0].shape)
    ones = jnp.ones((2 * sources, LANES), jnp.float32).astype(jnp.bfloat16)
    for k in range(0, half, pair_rows):
        rows = []
        for i in range(pair_rows):
            high, mid, low = thirds(turn_freq * spread_ref[pl.ds(k + i, high_rows, stride=0), :])
            rows.append(jnp.where(mids, mid, jnp.where(lows, low, high)))
        rows = jnp.concatenate(rows, axis=0).astype(jnp.bfloat16)
        sky_ref[k * high_rows : (k + pair_rows) * high_rows, :] = rows
        if k % BATCH == 0:
            left = []
            for i in range(2 * k, 2 * k + 2 * BATCH):
                here = order_row == i
                left.append(jnp.concatenate([jnp.where(here, part, 0.0) for part in share], axis=1))
            left = jnp.concatenate(left, axis=0).astype(jnp.bfloat16)
            amounts = jnp.dot(left, ones, preferred_element_type=jnp.float32)
            amounts = amounts.reshape(2 * BATCH, share[0].shape[0], LANES)[:, 0:cl]
            wide_ref[2 * k : 2 * k + 2 * BATCH] = amounts
    for g in range(groups):
        part = jnp.sum(flux[:, g * per_group : (g + 1) * per_group], axis=1, keepdims=True)
        base_ref[g] = jnp.broadcast_to(part, (cl, LANES))

    for k in range(owners):
        rows = uvw_ref[:, k * slots : (k + 1) * slots]
        rows = jnp.concatenate([rows, jnp.zeros((8 - rows.shape[0], slots), jnp.float32)], axis=0)
        high, mid, low = thirds(rows)
        rows = jnp.concatenate([high, mid, high, mid, low, high], axis=0)
        order_ref[plan_smem[p, k]] = rows.astype(jnp.bfloat16)
    plan = plan_ref[...].astype(jnp.float32)
    own_plan = jnp.sum(
        jnp.where(iota((owners, owners), 0) == p, plan, 0.0), axis=0, keepdims=True
    )
    held_by = jnp.abs(own_plan - iota((owners, owners), 0).astype(jnp.float32)) < 0.5
    block_of = jnp.sum(
        jnp.where(held_by, iota((owners, owners), 1).astype(jnp.float32), 0.0), axis=1, keepdims=True
    )

    lane = iota((owners, LANES), 1)
    row = iota((owners, LANES), 0)
    for g in range(groups):
        for z in range(2):
            table_ref[g, z] = gain_ref[0, g * cl : (g + 1) * cl, z, :]
    for chunk in range(chunks):
        lanes = pl.ds(chunk * LANES, LANES)
        where_from = jnp.where((chunk * LANES + lane) // block_len == row, block_of, 0.0)
        where_from = (jnp.sum(where_from, axis=0, keepdims=True) + 0.5).astype(jnp.int32)
        source = where_from * block_len + (chunk * LANES + iota((1, LANES), 1)) % block_len
        source = jnp.broadcast_to(source, (cl, LANES))
        for which in range(3):
            ids = jnp.zeros((cl, LANES), jnp.int32)
            for part in range(chunks):
                begin = part * LANES
                if which == 2:
                    begin = pl.multiple_of(p * bl_dev + begin, LANES)
                table = (first_ref, second_ref, exps_ref)[which][:, pl.ds(begin, LANES)]
                table = jnp.broadcast_to(table, (cl, LANES))
                ids = jnp.where((source >> 7) == part, take(table, source & (LANES - 1)), ids)
            ids_ref[which : which + 1, lanes] = ids[0:1]

    exps_all = jnp.concatenate(
        [exps_ref[:, i * bl_dev : (i + 1) * bl_dev] for i in range(owners)], axis=0
    )
    rows_all = jnp.right_shift(jnp.full(exps_all.shape, time, jnp.int32), exps_all)
    rows_all = rows_all.astype(jnp.float32)
    to_owner = jnp.zeros((owners, 1), jnp.float32)
    for k in range(owners):
        count = jnp.sum(rows_all[:, k * block_len : (k + 1) * block_len], axis=1, keepdims=True)
        to_owner = to_owner + jnp.where(plan_ref[:, k : k + 1] == p, count, 0.0)
    starts = jnp.sum(jnp.where(row < lane, to_owner, 0.0), axis=0, keepdims=True)
    start_ref[...] = (starts + 0.5).astype(jnp.int32)


def predict_kernel(
    groups,
    owners,
    time,
    tiles,
    sky_ref,
    wide_ref,
    base_ref,
    order_ref,
    table_ref,
    ids_ref,
    piece_ref,
    pair_ref,
    mask_ref,
    kept_ref,
    send_ref,
    gather_ref,
    gain_send,
    gain_recv,
    piece_send,
    piece_recv,
    *more_refs,
):
    states, turns_refs = more_refs[:4], more_refs[4:]
    d = lax.axis_index("dir")
    p = lax.axis_index("bl")
    sources, cl, _ = wide_ref.shape
    per_group = sources // groups
    slots = order_ref.shape[2]
    block_len = slots // time
    block_tiles = slots // LANES
    per_tile = LANES // time
    log_time = int(math.log2(time))
    bits = int(math.log2(slots))

    barrier = pltpu.get_barrier_semaphore()
    for axis, me, size in (("dir", d, groups), ("bl", p, owners)):
        for step in range(1, size):
            pl.semaphore_signal(
                barrier, inc=1, device_id={axis: lax.rem(me + step, size)}, device_id_type=MESH
            )

    def owner_of(turn):
        return flip(p, owners - 1 - turn, owners)

    chunks = ids_ref.shape[1] // LANES
    per_chunk = LANES // block_len

    def gain_copy(step, chunk):
        other = lax.rem(d + step, groups)
        first = flip(lax.div(p, per_chunk), chunks - 1 - chunk, chunks) * LANES
        lanes = pl.ds(pl.multiple_of(first, LANES), LANES)
        return pltpu.make_async_remote_copy(
            src_ref=pair_ref.at[other, :, :, lanes],
            dst_ref=gather_ref.at[d, :, :, lanes],
            send_sem=gain_send.at[step - 1, chunk],
            recv_sem=gain_recv.at[step - 1, chunk],
            device_id={"dir": other},
            device_id_type=MESH,
        )

    def gains_arrive(chunk):
        for step in range(1, groups):
            gain_copy(step, chunk).wait()

    def piece_copy(step):
        return pltpu.make_async_remote_copy(
            src_ref=send_ref.at[step],
            dst_ref=piece_ref.at[p],
            send_sem=piece_send.at[step],
            recv_sem=piece_recv.at[step],
            device_id={"bl": owner_of(step)},
            device_id_type=MESH,
        )

    flux_sum = [base_ref[g] for g in range(groups)]
    lane = iota((cl, LANES), 1)
    steps = block_tiles // tiles

    def fill(turn, step, g):
        ln = pl.ds(pl.multiple_of(step * tiles * LANES, LANES), tiles * LANES)
        turns_ref = turns_refs[g]
        rows = per_group * turns_ref.shape[1]
        near = g % (groups // 2)
        right = order_ref[owner_of(turn), :, ln]
        fill_rows = LANES // 2 if g >= groups // 2 else LANES - right.shape[0]
        blank = jnp.zeros((fill_rows, tiles * LANES), jnp.bfloat16)
        if g >= groups // 2:
            rest = jnp.zeros((LANES // 2 - right.shape[0], tiles * LANES), jnp.bfloat16)
            right = jnp.concatenate([blank, right, rest], axis=0)
        else:
            right = jnp.concatenate([right, blank], axis=0)
        turns = jnp.dot(
            sky_ref[near * rows : (near + 1) * rows, :], right, preferred_element_type=jnp.float32
        )
        turns_ref[...] = turns.reshape(turns_ref.shape)

    def add_sources(turn, step, work=(), pace=3, drain=True):
        for g in range(groups):
            if g + 1 < groups:
                fill(turn, step, g + 1)
            else:
                ahead = step + 1
                fill(lax.rem(turn + lax.div(ahead, steps), owners), lax.rem(ahead, steps), 0)

            def source(i, acc):
                acc = list(acc)
                amount = wide_ref[g * per_group + i]
                for t in range(tiles):
                    turns = turns_refs[g][i, 0:cl, t * LANES : (t + 1) * LANES]
                    x = turns - jnp.round(turns)
                    z = x * x
                    m = (z + P0) * z
                    s = x * (m + P1)
                    weighted = amount * s
                    acc[2 * t] = acc[2 * t] + weighted * s
                    acc[2 * t + 1] = acc[2 * t + 1] + weighted * ((m + P2) * (m + P3))
                return tuple(acc)

            acc = tuple(jnp.zeros((cl, LANES), jnp.float32) for _ in range(2 * tiles))
            for begin in range(0, per_group, CHUNK):
                acc = lax.fori_loop(begin, begin + CHUNK, source, acc, unroll=CHUNK)
                for stage in list(work) * pace:
                    next(stage, None)
            for t in range(tiles):
                kept_ref[turn, step * tiles + t, 2 * g] = K0 * flux_sum[g] + K1 * acc[2 * t]
                kept_ref[turn, step * tiles + t, 2 * g + 1] = -K2 * acc[2 * t + 1]
        for stage in work if drain else ():
            for _ in stage:
                pass

    def finish(turn, out_ref, where, states):
        owner = owner_of(turn)
        chunk = pl.multiple_of(lax.div(owner * block_len, LANES) * LANES, LANES)
        first_bl = lax.rem(owner * block_len, LANES) + (lane >> log_time)

        def wide(index, t):
            return mask_ref[index, t, pl.ds(owner, cl, stride=0), :]

        for t in range(block_tiles):
            index = first_bl + t * per_tile
            model_r = jnp.zeros((cl, LANES), jnp.float32)
            model_i = jnp.zeros((cl, LANES), jnp.float32)
            for g in range(groups):
                gr = take(gather_ref[g, 0, :, pl.ds(chunk, LANES)], index)
                gi = take(gather_ref[g, 1, :, pl.ds(chunk, LANES)], index)
                real, imag = kept_ref[turn, t, 2 * g], kept_ref[turn, t, 2 * g + 1]
                model_r = model_r + (real * gr - imag * gi)
                model_i = model_i + (real * gi + imag * gr)
            scale = wide(log_time + bits + 1, t)
            states[0][0, t] = model_r * scale
            states[0][1, t] = model_i * scale
            yield

        stages = log_time + bits
        for stage in range(stages):
            size = 1 << (stage if stage < log_time else stage - log_time)
            jump, size = size // LANES, size % LANES
            for z in range(2):
                old, new = states[stage % 2], states[1 - stage % 2]
                spun = [old[z, t] for t in range(block_tiles)]
                if size:
                    spun = [pltpu.roll(x, LANES - size, 1) for x in spun]
                for t in range(block_tiles):
                    near = spun[(t + jump) % block_tiles]
                    if size:
                        near = jnp.where(lane < LANES - size, near, spun[(t + 1) % block_tiles])
                    if stage < log_time:
                        value = old[z, t] + wide(stage, t) * near
                    else:
                        value = jnp.where(wide(stage, t) > 0.5, near, old[z, t])
                    if stage == stages - 1:
                        value = jnp.where(wide(stages, t) > 0.5, value, 0.0)
                        out_ref[where, z, :, t * LANES : (t + 1) * LANES] = value
                    else:
                        new[z, t] = value
                yield

    def send(turn, which=0):
        yield from finish(turn, send_ref, turn, states[2 * which : 2 * which + 2])
        yield
        piece_copy(turn).start()

    def tables():
        station_total = table_ref.shape[3]
        for chunk in range(chunks):
            lanes = pl.ds(chunk * LANES, LANES)
            looked = []
            for which in range(2):
                ids = jnp.broadcast_to(ids_ref[which : which + 1, lanes], (cl, LANES))
                low, high = ids & (LANES - 1), ids >> 7
                rows = []
                for g in range(groups):
                    for z in range(2):
                        total = jnp.zeros((cl, LANES), jnp.float32)
                        for part in range(station_total // LANES):
                            table = table_ref[g, z, :, pl.ds(part * LANES, LANES)]
                            total = jnp.where(high == part, take(table, low), total)
                        rows.append(total)
                looked.append(rows)
                yield
            first, second = looked
            for g in range(groups):
                ar, ai, br, bi = first[2 * g], first[2 * g + 1], second[2 * g], second[2 * g + 1]
                pair_ref[g, 0, :, lanes] = ar * br + ai * bi
                pair_ref[g, 1, :, lanes] = ai * br - ar * bi
        gather_ref[d] = pair_ref[d]

        exps = []
        wide_lane = iota((owners, LANES), 1)
        for t in range(block_tiles):
            source = iota((owners, LANES), 0) * block_len + t * per_tile + (wide_lane >> log_time)
            found = jnp.zeros((owners, LANES), jnp.int32)
            for part in range(chunks):
                table = ids_ref[2:3, part * LANES : (part + 1) * LANES]
                table = jnp.broadcast_to(table, (owners, LANES))
                got = [take(table[i : i + 8], source[i : i + 8] & (LANES - 1)) for i in range(0, owners, 8)]
                got = jnp.concatenate(got) if owners > 8 else got[0]
                found = jnp.where((source >> 7) == part, got, found)
            exps.append(found)
            if t % 2 == 1:
                yield
        exps = jnp.concatenate(exps, axis=1)

        def put(index, values):
            for t in range(block_tiles):
                mask_ref[index, t] = values[:, t * LANES : (t + 1) * LANES]

        position = iota((owners, slots), 1)
        width = jnp.left_shift(jnp.ones_like(exps), exps)
        valid = ((position & (width - 1)) == 0).astype(jnp.int32)
        scale = jnp.ones((owners, slots), jnp.float32)
        for s in range(log_time):
            scale = jnp.where(exps > s, scale * 0.5, scale)
            put(s, (exps > s).astype(jnp.float32))
        put(log_time + bits + 1, scale)
        yield
        prefix = valid
        for b in range(bits):
            prefix = prefix + jnp.where(position >= 1 << b, pltpu.roll(prefix, 1 << b, 1), 0)
            if b % 2 == 1:
                yield
        count = jnp.max(prefix, axis=1, keepdims=True)
        put(log_time + bits, (position < count).astype(jnp.float32))
        held = jnp.where(valid == 1, position - (prefix - valid), 0)
        for b in range(bits):
            here = (held >> b) & 1
            moved = pltpu.roll(held, slots - (1 << b), 1)
            come = (moved >> b) & 1
            put(log_time + b, come.astype(jnp.float32))
            held = jnp.where(come == 1, moved, jnp.where(here == 1, 0, held))
            yield

    def early(index, carry):
        @pl.when(index == START)
        def _():
            pl.semaphore_wait(barrier, groups - 1 + owners - 1)
            for chunk in range(chunks):
                for step in range(1, groups):
                    gain_copy(step, chunk).start()

        add_sources(lax.div(index, steps), lax.rem(index, steps))
        return carry

    fill(0, 0, 0)
    work = [tables()]
    for index in range(FIRST):
        add_sources(index // steps, index % steps, work, 1, index == FIRST - 1)
    lax.fori_loop(FIRST, EARLY * steps, early, 0)

    def catch_up(index, carry):
        @pl.when(lax.rem(2 * index, per_chunk) == 0)
        def _():
            gains_arrive(lax.div(2 * index, per_chunk))

        for step in range(steps):
            first = 2 * index + (step if steps > 1 else 0)
            now = [first] if 0 < steps - 1 else [first, first + 1]
            now = now if step < 2 else []
            add_sources(EARLY + index, step, [send(done, which) for which, done in enumerate(now)])
        return carry

    lax.fori_loop(0, EARLY - 1, catch_up, 0)
    for chunk in range(-(-2 * (EARLY - 1) // per_chunk), chunks):
        gains_arrive(chunk)

    def block_body(turn, carry):
        add_sources(turn, 0, [send(turn - 1)], PACE)
        for step in range(1, steps):
            add_sources(turn, step)
        return carry

    lax.fori_loop(2 * EARLY - 1, owners, block_body, 0)

    for _ in finish(owners - 1, piece_ref, p, states):
        pass
    for step in range(owners - 1):
        piece_copy(step).wait()


def place_kernel(start_ref, piece_ref, observed_ref, out_ref, total_ref):
    owners, _, cl, slots = piece_ref.shape
    capacity = observed_ref.shape[2]
    total_ref[...] = jnp.zeros_like(total_ref)
    position = iota((cl, LANES), 1)
    for index in range(owners):
        start = start_ref[0, index]
        low = start & (LANES - 1)
        base = pl.multiple_of(start - low, LANES)
        for z in range(2):
            spun = [
                pltpu.roll(piece_ref[index, z, :, pl.ds(t * LANES, LANES)], low, 1)
                for t in range(slots // LANES)
            ]
            for t in range(slots // LANES + 1):
                lanes = pl.ds(pl.multiple_of(base + t * LANES, LANES), LANES)
                if t == 0:
                    value = jnp.where(position >= low, spun[t], total_ref[z, :, lanes])
                elif t < slots // LANES:
                    value = jnp.where(position >= low, spun[t], spun[t - 1])
                else:
                    value = jnp.where(position >= low, 0.0, spun[t - 1])
                total_ref[z, :, lanes] = value
    for z in range(2):
        out_ref[:, z, :] = observed_ref[:, z, :] - total_ref[z, :, pl.ds(0, capacity)]


def on_device(
    observed,
    baseline_uvw_rows,
    frequencies,
    source_offset,
    source_flux,
    source_group,
    direction_gain,
    station_first,
    station_second,
    average_exponent,
    owner_plan,
):
    owners = lax.axis_size("bl")
    groups = lax.axis_size("dir")
    cl, _, capacity = observed.shape
    bl_dev = station_first.shape[0] // owners
    rows = baseline_uvw_rows.shape[1]
    time = rows // bl_dev
    slots = rows // owners
    tiles = slots // LANES
    sources = source_group.shape[0]
    vmem = pl.BlockSpec(memory_space=pltpu.VMEM)
    masks = int(math.log2(time)) + int(math.log2(slots)) + 2
    rows_per = max(8, cl)
    f32 = jnp.float32
    shape = jax.ShapeDtypeStruct
    *prepared, starts = pl.pallas_call(
        functools.partial(prepare_kernel, groups, owners, time),
        out_shape=(
            shape((sources // 2 * rows_per, LANES), jnp.bfloat16),
            shape((sources, cl, LANES), f32),
            shape((groups, cl, LANES), f32),
            shape((owners, 48, slots), jnp.bfloat16),
            shape((groups, 2, cl, direction_gain.shape[3]), f32),
            shape((8, bl_dev), jnp.int32),
            shape((1, LANES), jnp.int32),
        ),
        in_specs=[pl.BlockSpec(memory_space=pltpu.HBM)] * 11,
        out_specs=(vmem,) * 7,
        scratch_shapes=[
            pltpu.VMEM((sources // 2, LANES), f32),
            pltpu.VMEM(baseline_uvw_rows.shape, f32),
            pltpu.VMEM((1, frequencies.shape[0]), f32),
            pltpu.VMEM(source_offset.shape, f32),
            pltpu.VMEM(source_flux.shape, f32),
            pltpu.VMEM((1, sources), jnp.int32),
            pltpu.VMEM(direction_gain.shape, f32),
            pltpu.VMEM((1, bl_dev), jnp.int32),
            pltpu.VMEM((1, bl_dev), jnp.int32),
            pltpu.VMEM((1, average_exponent.shape[0]), jnp.int32),
            pltpu.VMEM(owner_plan.shape, jnp.int32),
            pltpu.SMEM(owner_plan.shape, jnp.int32),
            pltpu.SemaphoreType.DMA((11,)),
        ],
        compiler_params=pltpu.CompilerParams(vmem_limit_bytes=32 << 20),
        name="prepare",
    )(
        *[
            pltpu.with_memory_space_constraint(array, pltpu.HBM)
            for array in (
                baseline_uvw_rows,
                frequencies.reshape(1, -1),
                source_offset,
                source_flux,
                source_group.reshape(1, -1),
                direction_gain,
                station_first.reshape(1, -1),
                station_second.reshape(1, -1),
                average_exponent.reshape(1, -1),
                owner_plan,
                owner_plan,
            )
        ]
    )
    dma = pltpu.SemaphoreType.DMA
    pieces = pl.pallas_call(
        functools.partial(predict_kernel, groups, owners, time, min(4, tiles)),
        out_shape=shape((owners, 2, cl, slots), f32),
        in_specs=[vmem] * 6,
        out_specs=vmem,
        scratch_shapes=[
            pltpu.VMEM((groups, 2, cl, bl_dev), f32),
            pltpu.VMEM((masks, tiles, owners, LANES), f32),
            pltpu.VMEM((owners, tiles, 2 * groups, cl, LANES), f32),
            pltpu.VMEM((owners - 1, 2, cl, slots), f32),
            pltpu.VMEM((groups, 2, cl, bl_dev), f32),
            dma((groups - 1, bl_dev // LANES)),
            dma((groups - 1, bl_dev // LANES)),
            dma((owners - 1,)),
            dma((owners - 1,)),
        ]
        + [pltpu.VMEM((2, tiles, cl, LANES), f32)] * 4
        + [pltpu.VMEM((sources // groups, rows_per, min(4, tiles) * LANES), f32)] * groups,
        compiler_params=pltpu.CompilerParams(
            vmem_limit_bytes=32 << 20, collective_id=0, has_side_effects=True
        ),
        name="predict",
    )(*prepared)
    return pl.pallas_call(
        place_kernel,
        out_shape=jax.ShapeDtypeStruct(observed.shape, f32),
        in_specs=[vmem, vmem, vmem],
        out_specs=vmem,
        scratch_shapes=[pltpu.VMEM((2, cl, capacity + slots + LANES), f32)],
        compiler_params=pltpu.CompilerParams(vmem_limit_bytes=32 << 20),
        name="place",
    )(starts, pieces, observed)


def solution(mesh):
    placed = (
        P("dir", None, "bl"),
        P(None, "bl"),
        P(),
        P(),
        P(),
        P(),
        P("dir", None, None, None),
        P(),
        P(),
        P(),
        P(),
    )
    return jax.shard_map(
        on_device, mesh=mesh, in_specs=placed, out_specs=P("dir", None, "bl"), check_vma=False
    )
```
